32 devices in a mesh: shard: 4 (over y, x), replica: 8 (over z, core).
Axes of the slice: x: 2, y: 2, z: 4, core: 2. Of those that a mesh axis runs over, the one named last changes fastest.
Arguments:
- series: bfloat16 [128, 16384], P(('shard', 'replica')), may hold values from -6 to 6
- mask: int32 [128, 256], P(('shard', 'replica')), may hold values from 0 to 1, as said below
- qkv_w: float32 [2, 512, 1536], P(None, 'shard'), may hold values from -0.25 to 0.25
- out_w: float32 [2, 512, 512], P(None, 'shard'), may hold values from -1 to 1
- up_w: float32 [2, 512, 2048], P(None, 'shard'), may hold values from -0.25 to 0.25
- down_w: float32 [2, 2048, 512], P(None, 'shard'), may hold values from -0.125 to 0.125
- patch_maps: float32 [384, 512], P(None, 'shard')
- norm_params: float32 [10, 512], P(None, 'shard')
- qkv_m: float32 [2, 512, 1536], P(None, 'shard'), may hold values from -5.9604645e-07 to 5.9604645e-07
- out_m: float32 [2, 512, 512], P(None, 'shard'), may hold values from -5.9604645e-07 to 5.9604645e-07
- up_m: float32 [2, 512, 2048], P(None, 'shard'), may hold values from -5.9604645e-07 to 5.9604645e-07
- down_m: float32 [2, 2048, 512], P(None, 'shard'), may hold values from -5.9604645e-07 to 5.9604645e-07
- patch_m: float32 [384, 512], P(None, 'shard'), may hold values from -5.9604645e-07 to 5.9604645e-07
- norm_m: float32 [10, 512], P(None, 'shard'), may hold values from -3.33786e-06 to 3.33786e-06
- qkv_v: float32 [2, 512, 1536], P(None, 'shard'), may hold values from 7.7003825e-17 to 1.2320612e-15
- out_v: float32 [2, 512, 512], P(None, 'shard'), may hold values from 7.7003825e-17 to 1.2320612e-15
- up_v: float32 [2, 512, 2048], P(None, 'shard'), may hold values from 7.7003825e-17 to 1.2320612e-15
- down_v: float32 [2, 2048, 512], P(None, 'shard'), may hold values from 7.7003825e-17 to 1.2320612e-15
- patch_v: float32 [384, 512], P(None, 'shard'), may hold values from 7.7003825e-17 to 1.2320612e-15
- norm_v: float32 [10, 512], P(None, 'shard'), may hold values from 1.9250956e-15 to 3.080153e-14
Outputs:
- loss: float32 [], replicated
- grad_norm: float32 [], replicated
- qkv_new: float32 [2, 512, 1536], P(None, 'shard')
- out_new: float32 [2, 512, 512], P(None, 'shard')
- up_new: float32 [2, 512, 2048], P(None, 'shard')
- down_new: float32 [2, 2048, 512], P(None, 'shard')
- patch_new: float32 [384, 512], P(None, 'shard')
- norm_new: float32 [10, 512], P(None, 'shard')
- qkv_m_new: float32 [2, 512, 1536], P(None, 'shard')
- out_m_new: float32 [2, 512, 512], P(None, 'shard')
- up_m_new: float32 [2, 512, 2048], P(None, 'shard')
- down_m_new: float32 [2, 2048, 512], P(None, 'shard')
- patch_m_new: float32 [384, 512], P(None, 'shard')
- norm_m_new: float32 [10, 512], P(None, 'shard')
- qkv_v_new: float32 [2, 512, 1536], P(None, 'shard')
- out_v_new: float32 [2, 512, 512], P(None, 'shard')
- up_v_new: float32 [2, 512, 2048], P(None, 'shard')
- down_v_new: float32 [2, 2048, 512], P(None, 'shard')
- patch_v_new: float32 [384, 512], P(None, 'shard')
- norm_v_new: float32 [10, 512], P(None, 'shard')
The draws below stay inside these ranges and needn't reach their ends.
Inputs may be any that keep to these rules, and one draw needn't show every extreme that they name: `mask`: each series has exactly 102 masked patches.
All inputs are finite; a program needn't handle non-finite values.
Results may differ from the reference program's by a relative error of at most 0.02.
Values may be sent and summed in bfloat16 or wider, within the bound.
No kernel may reach another device: no remote copies, remote signals or barrier semaphores. Data moves between devices by JAX's collectives and lax.ppermute only.
A program may use at most 256 MiB of HBM per device.

```python
import math
import jax
import jax.numpy as jnp
from jax import lax

D = 512
H = 8
DH = 64
FF = 2048
P_SIZE = 64
LEN = 256
L = 2
SERIES = 128
MASKED = 102
NORMS = 10
NPARAM = 6493184


def draw_mask(key, part):
    keys = jax.random.split(jax.random.fold_in(key, 11), SERIES)
    order = jax.vmap(lambda single: jax.random.permutation(single, LEN))(keys)
    return (order < MASKED).astype(jnp.int32)


def draw_patch_maps(key, part):
    first, second, third = jax.random.split(jax.random.fold_in(key, 23), 3)
    embed = jax.random.normal(first, (P_SIZE, D), jnp.float32) * P_SIZE ** (-0.5)
    head = jax.random.normal(second, (P_SIZE, D), jnp.float32) * D ** (-0.5)
    table = jax.random.normal(third, (LEN, D), jnp.float32) * 0.5
    return jnp.concatenate([embed, head, table], 0)


def draw_norm_params(key, part):
    first = jax.random.fold_in(jax.random.fold_in(key, 37), 0)
    noise = jax.random.normal(first, (NORMS, D), jnp.float32)
    parity = (jnp.arange(NORMS) % 2).astype(jnp.float32)[:, None]
    place = jnp.arange(D).astype(jnp.float32) / (D - 1)
    ramp = jnp.exp((place[None, :] * 2.0 - 1.0) * 0.8) * jnp.ones((NORMS, 1), jnp.float32)
    gains = ramp * (1.0 + 0.15 * jnp.clip(noise, -3.0, 3.0))
    return (1.0 - parity) * gains + parity * 0.2 * noise


def level_of(stream_key, extent, cuts, smallest, largest):
    loudness = 1.0
    for position, blocks in cuts:
        steps = jax.random.uniform(jax.random.fold_in(jax.random.fold_in(stream_key, 6), position), (blocks,), jnp.float32, smallest / len(cuts), largest / len(cuts))
        loudness = loudness * jnp.repeat(jnp.exp(steps), extent[position] // blocks).reshape((-1,) + (1,) * (len(extent) - 1 - position))
    return loudness


def bell_draw(key, extent, scale, reach, cuts=(), kind=jnp.bfloat16):
    entries = scale * jax.random.normal(key, extent, jnp.float32)
    if cuts:
        entries = entries * level_of(key, extent, cuts, -0.22, 0.18)
    return jnp.clip(entries, -reach, reach).astype(kind)


def setup_inputs(seed: int = 0) -> dict:
    splits = jax.random.split(jax.random.key(seed), 21)
    return {
        "series": bell_draw(splits[0], (SERIES, LEN * P_SIZE), 1.0, 6.0, ((0, 32),)),
        "mask": draw_mask(jax.random.fold_in(splits[20], 71), 0),
        "qkv_w": bell_draw(splits[2], (L, D, 3 * D), D ** -0.5, 0.25, ((1, 4),), jnp.float32),
        "out_w": bell_draw(splits[3], (L, D, D), (D // 16) ** -0.5, 1.0, ((1, 4),), jnp.float32),
        "up_w": bell_draw(splits[4], (L, D, FF), D ** -0.5, 0.25, ((1, 4),), jnp.float32),
        "down_w": bell_draw(splits[5], (L, FF, D), FF ** -0.5, 0.125, ((1, 4),), jnp.float32),
        "patch_maps": draw_patch_maps(jax.random.fold_in(splits[20], 71), 0),
        "norm_params": draw_norm_params(jax.random.fold_in(splits[20], 71), 0),
        "qkv_m": bell_draw(splits[8], (L, D, 3 * D), (0.00011 * NPARAM ** -0.5), 5.960464477539062e-07, ((1, 4),), jnp.float32),
        "out_m": bell_draw(splits[9], (L, D, D), (0.00011 * NPARAM ** -0.5), 5.960464477539062e-07, ((1, 4),), jnp.float32),
        "up_m": bell_draw(splits[10], (L, D, FF), (0.00011 * NPARAM ** -0.5), 5.960464477539062e-07, ((1, 4),), jnp.float32),
        "down_m": bell_draw(splits[11], (L, FF, D), (0.00011 * NPARAM ** -0.5), 5.960464477539062e-07, ((1, 4),), jnp.float32),
        "patch_m": bell_draw(splits[12], (2 * P_SIZE + LEN, D), (0.00011 * NPARAM ** -0.5), 5.960464477539062e-07, ((1, 4),), jnp.float32),
        "norm_m": bell_draw(splits[13], (NORMS, D), (0.00055 * NPARAM ** -0.5), 3.337860107421875e-06, ((1, 4),), jnp.float32),
        "qkv_v": jnp.clip(jnp.exp(math.log(1.2320611966702808e-15) - 2.7725887 * jax.random.uniform(splits[14], (L, D, 3 * D), jnp.float32) ** level_of(splits[14], (L, D, 3 * D), ((1, 4),), -0.2, 0.2)), 7.700382479189255e-17, 1.2320611966702808e-15),
        "out_v": jnp.clip(jnp.exp(math.log(1.2320611966702808e-15) - 2.7725887 * jax.random.uniform(splits[15], (L, D, D), jnp.float32) ** level_of(splits[15], (L, D, D), ((1, 4),), -0.2, 0.2)), 7.700382479189255e-17, 1.2320611966702808e-15),
        "up_v": jnp.clip(jnp.exp(math.log(1.2320611966702808e-15) - 2.7725887 * jax.random.uniform(splits[16], (L, D, FF), jnp.float32) ** level_of(splits[16], (L, D, FF), ((1, 4),), -0.2, 0.2)), 7.700382479189255e-17, 1.2320611966702808e-15),
        "down_v": jnp.clip(jnp.exp(math.log(1.2320611966702808e-15) - 2.7725887 * jax.random.uniform(splits[17], (L, FF, D), jnp.float32) ** level_of(splits[17], (L, FF, D), ((1, 4),), -0.2, 0.2)), 7.700382479189255e-17, 1.2320611966702808e-15),
        "patch_v": jnp.clip(jnp.exp(math.log(1.2320611966702808e-15) - 2.7725887 * jax.random.uniform(splits[18], (2 * P_SIZE + LEN, D), jnp.float32) ** level_of(splits[18], (2 * P_SIZE + LEN, D), ((1, 4),), -0.2, 0.2)), 7.700382479189255e-17, 1.2320611966702808e-15),
        "norm_v": jnp.clip(jnp.exp(math.log(3.08015298108779e-14) - 2.7725887 * jax.random.uniform(splits[19], (NORMS, D), jnp.float32) ** level_of(splits[19], (NORMS, D), ((1, 4),), -0.2, 0.2)), 1.9250956131798688e-15, 3.08015298108779e-14),
    }


HI = lax.Precision.HIGHEST
EPS = 1e-05
CLIP = 0.001
RATE = 0.05
TABLE_RATE = 0.3
BETA_ONE = 0.9
BETA_TWO = 0.999
ADAM_EPS = 1e-08
DECAY = 0.1
STEP_COUNT = 10

@jax.custom_vjp
def low(v):
    return lax.optimization_barrier(v.astype(jnp.bfloat16)).astype(jnp.float32)

@jax.custom_vjp
def low_back(v):
    return v

def low_keep(v):
    return (low(v), None)

def low_pass(kept, grad):
    return (grad,)

def back_keep(v):
    return (v, None)

def back_low(kept, grad):
    return (low(grad),)
low.defvjp(low_keep, low_pass)
low_back.defvjp(back_keep, back_low)

def layer_norm(x, gain, bias):
    center = x - lax.optimization_barrier(jnp.mean(x, -1, keepdims=True))
    spread = lax.optimization_barrier(jnp.mean(center * center, -1, keepdims=True))
    return center * lax.rsqrt(spread + EPS) * gain + bias

def proj(x, w):
    return jnp.einsum('bld,de->ble', x, low(w), precision=HI)

def layer(x, w_qkv, w_out, w_up, w_down, norms):
    batch = x.shape[0]
    normed = low(layer_norm(x, norms[0], norms[1]))
    qkv = low(low_back(proj(normed, w_qkv))).reshape(batch, LEN, 3, H, DH)
    query, key, value = (qkv[:, :, 0], qkv[:, :, 1], qkv[:, :, 2])
    scores = low_back(jnp.einsum('bqhd,bkhd->bhqk', query, key, precision=HI) * DH ** (-0.5))
    probs = low(jax.nn.softmax(scores, axis=-1))
    attended = low(low_back(jnp.einsum('bhqk,bkhd->bqhd', probs, value, precision=HI))).reshape(batch, LEN, D)
    x = x + low_back(proj(attended, w_out))
    normed = low(layer_norm(x, norms[2], norms[3]))
    upper = low_back(proj(normed, w_up))
    active = low(jax.nn.gelu(upper, approximate=False))
    return x + low_back(proj(active, w_down))

def forward(params, target, maskf, count):
    qkv_w, out_w, up_w, down_w, patch_maps, norm_params = params
    embed = low(patch_maps[:P_SIZE])
    head = low(patch_maps[P_SIZE:2 * P_SIZE])
    pos = patch_maps[2 * P_SIZE:]
    inputs = target * (1.0 - maskf[..., None])
    x = low_back(jnp.einsum('blp,pd->bld', inputs, embed, precision=HI)) + pos
    for index in range(L):
        x = layer(x, qkv_w[index], out_w[index], up_w[index], down_w[index], norm_params[4 * index:4 * index + 4])
    final = low(layer_norm(x, norm_params[4 * L], norm_params[4 * L + 1]))
    pred = low_back(jnp.einsum('bld,pd->blp', final, head, precision=HI))
    err = pred - target
    return jnp.sum(maskf * lax.optimization_barrier(jnp.mean(err * err, -1))) / count

def adam(weight, first, second, grad, rate):
    first = BETA_ONE * first + (1 - BETA_ONE) * grad
    second = BETA_TWO * second + (1 - BETA_TWO) * grad * grad
    fixed_one = first / (1 - BETA_ONE ** STEP_COUNT)
    fixed_two = second / (1 - BETA_TWO ** STEP_COUNT)
    weight = weight - rate * (fixed_one / (jnp.sqrt(fixed_two) + ADAM_EPS) + DECAY * weight)
    return (weight, first, second)

def reference(series, mask, qkv_w, out_w, up_w, down_w, patch_maps, norm_params, qkv_m, out_m, up_m, down_m, patch_m, norm_m, qkv_v, out_v, up_v, down_v, patch_v, norm_v):
    params = (qkv_w, out_w, up_w, down_w, patch_maps, norm_params)
    block = math.gcd(SERIES, max(1, 4096 // LEN))
    targets = series.astype(jnp.float32).reshape(SERIES // block, block, LEN, P_SIZE)
    masks = mask.astype(jnp.float32).reshape(SERIES // block, block, LEN)
    count = SERIES * MASKED

    def one_block(total, item):
        target, maskf = item
        value, back = jax.vjp(lambda prm: forward(prm, target, maskf, count), params)
        grads = back(jnp.ones_like(value))[0]
        return ((total[0] + value, jax.tree.map(jnp.add, total[1], grads)), None)
    start = (jnp.zeros((), jnp.float32), jax.tree.map(jnp.zeros_like, params))
    (loss, grads), _ = lax.scan(one_block, start, (targets, masks))
    total = jnp.zeros((), jnp.float32)
    for grad in grads:
        total = total + jnp.sum(grad * grad)
    grad_norm = jnp.sqrt(total)
    factor = CLIP / jnp.maximum(grad_norm, CLIP)
    firsts = (qkv_m, out_m, up_m, down_m, patch_m, norm_m)
    seconds = (qkv_v, out_v, up_v, down_v, patch_v, norm_v)
    rates = (RATE, RATE, RATE, RATE, TABLE_RATE, TABLE_RATE)
    results = [adam(w, m, v, g * factor, r) for w, m, v, g, r in zip(params, firsts, seconds, grads, rates)]
    news = tuple((r[0] for r in results))
    new_m = tuple((r[1] for r in results))
    new_v = tuple((r[2] for r in results))
    return (loss, grad_norm, news[0], news[1], news[2], news[3], news[4], news[5], new_m[0], new_m[1], new_m[2], new_m[3], new_m[4], new_m[5], new_v[0], new_v[1], new_v[2], new_v[3], new_v[4], new_v[5])
```

```python
import jax
import jax.numpy as jnp
from jax import lax
from jax.experimental import pallas as pl
from jax.experimental.pallas import tpu as pltpu
from jax.sharding import PartitionSpec as P

D = 512
H = 8
DH = 64
FF = 2048
P_SIZE = 64
LEN = 256
L = 2
MASKED = 102

EPS = 1e-05
CLIP = 0.001
RATE = 0.05
TABLE_RATE = 0.3
BETA_ONE = 0.9
BETA_TWO = 0.999
ADAM_EPS = 1e-08
DECAY = 0.1
STEP_COUNT = 10

W = 512
F32 = jnp.float32
BF16 = jnp.bfloat16


def dense(left, right):
    return jnp.dot(left, right, preferred_element_type=F32)


def dense_tn(left, right):
    return lax.dot_general(left, right, (((0,), (0,)), ((), ())), preferred_element_type=F32)


def dense_nt(left, right):
    return lax.dot_general(left, right, (((1,), (1,)), ((), ())), preferred_element_type=F32)


def layer_norm(x, gain, bias):
    center = x - jnp.mean(x, -1, keepdims=True)
    spread = jnp.mean(center * center, -1, keepdims=True)
    return center * lax.rsqrt(spread + EPS) * gain + bias


def params(**more):
    return pltpu.CompilerParams(vmem_limit_bytes=60 * 2**20, **more)


def cost(flops, data, trans=0):
    return pl.CostEstimate(flops=int(flops), bytes_accessed=int(data), transcendentals=int(trans))


def whole(shape):
    return pl.BlockSpec(shape, lambda *_: (0,) * len(shape))


ANY = pl.BlockSpec(memory_space=pl.ANY)
SMEM = pl.BlockSpec(memory_space=pltpu.SMEM)


def permute(x, axis, mask, size):
    return lax.ppermute(x, axis, [(i, i ^ mask) for i in range(size)])


def pick(x, index):
    return lax.dynamic_index_in_dim(x, index, 0, keepdims=False)


class Place:
    def __init__(self):
        self.shards = lax.axis_size("shard")
        self.replicas = lax.axis_size("replica")
        self.chips = self.replicas // 2
        self.shard = lax.axis_index("shard")
        replica = lax.axis_index("replica")
        self.core = replica % 2
        self.chip = replica // 2

    def to_core(self, x):
        return permute(x, "replica", 1, self.replicas)

    def to_shard(self, x, mask):
        return permute(x, "shard", mask, self.shards)

    def to_chip(self, x, mask):
        return permute(x, "replica", 2 * mask, self.replicas)


def gather_group(place, mine):
    ours = [place.to_shard(mine, mask) for mask in range(1, place.shards)]
    return ours, [place.to_core(part) for part in ours]


def stages_of(size):
    found = []
    bit = 1
    while bit < size:
        radix = 4 if bit * 4 <= size else 2
        found.append((bit, radix))
        bit *= radix
    return found


def add_up(parts):
    total = parts[0].astype(F32)
    for part in parts[1:]:
        total = total + part.astype(F32)
    return total.astype(BF16)


def reduce_chips(place, x):
    stages = stages_of(place.chips)
    for bit, radix in stages:
        digit = (place.chip // bit) % radix
        x = x.reshape((radix, x.shape[0] // radix) + x.shape[1:])
        got = [place.to_chip(pick(x, digit ^ k), k * bit) for k in range(1, radix)]
        x = add_up([pick(x, digit)] + got)
    for bit, radix in reversed(stages):
        digit = (place.chip // bit) % radix
        got = [x] + [place.to_chip(x, k * bit) for k in range(1, radix)]
        x = jnp.concatenate([select_of(got, digit ^ k) for k in range(radix)], 0)
    return x


def select_of(items, index):
    out = items[0]
    for k in range(1, len(items)):
        out = jnp.where(index == k, items[k], out)
    return out


def reduce_shards(place, keep, other):
    pieces = [
        add_up([pick(keep, place.shard ^ k), pick(other, place.shard ^ k)])
        for k in range(place.shards)
    ]
    return add_up([pieces[0]] + [place.to_shard(pieces[k], k) for k in range(1, place.shards)])


def fill_weights(step, where_ref, sources, targets, sem):
    shard, core = where_ref[0], where_ref[1]
    count = (len(sources) - 1) // 2

    def copies():
        made = []
        for piece, index in [(sources[0], None)] + [(s, k) for k, s in enumerate(sources[1:])]:
            if index is None:
                at, half = shard, None
            else:
                at = shard ^ (index % count + 1)
                half = core if index < count else 1 - core
            made += targets(piece, at, half)
        return [pltpu.make_async_copy(s, t, sem.at[n]) for n, (s, t) in enumerate(made)]

    @pl.when(step == 0)
    def _():
        todo = copies()
        for copy in todo:
            copy.start()
        for copy in todo:
            copy.wait()


def attn_targets(w_ref, rows):
    def targets(piece, at, half):
        at = pl.ds(pl.multiple_of(at * rows, rows), rows)
        if half is None:
            return [(piece.at[h], w_ref.at[pl.ds(2 * h, 2), at]) for h in range(2)]
        return [(piece, w_ref.at[pl.ds(half * 2, 2), at])]

    return targets


def mlp_targets(up_ref, down_ref, rows):
    def one(piece, at, half):
        spot = pl.ds(pl.multiple_of(at * rows, rows), rows)
        return [
            (piece.at[pl.ds(0, 2)], up_ref.at[pl.ds(half * 2, 2), spot]),
            (piece.at[pl.ds(2, 2)], down_ref.at[pl.ds(at * 4 + half * 2, 2)]),
        ]

    def targets(piece, at, half):
        if half is None:
            return one(piece.at[0], at, 0) + one(piece.at[1], at, 1)
        return one(piece, at, half)

    return targets


def norm_parts(x):
    center = x - jnp.mean(x, -1, keepdims=True)
    rstd = lax.rsqrt(jnp.mean(center * center, -1, keepdims=True) + EPS)
    return center * rstd, rstd


def norm_back(xhat, rstd, dy, gain):
    dxh = dy * gain
    return rstd * (
        dxh - jnp.mean(dxh, -1, keepdims=True) - xhat * jnp.mean(dxh * xhat, -1, keepdims=True)
    )


def attn_fwd(place, where, x, norms, group):
    rows = D // place.shards
    seqs = x.shape[0] // LEN
    sources = len(group)

    def kernel(where_ref, x_ref, norm_ref, *refs):
        pieces, refs = refs[:sources], refs[sources:]
        mid_ref, qkv_ref, pt_ref, ot_ref, w_ref, sem = refs
        fill_weights(pl.program_id(0), where_ref, pieces, attn_targets(w_ref, rows), sem)
        x = x_ref[...]
        xhat, _ = norm_parts(x)
        a = (xhat * norm_ref[0:1, :] + norm_ref[1:2, :]).astype(BF16)
        q = (dense(a, w_ref[0]) * DH**-0.5).astype(BF16)
        k = dense(a, w_ref[1]).astype(BF16)
        v = dense(a, w_ref[2]).astype(BF16)
        qkv_ref[:, :D] = q
        qkv_ref[:, D : 2 * D] = k
        qkv_ref[:, 2 * D :] = v
        vt = v.T
        lane = lax.broadcasted_iota(jnp.int32, (LEN, 128), 1)
        for h in range(H):
            pair = slice(128 * (h // 2), 128 * (h // 2) + 128)
            one = slice(DH * h, DH * h + DH)
            own = (lane < DH) if h % 2 == 0 else (lane >= DH)
            st = dense_nt(k[:, pair], jnp.where(own, q[:, pair], 0))
            e = jnp.exp(st - jnp.max(st, axis=0, keepdims=True))
            p = (e * (1.0 / jnp.sum(e, axis=0, keepdims=True))).astype(BF16)
            pt_ref[h] = p
            ot_ref[one, :] = dense(vt[one, :], p).astype(BF16)
        mid_ref[...] = x + dense_tn(ot_ref[...], w_ref[3])

    n = x.shape[0]
    return pl.pallas_call(
        kernel,
        grid=(seqs,),
        in_specs=[SMEM, pl.BlockSpec((LEN, D), lambda i: (i, 0)), whole((4, D))] + [ANY] * sources,
        out_specs=[
            pl.BlockSpec((LEN, D), lambda i: (i, 0)),
            pl.BlockSpec((LEN, 3 * D), lambda i: (i, 0)),
            pl.BlockSpec((None, H, LEN, LEN), lambda i: (i, 0, 0, 0)),
            pl.BlockSpec((None, D, LEN), lambda i: (i, 0, 0)),
        ],
        out_shape=[
            jax.ShapeDtypeStruct((n, D), F32),
            jax.ShapeDtypeStruct((n, 3 * D), BF16),
            jax.ShapeDtypeStruct((seqs, H, LEN, LEN), BF16),
            jax.ShapeDtypeStruct((seqs, D, LEN), BF16),
        ],
        scratch_shapes=[pltpu.VMEM((4, D, W), BF16), pltpu.SemaphoreType.DMA((2 * sources,))],
        compiler_params=params(),
        cost_estimate=cost(2 * n * D * (4 * D + 2 * LEN), n * D * 20, n * H * LEN),
        name="attn_fwd",
    )(where, x, norms, *group)


def gelu_pair(u):
    z = jnp.abs(u) * 0.7071067811865476
    t = 1.0 / (1.0 + 0.3275911 * z)
    poly = t * (
        0.254829592
        + t * (-0.284496736 + t * (1.421413741 + t * (-1.453152027 + t * 1.061405429)))
    )
    e = jnp.exp(-z * z)
    tail = 0.5 * poly * e
    cdf = jnp.where(u >= 0, 1.0 - tail, tail)
    return u * cdf, cdf + u * e * 0.3989422804014327


def mlp_fwd(place, where, mid, norms, group):
    rows = D // place.shards
    n = mid.shape[0]
    sources = len(group)
    per = W // rows

    def kernel(where_ref, mid_ref, norm_ref, *refs):
        pieces, refs = refs[:sources], refs[sources:]
        out_ref, act_ref, gp_ref, up_ref, down_ref, sem = refs
        fill_weights(pl.program_id(0), where_ref, pieces, mlp_targets(up_ref, down_ref, rows), sem)
        mid = mid_ref[...]
        xhat, _ = norm_parts(mid)
        c = (xhat * norm_ref[2:3, :] + norm_ref[3:4, :]).astype(BF16)
        total = mid
        for b in range(FF // W):
            cols = slice(W * b, W * b + W)
            act, slope = gelu_pair(dense(c, up_ref[b]))
            act = act.astype(BF16)
            act_ref[:, cols] = act
            gp_ref[:, cols] = slope.astype(BF16)
            total = total + dense(act, down_ref[per * b : per * b + per].reshape(W, D))
        out_ref[...] = total

    return pl.pallas_call(
        kernel,
        grid=(n // LEN,),
        in_specs=[SMEM, pl.BlockSpec((LEN, D), lambda i: (i, 0)), whole((4, D))] + [ANY] * sources,
        out_specs=[
            pl.BlockSpec((LEN, D), lambda i: (i, 0)),
            pl.BlockSpec((LEN, FF), lambda i: (i, 0)),
            pl.BlockSpec((LEN, FF), lambda i: (i, 0)),
        ],
        out_shape=[
            jax.ShapeDtypeStruct((n, D), F32),
            jax.ShapeDtypeStruct((n, FF), BF16),
            jax.ShapeDtypeStruct((n, FF), BF16),
        ],
        scratch_shapes=[
            pltpu.VMEM((4, D, W), BF16),
            pltpu.VMEM((FF // rows, rows, D), BF16),
            pltpu.SemaphoreType.DMA((2 * sources + 2,)),
        ],
        compiler_params=params(),
        cost_estimate=cost(4 * n * D * FF, n * D * 24, n * FF * 2),
        name="mlp_fwd",
    )(where, mid, norms, *group)


def mlp_bwd(place, where, dz, mid, act, gp, norms, group):
    rows = D // place.shards
    n = mid.shape[0]
    sources = len(group)
    per = W // rows

    def kernel(where_ref, dz_ref, mid_ref, gp_ref, norm_ref, *refs):
        pieces, refs = refs[:sources], refs[sources:]
        dmid_ref, du_ref, c_ref, dm_ref, dn_ref, up_ref, down_ref, sem = refs
        i = pl.program_id(0)
        fill_weights(i, where_ref, pieces, mlp_targets(up_ref, down_ref, rows), sem)
        dz = dz_ref[...]
        dm = dz.astype(BF16)
        dm_ref[...] = dm
        xhat, rstd = norm_parts(mid_ref[...])
        gain = norm_ref[2:3, :]
        c_ref[...] = (xhat * gain + norm_ref[3:4, :]).astype(BF16)
        dc = jnp.zeros((LEN, D), F32)
        for b in range(FF // W):
            cols = slice(W * b, W * b + W)
            da = dense_nt(dm, down_ref[per * b : per * b + per].reshape(W, D))
            du = (gp_ref[:, cols].astype(F32) * da).astype(BF16)
            du_ref[:, cols] = du
            dc = dc + dense_nt(du, up_ref[b])
        dmid_ref[...] = dz + norm_back(xhat, rstd, dc, gain)

        @pl.when(i == 0)
        def _():
            dn_ref[...] = jnp.zeros_like(dn_ref)

        dn_ref[0:1, :] += jnp.sum(dc * xhat, 0, keepdims=True)
        dn_ref[1:2, :] += jnp.sum(dc, 0, keepdims=True)

    def row(width):
        return pl.BlockSpec((LEN, width), lambda i: (i, 0))

    return pl.pallas_call(
        kernel,
        grid=(n // LEN,),
        in_specs=[SMEM, row(D), row(D), row(FF), whole((4, D))] + [ANY] * sources,
        out_specs=[row(D), row(FF), row(D), row(D), whole((8, D))],
        out_shape=[
            jax.ShapeDtypeStruct((n, D), F32),
            jax.ShapeDtypeStruct((n, FF), BF16),
            jax.ShapeDtypeStruct((n, D), BF16),
            jax.ShapeDtypeStruct((n, D), BF16),
            jax.ShapeDtypeStruct((8, D), F32),
        ],
        scratch_shapes=[
            pltpu.VMEM((4, D, W), BF16),
            pltpu.VMEM((FF // rows, rows, D), BF16),
            pltpu.SemaphoreType.DMA((2 * sources + 2,)),
        ],
        compiler_params=params(),
        cost_estimate=cost(4 * n * D * FF, n * D * 32),
        name="mlp_bwd",
    )(where, dz, mid, gp, norms, *group)


def attn_bwd(place, where, dmid, x, qkv, pt, ot, norms, group):
    rows = D // place.shards
    n = x.shape[0]
    seqs = n // LEN
    sources = len(group)

    def kernel(where_ref, dmid_ref, x_ref, qkv_ref, pt_ref, ot_ref, norm_ref, *refs):
        pieces, refs = refs[:sources], refs[sources:]
        dx_ref, dqkv_ref, a_ref, dh_ref, dn_ref, w_ref, dqt_ref, sem = refs
        i = pl.program_id(0)
        fill_weights(i, where_ref, pieces, attn_targets(w_ref, rows), sem)
        dmid = dmid_ref[...]
        dh = dmid.astype(BF16)
        dh_ref[...] = dh
        do = dense_nt(dh, w_ref[3]).astype(BF16)
        along = do.T.astype(F32) * ot_ref[...].astype(F32)
        q = qkv_ref[:, :D]
        k = qkv_ref[:, D : 2 * D]
        v = qkv_ref[:, 2 * D :]
        kt = k.T
        lane = lax.broadcasted_iota(jnp.int32, (LEN, 128), 1)
        for j in range(H // 2):
            pair = slice(128 * j, 128 * j + 128)
            dk = jnp.zeros((LEN, 128), F32)
            dv = jnp.zeros((LEN, 128), F32)
            for h in (2 * j, 2 * j + 1):
                one = slice(DH * h, DH * h + DH)
                own = (lane < DH) if h % 2 == 0 else (lane >= DH)
                doh = jnp.where(own, do[:, pair], 0)
                pth = pt_ref[h]
                dpt = dense_nt(v[:, pair], doh)
                delta = jnp.sum(along[one, :], axis=0, keepdims=True)
                dst = (pth.astype(F32) * (dpt - delta)).astype(BF16)
                dv = dv + dense(pth, doh)
                dk = dk + dense(dst, jnp.where(own, q[:, pair], 0))
                dqt_ref[one, :] = (dense(kt[one, :], dst) * DH**-0.5).astype(BF16)
            dqkv_ref[:, D + 128 * j : D + 128 * j + 128] = dk.astype(BF16)
            dqkv_ref[:, 2 * D + 128 * j : 2 * D + 128 * j + 128] = dv.astype(BF16)
        dqkv_ref[:, :D] = dqt_ref[...].T
        da = dense_nt(dqkv_ref[:, :D], w_ref[0])
        da = da + dense_nt(dqkv_ref[:, D : 2 * D], w_ref[1])
        da = da + dense_nt(dqkv_ref[:, 2 * D :], w_ref[2])
        xhat, rstd = norm_parts(x_ref[...])
        gain = norm_ref[0:1, :]
        a_ref[...] = (xhat * gain + norm_ref[1:2, :]).astype(BF16)
        dx_ref[...] = dmid + norm_back(xhat, rstd, da, gain)

        @pl.when(i == 0)
        def _():
            dn_ref[...] = jnp.zeros_like(dn_ref)

        dn_ref[0:1, :] += jnp.sum(da * xhat, 0, keepdims=True)
        dn_ref[1:2, :] += jnp.sum(da, 0, keepdims=True)

    def row(width):
        return pl.BlockSpec((LEN, width), lambda i: (i, 0))

    return pl.pallas_call(
        kernel,
        grid=(seqs,),
        in_specs=[
            SMEM,
            row(D),
            row(D),
            row(3 * D),
            pl.BlockSpec((None, H, LEN, LEN), lambda i: (i, 0, 0, 0)),
            pl.BlockSpec((None, D, LEN), lambda i: (i, 0, 0)),
            whole((4, D)),
        ]
        + [ANY] * sources,
        out_specs=[row(D), row(3 * D), row(D), row(D), whole((8, D))],
        out_shape=[
            jax.ShapeDtypeStruct((n, D), F32),
            jax.ShapeDtypeStruct((n, 3 * D), BF16),
            jax.ShapeDtypeStruct((n, D), BF16),
            jax.ShapeDtypeStruct((n, D), BF16),
            jax.ShapeDtypeStruct((8, D), F32),
        ],
        scratch_shapes=[
            pltpu.VMEM((4, D, W), BF16),
            pltpu.VMEM((D, LEN), BF16),
            pltpu.SemaphoreType.DMA((2 * sources,)),
        ],
        compiler_params=params(),
        cost_estimate=cost(2 * n * D * (4 * D + 5 * LEN), n * D * 32),
        name="attn_bwd",
    )(where, dmid, x, qkv, pt, ot, norms, *group)


def grad_mlp(place, where, c, du, act, dm):
    shards = place.shards
    rows = D // shards
    n = c.shape[0]
    wide = FF // (2 * shards)

    def half_of(p, where_ref):
        return where_ref[1] ^ (1 - p)

    def kernel(where_ref, c_ref, du_ref, act_ref, dm_ref, send_ref, keep_ref, ct_ref):
        p, i = pl.program_id(0), pl.program_id(1)

        @pl.when((p == 0) & (i == 0))
        def _():
            ct_ref[...] = c_ref[...].T

        def put(out_ref):
            @pl.when(i < 2)
            def _():
                out_ref[:, i] = dense(ct_ref[...], du_ref[...]).astype(BF16).reshape(shards, rows, W)

            @pl.when(i >= 2)
            def _():
                block = dense_tn(act_ref[...], dm_ref[...]).astype(BF16)
                out_ref[i - 2, 2:4] = block.reshape(2, rows, W)

        @pl.when(p == 0)
        def _():
            put(send_ref)

        @pl.when(p == 1)
        def _():
            put(keep_ref)

    shape = (shards, 4, rows, W)
    return pl.pallas_call(
        kernel,
        grid_spec=pltpu.PrefetchScalarGridSpec(
            num_scalar_prefetch=1,
            grid=(2, 2 + shards),
            in_specs=[
                whole((n, D)),
                pl.BlockSpec((n, W), lambda p, i, w: (0, 2 * half_of(p, w) + jnp.minimum(i, 1))),
                pl.BlockSpec(
                    (n, wide), lambda p, i, w: (0, 2 * jnp.maximum(i - 2, 0) + half_of(p, w))
                ),
                whole((n, D)),
            ],
            out_specs=[whole(shape), whole(shape)],
            scratch_shapes=[pltpu.VMEM((D, n), BF16)],
        ),
        out_shape=[jax.ShapeDtypeStruct(shape, BF16)] * 2,
        compiler_params=params(),
        cost_estimate=cost(4 * n * D * FF, n * (4 * D + 4 * FF) + 4 * D * FF),
        name="grad_mlp",
    )(where, c, du, act, dm)


def grad_attn(place, where, a, dqkv, ot, dh):
    shards = place.shards
    rows = D // shards
    n = a.shape[0]
    seqs = n // LEN

    def block_of(p, i, where_ref):
        return 2 * (where_ref[1] ^ (1 - p)) + i

    def kernel(where_ref, a_ref, dqkv_ref, ot_ref, dh_ref, send_ref, keep_ref, at_ref):
        p, i = pl.program_id(0), pl.program_id(1)
        block = block_of(p, i, where_ref)

        @pl.when((p == 0) & (i == 0))
        def _():
            at_ref[...] = a_ref[...].T

        def put(out_ref):
            @pl.when(block < 3)
            def _():
                out_ref[:, i] = dense(at_ref[...], dqkv_ref[...]).astype(BF16).reshape(shards, rows, W)

            @pl.when(block == 3)
            def _():
                total = dense(ot_ref[0], dh_ref[:LEN, :])
                for s in range(1, seqs):
                    total = total + dense(ot_ref[s], dh_ref[LEN * s : LEN * s + LEN, :])
                out_ref[:, i] = total.astype(BF16).reshape(shards, rows, W)

        @pl.when(p == 0)
        def _():
            put(send_ref)

        @pl.when(p == 1)
        def _():
            put(keep_ref)

    shape = (shards, 2, rows, W)
    return pl.pallas_call(
        kernel,
        grid_spec=pltpu.PrefetchScalarGridSpec(
            num_scalar_prefetch=1,
            grid=(2, 2),
            in_specs=[
                whole((n, D)),
                pl.BlockSpec((n, W), lambda p, i, w: (0, jnp.minimum(block_of(p, i, w), 2))),
                whole((seqs, D, LEN)),
                whole((n, D)),
            ],
            out_specs=[whole(shape), whole(shape)],
            scratch_shapes=[pltpu.VMEM((D, n), BF16)],
        ),
        out_shape=[jax.ShapeDtypeStruct(shape, BF16)] * 2,
        compiler_params=params(),
        cost_estimate=cost(8 * n * D * D, n * 14 * D + 8 * D * D),
        name="grad_attn",
    )(where, a, dqkv, ot, dh)


def adam(weight, first, second, grad, rate):
    first = BETA_ONE * first + (1 - BETA_ONE) * grad
    second = BETA_TWO * second + (1 - BETA_TWO) * grad * grad
    fixed_one = first / (1 - BETA_ONE**STEP_COUNT)
    fixed_two = second / (1 - BETA_TWO**STEP_COUNT)
    weight = weight - rate * (fixed_one / (jnp.sqrt(fixed_two) + ADAM_EPS) + DECAY * weight)
    return (weight, first, second)


def on_device(
    series,
    mask,
    qkv_w,
    out_w,
    up_w,
    down_w,
    patch_maps,
    norm_params,
    qkv_m,
    out_m,
    up_m,
    down_m,
    patch_m,
    norm_m,
    qkv_v,
    out_v,
    up_v,
    down_v,
    patch_v,
    norm_v,
):
    place = Place()
    shards = place.shards
    rows = D // shards
    seqs = series.shape[0]
    count = MASKED * seqs * shards * place.replicas
    where = jnp.stack([place.shard, place.core]).astype(jnp.int32)

    small_rows = 400
    table = jnp.concatenate(
        [patch_maps, norm_params, jnp.zeros((small_rows - 394, rows), F32)], 0
    ).reshape(2, small_rows // 2, rows)
    ours, theirs = gather_group(place, pick(table, place.core))
    parts = [table] + [
        jnp.where(place.core == 0, jnp.stack([a, b]), jnp.stack([b, a])) for a, b in zip(ours, theirs)
    ]
    maps = jnp.concatenate(
        [select_of(parts, place.shard ^ j).reshape(small_rows, rows) for j in range(shards)], 1
    )
    embed = maps[:P_SIZE].astype(BF16)
    head = maps[P_SIZE : 2 * P_SIZE].astype(BF16)
    pos = maps[2 * P_SIZE : 2 * P_SIZE + LEN]
    norms_all = maps[2 * P_SIZE + LEN : 2 * P_SIZE + LEN + 4 * L + 2]

    attn_groups = []
    mlp_groups = []
    for index in range(L):
        cols = qkv_w[index].reshape(rows, 3, W)
        local = jnp.concatenate([cols.transpose(1, 0, 2), out_w[index][None]], 0).astype(BF16)
        local = local.reshape(2, 2, rows, W)
        ours, theirs = gather_group(place, pick(local, place.core))
        attn_groups.append([local] + ours + theirs)
        up = up_w[index].reshape(rows, 2, 2, W).transpose(1, 2, 0, 3)
        down = down_w[index].reshape(2, 2, rows, W)
        local = jnp.concatenate([up, down], 1).astype(BF16)
        ours, theirs = gather_group(place, pick(local, place.core))
        mlp_groups.append([local] + ours + theirs)

    target = series.reshape(seqs * LEN, P_SIZE).astype(F32)
    maskf = mask.reshape(seqs * LEN, 1).astype(F32)
    inputs = (target * (1.0 - maskf)).astype(BF16)
    x = dense(inputs, embed) + jnp.tile(pos, (seqs, 1))
    saved = []
    for index in range(L):
        norms = norms_all[4 * index : 4 * index + 4]
        mid, qkv, pt, ot = attn_fwd(place, where, x, norms, attn_groups[index])
        y, act, gp = mlp_fwd(place, where, mid, norms, mlp_groups[index])
        saved.append((x, mid, qkv, pt, ot, act, gp, norms))
        x = y

    final = layer_norm(x, norms_all[4 * L], norms_all[4 * L + 1])
    final_low = final.astype(BF16)
    err = dense_nt(final_low, head) - target
    loss = jnp.sum(maskf * jnp.mean(err * err, -1, keepdims=True)).reshape(1, 1)
    grad_pred = (maskf * err * (2.0 / (P_SIZE * count))).astype(BF16)
    g_head = dense_tn(grad_pred, final_low)
    _, final_back = jax.vjp(layer_norm, x, norms_all[4 * L], norms_all[4 * L + 1])
    grad, gain_f, bias_f = final_back(dense(grad_pred, head))

    pieces = []
    norm_grads = [None] * L
    for index in reversed(range(L)):
        x, mid, qkv, pt, ot, act, gp, norms = saved[index]
        dmid, du, c, dm, dn_mlp = mlp_bwd(place, where, grad, mid, act, gp, norms, mlp_groups[index])
        send, keep = grad_mlp(place, where, c, du, act, dm)
        piece_mlp = reduce_shards(place, keep, place.to_core(send))
        grad, dqkv, a, dh, dn_attn = attn_bwd(
            place, where, dmid, x, qkv, pt, ot, norms, attn_groups[index]
        )
        send, keep = grad_attn(place, where, a, dqkv, ot, dh)
        piece_attn = reduce_shards(place, keep, place.to_core(send))
        norm_grads[index] = jnp.concatenate([dn_attn[:2], dn_mlp[:2]], 0)
        piece_mlp = reduce_chips(place, piece_mlp.reshape(4 * rows, W))
        piece_attn = reduce_chips(place, piece_attn.reshape(2 * rows, W))
        pieces.append((index, piece_attn, piece_mlp))

    g_embed = dense_tn(inputs, grad.astype(BF16))
    g_table = jnp.sum(grad.reshape(seqs, LEN, D), 0)
    g_small = jnp.concatenate(
        [g_embed, g_head, g_table] + norm_grads + [jnp.stack([gain_f, bias_f])], 0
    )
    g_small = jnp.pad(g_small, ((0, small_rows - g_small.shape[0]), (0, 0))).astype(BF16)
    g_small = g_small.reshape(2, small_rows // 2, shards, rows).transpose(0, 2, 1, 3)
    other = place.to_core(pick(g_small, 1 - place.core))
    piece = reduce_shards(place, pick(g_small, place.core), other)
    pad = -piece.shape[0] % (8 * place.chips)
    piece = reduce_chips(place, jnp.pad(piece, ((0, pad), (0, 0))))
    piece_small = piece[: small_rows // 2]

    for bit in range(shards.bit_length() - 1):
        loss = loss + place.to_shard(loss, 1 << bit)
    for bit in range(place.chips.bit_length() - 1):
        loss = loss + place.to_chip(loss, 1 << bit)
    loss = (loss + place.to_core(loss)).reshape(()) / count

    squares = jnp.zeros((), F32)
    for part in [piece_small] + [p for _, a, b in pieces for p in (a, b)]:
        part = part.astype(F32)
        squares = squares + jnp.sum(part * part)
    squares = squares.reshape(1, 1)
    squares = squares + place.to_core(squares)
    squares = sum([place.to_shard(squares, k) for k in range(1, shards)], squares)
    grad_norm = jnp.sqrt(squares.reshape(()))
    factor = CLIP / jnp.maximum(grad_norm, CLIP)

    def halves(mine):
        other = place.to_core(mine)
        first = jnp.where(place.core == 0, mine, other)
        second = jnp.where(place.core == 0, other, mine)
        return first, second

    big = [None] * L
    for index, piece_attn, piece_mlp in pieces:
        low, high = halves(piece_attn)
        low, high = low.reshape(2, rows, W), high.reshape(2, rows, W)
        g_qkv = jnp.concatenate([low[0], low[1], high[0]], 1)
        g_out = high[1]
        low, high = halves(piece_mlp)
        low, high = low.reshape(4, rows, W), high.reshape(4, rows, W)
        g_up = jnp.concatenate([low[0], low[1], high[0], high[1]], 1)
        g_down = jnp.concatenate([low[2:].reshape(2 * rows, W), high[2:].reshape(2 * rows, W)], 0)
        big[index] = (g_qkv, g_out, g_up, g_down)
    low, high = halves(piece_small)
    g_small = jnp.concatenate([low, high], 0)
    grads_all = tuple(jnp.stack([big[i][j] for i in range(L)]) for j in range(4))
    grads_all = grads_all + (g_small[:384], g_small[384:394])

    weights = (qkv_w, out_w, up_w, down_w, patch_maps, norm_params)
    firsts = (qkv_m, out_m, up_m, down_m, patch_m, norm_m)
    seconds = (qkv_v, out_v, up_v, down_v, patch_v, norm_v)
    rates = (RATE, RATE, RATE, RATE, TABLE_RATE, TABLE_RATE)
    results = [
        adam(w, m, v, g.astype(F32) * factor, r)
        for w, m, v, g, r in zip(weights, firsts, seconds, grads_all, rates)
    ]
    news = tuple(r[0] for r in results)
    new_m = tuple(r[1] for r in results)
    new_v = tuple(r[2] for r in results)
    return (loss, grad_norm) + news + new_m + new_v


def solution(mesh):
    batch = P(("shard", "replica"), None)
    stack = P(None, "shard", None)
    flat = P(None, "shard")
    state = (stack, stack, stack, stack, flat, flat)
    return jax.shard_map(
        on_device,
        mesh=mesh,
        in_specs=(batch, batch) + state * 3,
        out_specs=(P(), P()) + state * 3,
        check_vma=False,
    )
```

```python
import jax
import jax.numpy as jnp
from jax import lax
from jax.experimental import pallas as pl
from jax.experimental.pallas import tpu as pltpu
from jax.sharding import PartitionSpec as P

D = 512
H = 8
DH = 64
FF = 2048
P_SIZE = 64
LEN = 256
L = 2
MASKED = 102

EPS = 1e-05
CLIP = 0.001
RATE = 0.05
TABLE_RATE = 0.3
BETA_ONE = 0.9
BETA_TWO = 0.999
ADAM_EPS = 1e-08
DECAY = 0.1
STEP_COUNT = 10

W = 512
SMALL = 512
F32 = jnp.float32
BF16 = jnp.bfloat16


def dense(left, right):
    return jnp.dot(left, right, preferred_element_type=F32)


def dense_tn(left, right):
    return lax.dot_general(left, right, (((0,), (0,)), ((), ())), preferred_element_type=F32)


def dense_nt(left, right):
    return lax.dot_general(left, right, (((1,), (1,)), ((), ())), preferred_element_type=F32)


def layer_norm(x, gain, bias):
    center = x - jnp.mean(x, -1, keepdims=True)
    spread = jnp.mean(center * center, -1, keepdims=True)
    return center * lax.rsqrt(spread + EPS) * gain + bias


def params(**more):
    return pltpu.CompilerParams(vmem_limit_bytes=60 * 2**20, **more)


def cost(flops, data, trans=0):
    return pl.CostEstimate(flops=int(flops), bytes_accessed=int(data), transcendentals=int(trans))


def whole(shape):
    return pl.BlockSpec(shape, lambda *_: (0,) * len(shape))


ANY = pl.BlockSpec(memory_space=pl.ANY)
SMEM = pl.BlockSpec(memory_space=pltpu.SMEM)


def permute(x, axis, mask, size):
    return lax.ppermute(x, axis, [(i, i ^ mask) for i in range(size)])


def pick(x, index):
    return lax.dynamic_index_in_dim(x, index, 0, keepdims=False)


class Place:
    def __init__(self):
        self.shards = lax.axis_size("shard")
        self.replicas = lax.axis_size("replica")
        self.chips = self.replicas // 2
        self.shard = lax.axis_index("shard")
        replica = lax.axis_index("replica")
        self.core = replica % 2
        self.chip = replica // 2

    def to_core(self, x):
        return permute(x, "replica", 1, self.replicas)

    def to_shard(self, x, mask):
        return permute(x, "shard", mask, self.shards)

    def to_chip(self, x, mask):
        return permute(x, "replica", 2 * mask, self.replicas)


def gate(x, *after):
    return lax.optimization_barrier((x,) + after)[0]


def gather_shards(place, mine):
    return [place.to_shard(mine, mask) for mask in range(1, place.shards)]


def gather_cores(place, ours, *after):
    return place.to_core(jnp.stack(gates(ours, *after)))


def gates(items, *after):
    return list(lax.optimization_barrier(tuple(items) + after)[: len(items)])


def bits_of(size):
    return list(range(size.bit_length() - 1))


def total_of(values):
    total = values[0].astype(F32)
    for value in values[1:]:
        total = total + value.astype(F32)
    return total


def combine(where, jobs, name):
    lanes = W // 2
    arrays, leads, plans, shapes = [], [], [], []

    def number(array, lead):
        for n, known in enumerate(arrays):
            if known is array:
                return n
        arrays.append(array)
        leads.append(lead)
        return len(arrays) - 1

    for segments, lead, cut, bit in jobs:
        plans.append([[(number(a, lead), f, b) for a, f, b in parts] for parts in segments])
        blocks = sum(parts[0][2] for parts in segments)
        rows = segments[0][0][0].shape[-2]
        if cut is None:
            shapes.append(lead + (blocks, rows, W))
        elif cut == "rows":
            shapes += [lead + (blocks, rows // 2, W)] * 2
        else:
            shapes += [lead[:cut] + lead[cut + 1 :] + (blocks, rows, W)] * 2
    arrays = [a.reshape(lead + a.shape[-3:]) for a, lead in zip(arrays, leads)]

    def block(shape):
        zeros = (0,) * (len(shape) - 1)
        return pl.BlockSpec(shape[:-1] + (lanes,), lambda i: zeros + (i,))

    def kernel(where_ref, *refs):
        ins, outs = refs[: len(arrays)], list(refs[len(arrays) :])
        for (segments, lead, cut, bit), plan in zip(jobs, plans):
            some = (slice(None),) * len(lead)
            fewer = (slice(None),) * (len(lead) - (cut is not None and cut != "rows"))
            if cut is None:
                targets = [(outs.pop(0), None)]
            else:
                value = where_ref[bit]
                targets = [(outs.pop(0), 1 - value), (outs.pop(0), value)]
            for out_ref, at in targets:
                start = 0
                for parts in plan:
                    got = []
                    for n, f, b in parts:
                        index = some
                        if cut is not None and cut != "rows":
                            index = some[:cut] + (at,) + some[cut + 1 :]
                        index += (slice(f, f + b),)
                        if cut == "rows":
                            few = ins[n].shape[-2] // 2
                            index += (pl.ds(pl.multiple_of(at * few, few), few),)
                        got.append(ins[n][index])
                    out_ref[fewer + (slice(start, start + parts[0][2]),)] = total_of(got).astype(BF16)
                    start += parts[0][2]

    size = sum(a.size for a in arrays) * 4
    return pl.pallas_call(
        kernel,
        grid=(2,),
        in_specs=[SMEM] + [block(a.shape) for a in arrays],
        out_specs=[block(s) for s in shapes],
        out_shape=[jax.ShapeDtypeStruct(s, BF16) for s in shapes],
        compiler_params=params(),
        cost_estimate=cost(size, size),
        name=name,
    )(where, *arrays)


class Flow:
    def __init__(self, place, where, name, spread):
        self.place, self.where, self.name, self.spread = place, where, name, spread
        self.bits = bits_of(place.shards)
        self.step = 0
        self.sources = []
        self.ranges = []

    def begin(self, send, keep, *ranges):
        other = self.place.to_core(send)
        for first, blocks, order in ranges:
            self.ranges.append((len(self.sources), first, blocks, order))
        self.sources += [keep, other]
        self.token = send
        return send

    def shards_step(self, *after):
        place, bits = self.place, self.bits
        if self.step == 0:
            flat = gates(self.sources, *after)
            parts = [[(flat[n], f, b), (flat[n + 1], f, b)] for n, f, b, _ in self.ranges]
            self.left = [list(reversed(bits)) for _ in self.ranges]
        else:
            flat = gates([x for pair in self.parts for x in pair], *after)
            parts = [[(x, 0, x.shape[-3]) for x in flat[2 * n : 2 * n + 2]] for n in range(len(self.ranges))]
        jobs, chosen = [], []
        for n, (_, _, _, order) in enumerate(self.ranges):
            bit = (bits if order == 0 else bits[::-1])[self.step]
            lead = (2,) * len(self.left[n])
            jobs.append(([parts[n]], lead, self.left[n].index(bit), 2 + bit))
            self.left[n].remove(bit)
            chosen.append(bit)
        out = combine(self.where, jobs, self.name)
        self.parts = [
            [out[2 * n + 1], place.to_shard(out[2 * n], 1 << bit)] for n, bit in enumerate(chosen)
        ]
        return out[0]

    def chips_step(self, *after):
        bit = self.step - len(self.bits)
        flat = gates([x for pair in self.parts for x in pair], *after)
        segments = [
            [(x, 0, x.shape[-3]) for x in flat[2 * n : 2 * n + 2]] for n in range(len(flat) // 2)
        ]
        if bit == 0 and self.spread:
            send, stay = combine(
                self.where, [(segments, (), "rows", 2 + len(self.bits))], self.name
            )
        else:
            send = combine(self.where, [(segments, (), None, 0)], self.name)[0]
            stay = send
        self.parts = [[stay, self.place.to_chip(send, 1 << bit)]]
        return send

    def advance(self, *after):
        if self.step < len(self.bits):
            self.token = self.shards_step(*after)
        else:
            self.token = self.chips_step(*after)
        self.step += 1
        return self.token

    def last(self):
        return self.step == len(self.bits) + len(bits_of(self.place.chips))

    def finish(self, *after):
        place = self.place
        flat = gates(self.parts[0], *after)
        segments = [[(x, 0, x.shape[-3]) for x in flat]]
        mine = combine(self.where, [(segments, (), None, 0)], self.name)[0]
        self.token = mine
        if not self.spread:
            return [mine, place.to_core(mine)]
        there = place.to_chip(mine, 1)
        return [mine, place.to_core(mine), there, place.to_core(there)]


def square_sum(pieces):
    def kernel(*refs):
        total = jnp.zeros((1, W), F32)
        for ref in refs[:-1]:
            for b in range(ref.shape[0]):
                x = ref[b].astype(F32)
                total = total + jnp.sum(x * x, 0, keepdims=True)
        refs[-1][...] = jnp.sum(total, 1, keepdims=True)

    return pl.pallas_call(
        kernel,
        grid=(1,),
        in_specs=[whole(p.shape) for p in pieces],
        out_specs=whole((1, 1)),
        out_shape=jax.ShapeDtypeStruct((1, 1), F32),
        compiler_params=params(),
        name="square_sum",
    )(*pieces)


def fill_weights(step, where_ref, sources, targets, sem):
    shard, core = where_ref[0], where_ref[1]
    count = len(sources) - 2

    @pl.when(step == 0)
    def _():
        made = targets(sources[0], shard, None)
        for k in range(count):
            made += targets(sources[1 + k], shard ^ (k + 1), core)
            made += targets(sources[-1].at[k], shard ^ (k + 1), 1 - core)
        todo = [pltpu.make_async_copy(s, t, sem.at[n]) for n, (s, t) in enumerate(made)]
        for copy in todo:
            copy.start()
        for copy in todo:
            copy.wait()


def attn_targets(w_ref, rows):
    def targets(piece, at, half):
        if half is None:
            return [(piece.at[pl.ds(0, 4)], w_ref.at[:, pl.ds(pl.multiple_of(at * rows, rows), rows)])]
        start = pl.multiple_of(at * rows + half * (rows // 2), rows // 2)
        return [(piece.at[pl.ds(0, 4)], w_ref.at[:, pl.ds(start, rows // 2)])]

    return targets


def mlp_targets(up_ref, down_ref, rows):
    def targets(piece, at, half):
        few = rows if half is None else rows // 2
        skip = 0 if half is None else half * few
        start = pl.multiple_of(at * rows + skip, few)
        skip = pl.multiple_of(skip, few) if half is not None else 0
        return [
            (piece.at[pl.ds(0, 4)], up_ref.at[:, pl.ds(start, few)]),
            (piece.at[pl.ds(4, 4)], down_ref.at[pl.ds(at * 4, 4), pl.ds(skip, few)]),
        ]

    return targets


def pack(place, where, index, tall, wide, small):
    rows = D // place.shards
    half = rows // 2
    wide = [x.reshape(L, 4, rows, W) for x in wide]
    total = sum(x.shape[2] // W for x in tall) + 4 * len(wide) + 2 * bool(small)
    count = len(tall) + len(wide)

    def kernel(where_ref, *refs):
        full_ref, mine_ref = refs[count + len(small) : count + len(small) + 2]

        def run(core):
            own = slice(core * half, core * half + half)
            at = 0
            for ref in refs[: len(tall)]:
                for b in range(ref.shape[1] // W):
                    block = ref[:, W * b : W * b + W].astype(BF16)
                    full_ref[at] = block
                    mine_ref[at] = block[own]
                    at += 1
            for ref in refs[len(tall) : count]:
                for b in range(4):
                    block = ref[b].astype(BF16)
                    full_ref[at] = block
                    mine_ref[at] = block[own]
                    at += 1
            if small:
                table_ref = refs[-1]
                start = 0
                for ref in refs[count : count + len(small)]:
                    table_ref[start : start + ref.shape[0]] = ref[...]
                    start += ref.shape[0]
                table_ref[start:] = jnp.zeros((SMALL - start, rows), F32)
                for h in range(2):
                    for q in range(W // rows):
                        first = h * (SMALL // 2) + q * half
                        value = table_ref[first : first + half, :]
                        high = value.astype(BF16)
                        spot = slice(q * rows, q * rows + rows)
                        for n, x in enumerate((high, (value - high.astype(F32)).astype(BF16))):
                            full_ref[at + n, h * half : h * half + half, spot] = x
                            if h == core:
                                mine_ref[at + n, :, spot] = x

        for core in range(2):

            @pl.when(where_ref[1] == core)
            def _(core=core):
                run(core)

    return pl.pallas_call(
        kernel,
        grid=(1,),
        in_specs=[SMEM]
        + [pl.BlockSpec((None, rows, x.shape[2]), lambda i: (index, 0, 0)) for x in tall]
        + [pl.BlockSpec((None, 4, rows, W), lambda i: (index, 0, 0, 0)) for x in wide]
        + [whole(x.shape) for x in small],
        out_specs=[whole((total, rows, W)), whole((total, half, W))],
        out_shape=[
            jax.ShapeDtypeStruct((total, rows, W), BF16),
            jax.ShapeDtypeStruct((total, half, W), BF16),
        ],
        scratch_shapes=[pltpu.VMEM((SMALL, rows), F32)] * bool(small),
        compiler_params=params(),
        cost_estimate=cost(total * rows * W, total * rows * W * 7),
        name="pack",
    )(where, *tall, *wide, *small)


def embed_step(place, where, target, maskf, group):
    shards = place.shards
    rows = D // shards
    half = rows // 2
    n = target.shape[0]
    sources = len(group)

    def kernel(where_ref, target_ref, mask_ref, *refs):
        pieces, refs = refs[:sources], refs[sources:]
        x_ref, inputs_ref, head_ref, norm_ref, got_ref, table_ref, sem = refs

        def targets(piece, at, part):
            start = 0 if part is None else pl.multiple_of(part * half, half)
            few = rows if part is None else half
            return [(piece.at[pl.ds(4, 2)], got_ref.at[at, :, pl.ds(start, few)])]

        fill_weights(0, where_ref, pieces, targets, sem)
        for j in range(shards):
            for h in range(2):
                for q in range(W // rows):
                    spot = slice(q * rows, q * rows + rows)
                    part = slice(h * half, h * half + half)
                    value = got_ref[j, 0, part, spot].astype(F32)
                    value = value + got_ref[j, 1, part, spot].astype(F32)
                    first = h * (SMALL // 2) + q * half
                    table_ref[first : first + half, j * rows : j * rows + rows] = value
        inputs = jnp.where(mask_ref[...] > 0, 0.0, target_ref[...].astype(F32)).astype(BF16)
        inputs_ref[...] = inputs
        embed = table_ref[:P_SIZE].astype(BF16)
        for s in range(n // LEN):
            part = slice(s * LEN, s * LEN + LEN)
            x_ref[part] = dense(inputs[part], embed) + table_ref[2 * P_SIZE : 2 * P_SIZE + LEN]
        head_ref[...] = table_ref[P_SIZE : 2 * P_SIZE].astype(BF16)
        norm_ref[...] = table_ref[2 * P_SIZE + LEN : 2 * P_SIZE + LEN + 16]

    return pl.pallas_call(
        kernel,
        grid=(1,),
        in_specs=[SMEM, whole((n, P_SIZE)), whole((n, 1))] + [ANY] * sources,
        out_specs=[whole((n, D)), whole((n, P_SIZE)), whole((P_SIZE, D)), whole((16, D))],
        out_shape=[
            jax.ShapeDtypeStruct((n, D), F32),
            jax.ShapeDtypeStruct((n, P_SIZE), BF16),
            jax.ShapeDtypeStruct((P_SIZE, D), BF16),
            jax.ShapeDtypeStruct((16, D), F32),
        ],
        scratch_shapes=[
            pltpu.VMEM((shards, 2, rows, W), BF16),
            pltpu.VMEM((SMALL, D), F32),
            pltpu.SemaphoreType.DMA((copies_of(group),)),
        ],
        compiler_params=params(),
        cost_estimate=cost(2 * n * D * P_SIZE, n * D * 5),
        name="embed_step",
    )(where, target, maskf, *group)


def copies_of(group):
    return 2 * (2 * (len(group) - 2) + 1)


def norm_parts(x):
    center = x - jnp.mean(x, -1, keepdims=True)
    rstd = lax.rsqrt(jnp.mean(center * center, -1, keepdims=True) + EPS)
    return center * rstd, rstd


def norm_back(xhat, rstd, dy, gain):
    dxh = dy * gain
    return rstd * (
        dxh - jnp.mean(dxh, -1, keepdims=True) - xhat * jnp.mean(dxh * xhat, -1, keepdims=True)
    )


def head_lanes(x, h):
    lane = lax.broadcasted_iota(jnp.int32, (x.shape[0], 128), 1)
    own = (lane < DH) if h % 2 == 0 else (lane >= DH)
    return jnp.where(own, x[:, pair_of(h)], 0)


def pair_of(h):
    return slice(128 * (h // 2), 128 * (h // 2) + 128)


def head_of(h):
    return slice(DH * h, DH * h + DH)


SP = 2


def attn_fwd(place, where, x, norms, group):
    rows = D // place.shards
    n = x.shape[0]
    seqs = n // LEN
    sources = len(group)

    def kernel(where_ref, x_ref, norm_ref, *refs):
        pieces, refs = refs[:sources], refs[sources:]
        mid_ref, qkv_ref, pt_ref, ot_ref, w_ref, sem = refs
        fill_weights(pl.program_id(0), where_ref, pieces, attn_targets(w_ref, rows), sem)
        spans = [slice(LEN * s, LEN * s + LEN) for s in range(SP)]
        a, q, k, vt = [], [], [], []
        for s, span in enumerate(spans):
            xhat, _ = norm_parts(x_ref[span])
            a.append((xhat * norm_ref[0:1, :] + norm_ref[1:2, :]).astype(BF16))
            q.append((dense(a[s], w_ref[0]) * DH**-0.5).astype(BF16))
            k.append(dense(a[s], w_ref[1]).astype(BF16))
            qkv_ref[span, :D] = q[s]
            qkv_ref[span, D : 2 * D] = k[s]

        def scores(s, h):
            return dense_nt(k[s][:, pair_of(h)], head_lanes(q[s], h))

        def gather_values(s, h, p):
            ot_ref[s, head_of(h), :] = dense(vt[s][head_of(h), :], p).astype(BF16)

        items = [(s, h) for h in range(H) for s in range(SP)]
        ahead = scores(*items[0])
        for s, span in enumerate(spans):
            v = dense(a[s], w_ref[2]).astype(BF16)
            qkv_ref[span, 2 * D :] = v
            vt.append(v.T)
        last = None
        for at, (s, h) in enumerate(items):
            st = ahead
            if at + 1 < len(items):
                ahead = scores(*items[at + 1])
            if last is not None:
                gather_values(*last)
            e = jnp.exp(st - jnp.max(st, axis=0, keepdims=True))
            p = (e * (1.0 / jnp.sum(e, axis=0, keepdims=True))).astype(BF16)
            pt_ref[s, h] = p
            last = (s, h, p)
        gather_values(*last)
        for s, span in enumerate(spans):
            mid_ref[span] = x_ref[span] + dense_tn(ot_ref[s], w_ref[3])

    return pl.pallas_call(
        kernel,
        grid=(seqs // SP,),
        in_specs=[SMEM, pl.BlockSpec((SP * LEN, D), lambda i: (i, 0)), whole((4, D))]
        + [ANY] * sources,
        out_specs=[
            pl.BlockSpec((SP * LEN, D), lambda i: (i, 0)),
            pl.BlockSpec((SP * LEN, 3 * D), lambda i: (i, 0)),
            pl.BlockSpec((SP, H, LEN, LEN), lambda i: (i, 0, 0, 0)),
            pl.BlockSpec((SP, D, LEN), lambda i: (i, 0, 0)),
        ],
        out_shape=[
            jax.ShapeDtypeStruct((n, D), F32),
            jax.ShapeDtypeStruct((n, 3 * D), BF16),
            jax.ShapeDtypeStruct((seqs, H, LEN, LEN), BF16),
            jax.ShapeDtypeStruct((seqs, D, LEN), BF16),
        ],
        scratch_shapes=[
            pltpu.VMEM((4, D, W), BF16),
            pltpu.SemaphoreType.DMA((copies_of(group),)),
        ],
        compiler_params=params(),
        cost_estimate=cost(2 * n * D * (4 * D + 2 * LEN), n * D * 20, n * H * LEN),
        name="attn_fwd",
    )(where, x, norms, *group)


def gelu_pair(u):
    cdf = 0.5 * lax.erf(u * 0.7071067811865476) + 0.5
    density = jnp.exp(u * u * -0.5) * 0.3989422804014327
    return u * cdf, cdf + u * density


def mlp_fwd(place, where, mid, norms, group):
    rows = D // place.shards
    n = mid.shape[0]
    tall = 2 * LEN
    sources = len(group)
    per = W // rows

    def kernel(where_ref, mid_ref, norm_ref, *refs):
        pieces, refs = refs[:sources], refs[sources:]
        out_ref, act_ref, gp_ref, up_ref, down_ref, sem = refs
        fill_weights(pl.program_id(0), where_ref, pieces, mlp_targets(up_ref, down_ref, rows), sem)
        mid = mid_ref[...]
        xhat, _ = norm_parts(mid)
        c = (xhat * norm_ref[2:3, :] + norm_ref[3:4, :]).astype(BF16)
        total = mid

        def lower(act, b):
            return dense(act, down_ref[per * b : per * b + per].reshape(W, D))

        ahead = dense(c, up_ref[0])
        for b in range(FF // W):
            cols = slice(W * b, W * b + W)
            u = ahead
            if b + 1 < FF // W:
                ahead = dense(c, up_ref[b + 1])
            if b > 0:
                total = total + lower(last, b - 1)
            act, slope = gelu_pair(u)
            last = act.astype(BF16)
            act_ref[:, cols] = last
            gp_ref[:, cols] = slope.astype(BF16)
        out_ref[...] = total + lower(last, FF // W - 1)

    def row(width):
        return pl.BlockSpec((tall, width), lambda i: (i, 0))

    return pl.pallas_call(
        kernel,
        grid=(n // tall,),
        in_specs=[SMEM, row(D), whole((4, D))] + [ANY] * sources,
        out_specs=[row(D), row(FF), row(FF)],
        out_shape=[
            jax.ShapeDtypeStruct((n, D), F32),
            jax.ShapeDtypeStruct((n, FF), BF16),
            jax.ShapeDtypeStruct((n, FF), BF16),
        ],
        scratch_shapes=[
            pltpu.VMEM((4, D, W), BF16),
            pltpu.VMEM((FF // rows, rows, D), BF16),
            pltpu.SemaphoreType.DMA((copies_of(group),)),
        ],
        compiler_params=params(),
        cost_estimate=cost(4 * n * D * FF, n * D * 24, n * FF * 2),
        name="mlp_fwd",
    )(where, mid, norms, *group)


def mlp_bwd(place, where, dz, mid, gp, norms, group):
    rows = D // place.shards
    n = mid.shape[0]
    sources = len(group)
    per = W // rows

    def kernel(where_ref, dz_ref, mid_ref, gp_ref, norm_ref, *refs):
        pieces, refs = refs[:sources], refs[sources:]
        dmid_ref, dh_ref, du_ref, c_ref, dm_ref, dn_ref, up_ref, down_ref, sem = refs
        i = pl.program_id(0)
        fill_weights(i, where_ref, pieces, mlp_targets(up_ref, down_ref, rows), sem)
        dm = dz_ref[...].astype(BF16)
        dm_ref[...] = dm

        def upper(b):
            return dense_nt(dm, down_ref[per * b : per * b + per].reshape(W, D))

        dc = jnp.zeros((LEN, D), F32)
        ahead = upper(0)
        for b in range(FF // W):
            cols = slice(W * b, W * b + W)
            da = ahead
            if b + 1 < FF // W:
                ahead = upper(b + 1)
            if b > 0:
                dc = dc + dense_nt(last, up_ref[b - 1])
            last = (gp_ref[:, cols].astype(F32) * da).astype(BF16)
            du_ref[:, cols] = last
        dc = dc + dense_nt(last, up_ref[FF // W - 1])
        xhat, rstd = norm_parts(mid_ref[...])
        gain = norm_ref[2:3, :]
        c_ref[...] = (xhat * gain + norm_ref[3:4, :]).astype(BF16)
        dmid = dz_ref[...] + norm_back(xhat, rstd, dc, gain)
        dmid_ref[...] = dmid
        dh_ref[...] = dmid.astype(BF16)

        @pl.when(i == 0)
        def _():
            dn_ref[...] = jnp.zeros_like(dn_ref)

        dn_ref[0:1, :] += jnp.sum(dc * xhat, 0, keepdims=True)
        dn_ref[1:2, :] += jnp.sum(dc, 0, keepdims=True)

    def row(width):
        return pl.BlockSpec((LEN, width), lambda i: (i, 0))

    return pl.pallas_call(
        kernel,
        grid=(n // LEN,),
        in_specs=[SMEM, row(D), row(D), row(FF), whole((4, D))] + [ANY] * sources,
        out_specs=[row(D), row(D), row(FF), row(D), row(D), whole((8, D))],
        out_shape=[
            jax.ShapeDtypeStruct((n, D), F32),
            jax.ShapeDtypeStruct((n, D), BF16),
            jax.ShapeDtypeStruct((n, FF), BF16),
            jax.ShapeDtypeStruct((n, D), BF16),
            jax.ShapeDtypeStruct((n, D), BF16),
            jax.ShapeDtypeStruct((8, D), F32),
        ],
        scratch_shapes=[
            pltpu.VMEM((4, D, W), BF16),
            pltpu.VMEM((FF // rows, rows, D), BF16),
            pltpu.SemaphoreType.DMA((copies_of(group),)),
        ],
        compiler_params=params(),
        cost_estimate=cost(4 * n * D * FF, n * D * 32),
        name="mlp_bwd",
    )(where, dz, mid, gp, norms, *group)


def attn_bwd(place, where, dmid, dh, x, qkv, pt, ot, norms, group):
    rows = D // place.shards
    n = x.shape[0]
    seqs = n // LEN
    sources = len(group)

    def kernel(where_ref, dmid_ref, dh_ref, x_ref, qkv_ref, pt_ref, ot_ref, norm_ref, *refs):
        pieces, refs = refs[:sources], refs[sources:]
        dx_ref, dqkv_ref, a_ref, dn_ref, w_ref, dqt_ref, sem = refs
        i = pl.program_id(0)
        fill_weights(i, where_ref, pieces, attn_targets(w_ref, rows), sem)
        spans = [slice(LEN * s, LEN * s + LEN) for s in range(SP)]
        do, delta, kt = [], [], []
        for s, span in enumerate(spans):
            do.append(dense_nt(dh_ref[span], w_ref[3]).astype(BF16))
            along = do[s].T.astype(F32) * ot_ref[s].astype(F32)
            delta.append([jnp.sum(along[head_of(h), :], axis=0, keepdims=True) for h in range(H)])
            kt.append(qkv_ref[span, D : 2 * D].T)

        def first(s, h):
            doh = head_lanes(do[s], h)
            v = qkv_ref[spans[s], 2 * D + 128 * (h // 2) : 2 * D + 128 * (h // 2) + 128]
            return dense_nt(v, doh), dense(pt_ref[s, h], doh)

        halves = {}

        def second(s, h, dst, dv):
            q = qkv_ref[spans[s], pair_of(h)]
            lane = lax.broadcasted_iota(jnp.int32, (LEN, 128), 1)
            own = (lane < DH) if h % 2 == 0 else (lane >= DH)
            dk = dense(dst, jnp.where(own, q, 0))
            dqt_ref[s, head_of(h), :] = (dense(kt[s][head_of(h), :], dst) * DH**-0.5).astype(BF16)
            if h % 2 == 0:
                halves[s] = (dk, dv)
                return
            at = 128 * (h // 2)
            dk, dv = dk + halves[s][0], dv + halves[s][1]
            dqkv_ref[spans[s], D + at : D + at + 128] = dk.astype(BF16)
            dqkv_ref[spans[s], 2 * D + at : 2 * D + at + 128] = dv.astype(BF16)

        items = [(s, h) for h in range(H) for s in range(SP)]
        ahead = first(*items[0])
        last = None
        for at, (s, h) in enumerate(items):
            dpt, dv = ahead
            if at + 1 < len(items):
                ahead = first(*items[at + 1])
            if last is not None:
                second(*last)
            dst = (pt_ref[s, h].astype(F32) * (dpt - delta[s][h])).astype(BF16)
            last = (s, h, dst, dv)
        second(*last)

        @pl.when(i == 0)
        def _():
            dn_ref[...] = jnp.zeros_like(dn_ref)

        gain = norm_ref[0:1, :]
        for s, span in enumerate(spans):
            da = dense_nt(dqkv_ref[span, D : 2 * D], w_ref[1])
            da = da + dense_nt(dqkv_ref[span, 2 * D :], w_ref[2])
            dq = dqt_ref[s].T
            dqkv_ref[span, :D] = dq
            da = da + dense_nt(dq, w_ref[0])
            xhat, rstd = norm_parts(x_ref[span])
            a_ref[span] = (xhat * gain + norm_ref[1:2, :]).astype(BF16)
            dx_ref[span] = dmid_ref[span] + norm_back(xhat, rstd, da, gain)
            dn_ref[0:1, :] += jnp.sum(da * xhat, 0, keepdims=True)
            dn_ref[1:2, :] += jnp.sum(da, 0, keepdims=True)

    def row(width):
        return pl.BlockSpec((SP * LEN, width), lambda i: (i, 0))

    return pl.pallas_call(
        kernel,
        grid=(seqs // SP,),
        in_specs=[
            SMEM,
            row(D),
            row(D),
            row(D),
            row(3 * D),
            pl.BlockSpec((SP, H, LEN, LEN), lambda i: (i, 0, 0, 0)),
            pl.BlockSpec((SP, D, LEN), lambda i: (i, 0, 0)),
            whole((4, D)),
        ]
        + [ANY] * sources,
        out_specs=[row(D), row(3 * D), row(D), whole((8, D))],
        out_shape=[
            jax.ShapeDtypeStruct((n, D), F32),
            jax.ShapeDtypeStruct((n, 3 * D), BF16),
            jax.ShapeDtypeStruct((n, D), BF16),
            jax.ShapeDtypeStruct((8, D), F32),
        ],
        scratch_shapes=[
            pltpu.VMEM((4, D, W), BF16),
            pltpu.VMEM((SP, D, LEN), BF16),
            pltpu.SemaphoreType.DMA((copies_of(group),)),
        ],
        compiler_params=params(),
        cost_estimate=cost(2 * n * D * (4 * D + 5 * LEN), n * D * 32),
        name="attn_bwd",
    )(where, dmid, dh, x, qkv, pt, ot, norms, *group)


def head_step(place, x, target, maskf, head, norms, count):
    n = x.shape[0]

    def kernel(x_ref, target_ref, mask_ref, head_ref, norm_ref, dx_ref, loss_ref, gh_ref, dn_ref):
        i = pl.program_id(0)
        xhat, rstd = norm_parts(x_ref[...])
        gain = norm_ref[0:1, :]
        y = (xhat * gain + norm_ref[1:2, :]).astype(BF16)
        masked = mask_ref[...]
        err = (dense_nt(y, head_ref[...]) - target_ref[...].astype(F32)) * masked
        dpred = (err * (2.0 / (P_SIZE * count))).astype(BF16)
        dy = dense(dpred, head_ref[...])
        dx_ref[...] = norm_back(xhat, rstd, dy, gain)

        @pl.when(i == 0)
        def _():
            loss_ref[...] = jnp.zeros_like(loss_ref)
            gh_ref[...] = jnp.zeros_like(gh_ref)
            dn_ref[...] = jnp.zeros_like(dn_ref)

        loss_ref[...] += jnp.sum(err * err, 0, keepdims=True)
        gh_ref[...] += dense_tn(dpred, y)
        dn_ref[0:1, :] += jnp.sum(dy * xhat, 0, keepdims=True)
        dn_ref[1:2, :] += jnp.sum(dy, 0, keepdims=True)

    def row(width):
        return pl.BlockSpec((LEN, width), lambda i: (i, 0))

    return pl.pallas_call(
        kernel,
        grid=(n // LEN,),
        in_specs=[row(D), row(P_SIZE), row(1), whole((P_SIZE, D)), whole((2, D))],
        out_specs=[row(D), whole((1, P_SIZE)), whole((P_SIZE, D)), whole((8, D))],
        out_shape=[
            jax.ShapeDtypeStruct((n, D), F32),
            jax.ShapeDtypeStruct((1, P_SIZE), F32),
            jax.ShapeDtypeStruct((P_SIZE, D), F32),
            jax.ShapeDtypeStruct((8, D), F32),
        ],
        compiler_params=params(),
        cost_estimate=cost(6 * n * D * P_SIZE, n * D * 8),
        name="head_step",
    )(x, target, maskf, head, norms)


def put_block(core, block, lead, send_ref, keep_ref, at):
    rows = block.shape[0]
    for c in range(2):

        @pl.when(core == c)
        def _(c=c):
            halves = block.reshape(lead + (2, rows // (2 * lead_size(lead)), W))
            keep_ref[at] = halves[..., c, :, :]
            send_ref[at] = halves[..., 1 - c, :, :]


def lead_size(lead):
    size = 1
    for n in lead:
        size *= n
    return size


def grad_mlp(place, where, c, du, act, dm, ot, dh):
    shards = place.shards
    rows = D // shards
    n = c.shape[0]
    seqs = n // LEN
    steps = FF // W
    per = max(shards // steps, 1)
    blocks = 9

    def kernel(where_ref, c_ref, du_ref, act_ref, dm_ref, ot_ref, dh_ref, send_ref, keep_ref, ct_ref):
        i = pl.program_id(0)
        core = where_ref[1]

        @pl.when(i == 0)
        def _():
            ct_ref[...] = c_ref[...].T

        @pl.when(i < steps)
        def _():
            block = dense(ct_ref[...], du_ref[...]).astype(BF16)
            put_block(core, block, (shards,), send_ref, keep_ref, (slice(None), i))

        @pl.when((i >= steps) & (i < 2 * steps))
        def _():
            block = dense_tn(act_ref[...], dm_ref[...]).astype(BF16)
            at = (pl.ds((i - steps) * per, per), slice(4, 8))
            put_block(core, block, (per, 4), send_ref, keep_ref, at)

        @pl.when(i == 2 * steps)
        def _():
            total = dense(ot_ref[0], dh_ref[:LEN, :])
            for s in range(1, seqs):
                total = total + dense(ot_ref[s], dh_ref[LEN * s : LEN * s + LEN, :])
            put_block(core, total.astype(BF16), (shards,), send_ref, keep_ref, (slice(None), 8))

    shape = (shards, blocks, rows // 2, W)
    return pl.pallas_call(
        kernel,
        grid=(2 * steps + 1,),
        in_specs=[
            SMEM,
            whole((n, D)),
            pl.BlockSpec((n, W), lambda i: (0, jnp.minimum(i, steps - 1))),
            pl.BlockSpec((n, W), lambda i: (0, jnp.clip(i - steps, 0, steps - 1))),
            whole((n, D)),
            whole((seqs, D, LEN)),
            whole((n, D)),
        ],
        out_specs=[whole(shape), whole(shape)],
        scratch_shapes=[pltpu.VMEM((D, n), BF16)],
        out_shape=[jax.ShapeDtypeStruct(shape, BF16)] * 2,
        compiler_params=params(),
        cost_estimate=cost(4 * n * D * FF, n * (4 * D + 4 * FF) + 4 * D * FF),
        name="grad_mlp",
    )(where, c, du, act, dm, ot, dh)


def grad_qkv(place, where, a, dqkv, small=()):
    shards = place.shards
    rows = D // shards
    half = rows // 2
    n = a.shape[0]
    blocks = 3 + bool(small)
    extra = len(small)

    def kernel(where_ref, a_ref, dqkv_ref, *refs):
        small_refs, refs = refs[:extra], refs[extra:]
        send_ref, keep_ref, at_ref = refs[:3]
        i = pl.program_id(0)

        @pl.when(i == 0)
        def _():
            at_ref[...] = a_ref[...].T

        @pl.when(i < 3)
        def _():
            block = dense(at_ref[...], dqkv_ref[...]).astype(BF16)
            put_block(where_ref[1], block, (shards,), send_ref, keep_ref, (slice(None), i))

        if extra:
            table_ref = refs[3]
            inputs_ref, dx_ref, head_ref = small_refs[:3]

            @pl.when(i == 3)
            def _():
                dx = dx_ref[...]
                table_ref[:P_SIZE] = dense_tn(inputs_ref[...], dx.astype(BF16)).astype(BF16)
                table_ref[P_SIZE : 2 * P_SIZE] = head_ref[...].astype(BF16)
                total = dx[:LEN]
                for s in range(1, n // LEN):
                    total = total + dx[s * LEN : s * LEN + LEN]
                table_ref[2 * P_SIZE : 2 * P_SIZE + LEN] = total.astype(BF16)
                norms = jnp.concatenate(
                    [ref[0:2, :] for ref in small_refs[3:]]
                    + [jnp.zeros((16 - 2 * (extra - 3), D), F32)],
                    0,
                )
                start = 2 * P_SIZE + LEN
                table_ref[start : start + 16] = norms.astype(BF16)
                table_ref[start + 16 :] = jnp.zeros((SMALL - start - 16, D), BF16)
                for core in range(2):

                    @pl.when(where_ref[1] == core)
                    def _(core=core):
                        for h in range(2):
                            out_ref = keep_ref if h == core else send_ref
                            for j in range(shards):
                                for q in range(W // rows):
                                    first = h * (SMALL // 2) + q * half
                                    value = table_ref[first : first + half, j * rows : j * rows + rows]
                                    out_ref[j, 3, :, q * rows : q * rows + rows] = value

    shape = (shards, blocks, half, W)
    return pl.pallas_call(
        kernel,
        grid=(blocks,),
        in_specs=[SMEM, whole((n, D)), pl.BlockSpec((n, W), lambda i: (0, jnp.minimum(i, 2)))]
        + [whole(x.shape) for x in small],
        out_specs=[whole(shape), whole(shape)],
        scratch_shapes=[pltpu.VMEM((D, n), BF16)] + [pltpu.VMEM((SMALL, D), BF16)] * bool(small),
        out_shape=[jax.ShapeDtypeStruct(shape, BF16)] * 2,
        compiler_params=params(),
        cost_estimate=cost(6 * n * D * D, n * 8 * D + 6 * D * D),
        name="grad_qkv",
    )(where, a, dqkv, *small)


def adam(weight, first, second, grad, rate):
    first = BETA_ONE * first + (1 - BETA_ONE) * grad
    second = BETA_TWO * second + (1 - BETA_TWO) * grad * grad
    fixed_one = first / (1 - BETA_ONE**STEP_COUNT)
    fixed_two = second / (1 - BETA_TWO**STEP_COUNT)
    weight = weight - rate * (fixed_one / (jnp.sqrt(fixed_two) + ADAM_EPS) + DECAY * weight)
    return (weight, first, second)


def adam_step(place, where, factor, state, small, grads, chip):
    rows = D // place.shards
    half = rows // 2
    few = half // 2
    flat = [x for group in state for x in group]
    flat = [x.reshape(L, 4, rows, W) if x.shape[1] != rows else x for x in flat]
    tiny = [x for group in small for x in group]

    def spec(x):
        if x.ndim == 4:
            return pl.BlockSpec((None, 4, few, W), lambda i, h, q: (i, 0, 2 * h + q, 0))
        return pl.BlockSpec((None, few, x.shape[2]), lambda i, h, q: (i, 2 * h + q, 0))

    gflat, spots = [], []
    for layer in grads:
        spots.append([])
        for pieces, first in layer:
            known = [n for n, x in enumerate(gflat) if x is pieces[0]]
            spots[-1].append((known[0] if known else len(gflat), len(pieces), first))
            gflat += [] if known else list(pieces)
    total = len(flat) + len(tiny)

    def kernel(where_ref, factor_ref, *refs):
        grad_refs, refs = refs[: len(gflat)], refs[len(gflat) :]
        ins, outs, table_ref = refs[:total], refs[total : 2 * total], refs[-1]
        layer, h, q = pl.program_id(0), pl.program_id(1), pl.program_id(2)
        scale = factor_ref[0]
        own = where_ref[1] == h
        near = where_ref[chip] == q

        def update(n, at, grad, rate):
            got = adam(ins[3 * n][at], ins[3 * n + 1][at], ins[3 * n + 2][at], grad, rate)
            for k in range(3):
                outs[3 * n + k][at] = got[k]

        part = pl.ds(pl.multiple_of(q * few, few), few)

        def run(layer):
            def grad(group, b):
                base, count, first = spots[layer][group]
                refs = grad_refs[base : base + count]
                if count == 2:
                    got = jnp.where(own, refs[0][first + b, part], refs[1][first + b, part])
                else:
                    close = jnp.where(own, refs[0][first + b], refs[1][first + b])
                    away = jnp.where(own, refs[2][first + b], refs[3][first + b])
                    got = jnp.where(near, close, away)
                return got.astype(F32) * scale

            for b in range(3):
                update(0, (slice(None), slice(W * b, W * b + W)), grad(0, b), RATE)
            update(1, (slice(None), slice(None)), grad(1, 8), RATE)
            for b in range(4):
                update(2, (slice(None), slice(W * b, W * b + W)), grad(1, b), RATE)
                update(3, (b,), grad(1, 4 + b), RATE)

        for i in range(L):

            @pl.when(layer == i)
            def _(i=i):
                run(i)

        @pl.when((layer == 0) & (h == 0) & (q == 0))
        def _():
            base, _, at = spots[0][0]
            mine, other = grad_refs[base][at + 3], grad_refs[base + 1][at + 3]
            first = where_ref[1] == 0
            for n, block in enumerate((jnp.where(first, mine, other), jnp.where(first, other, mine))):
                for k in range(W // rows):
                    start = n * (SMALL // 2) + k * half
                    table_ref[start : start + half] = (
                        block[:, k * rows : k * rows + rows].astype(F32) * scale
                    )
            count = 2 * P_SIZE + LEN
            update(4, (slice(None), slice(None)), table_ref[:count], TABLE_RATE)
            norms = small[1][0].shape[0]
            update(5, (slice(None), slice(None)), table_ref[count : count + norms], TABLE_RATE)

    out = pl.pallas_call(
        kernel,
        grid=(L, 2, 2),
        in_specs=[SMEM, SMEM]
        + [whole(g.shape) for g in gflat]
        + [spec(x) for x in flat]
        + [whole(x.shape) for x in tiny],
        out_specs=[spec(x) for x in flat] + [whole(x.shape) for x in tiny],
        out_shape=[jax.ShapeDtypeStruct(x.shape, F32) for x in flat + tiny],
        scratch_shapes=[pltpu.VMEM((SMALL, rows), F32)],
        compiler_params=params(),
        cost_estimate=cost(20 * L * 12 * rows * W, 24 * L * 12 * rows * W),
        name="adam_step",
    )(where, factor, *gflat, *flat, *tiny)
    return [
        tuple(y.reshape(x.shape) for x, y in zip(group, out[3 * n : 3 * n + 3]))
        for n, group in enumerate(list(state) + list(small))
    ]


def on_device(
    series,
    mask,
    qkv_w,
    out_w,
    up_w,
    down_w,
    patch_maps,
    norm_params,
    qkv_m,
    out_m,
    up_m,
    down_m,
    patch_m,
    norm_m,
    qkv_v,
    out_v,
    up_v,
    down_v,
    patch_v,
    norm_v,
):
    place = Place()
    shards = place.shards
    rows = D // shards
    half = rows // 2
    seqs = series.shape[0]
    count = MASKED * seqs * shards * place.replicas
    shard_bits = [(place.shard >> bit) & 1 for bit in bits_of(shards)]
    where = jnp.stack([place.shard, place.core] + shard_bits + [place.chip & 1]).astype(jnp.int32)
    chip = 2 + len(shard_bits)

    small_now = [patch_maps, norm_params]
    packs = [
        (
            pack(place, where, i, [qkv_w, out_w], [], small_now if i == 0 else []),
            pack(place, where, i, [up_w], [down_w], []),
        )
        for i in range(L)
    ]

    def group_of(packed, ours, theirs):
        return [packed[0]] + ours + [theirs]

    attn_groups = [None] * L
    mlp_groups = [None] * L
    target = series.reshape(seqs * LEN, P_SIZE)
    maskf = mask.reshape(seqs * LEN, 1).astype(F32)
    ours = gather_shards(place, packs[0][0][1])
    theirs = gather_cores(place, ours, *[p[1] for pair in packs for p in pair], target, maskf)
    attn_groups[0] = group_of(packs[0][0], ours, theirs)
    mine = gate(packs[0][1][1], *ours)
    ours_mlp = gather_shards(place, mine)

    x, inputs, head, norms_all = embed_step(place, where, target, gate(maskf, mine), attn_groups[0])
    saved = []
    for index in range(L):
        norms = norms_all[4 * index : 4 * index + 4]
        mid, qkv, pt, ot = attn_fwd(place, where, x, norms, attn_groups[index])
        held = mid
        if index + 1 < L:
            got = gates(ours_mlp, mid)
            mine = gate(packs[index + 1][0][1], *got)
            ours_attn = gather_shards(place, mine)
            held = gate(mid, mine)
        theirs = gather_cores(place, ours_mlp, mid)
        mlp_groups[index] = group_of(packs[index][1], ours_mlp, theirs)
        y, act, gp = mlp_fwd(place, where, held, norms, mlp_groups[index])
        if index + 1 < L:
            got = gates(ours_attn, y)
            theirs = gather_cores(place, got)
            attn_groups[index + 1] = group_of(packs[index + 1][0], ours_attn, theirs)
            mine = gate(packs[index + 1][1][1], *got)
            ours_mlp = gather_shards(place, mine)
            y = gate(y, mine)
        saved.append((x, mid, qkv, pt, ot, act, gp, norms))
        x = y

    grad, loss, g_head, dn_final = head_step(
        place, x, target, maskf, head, norms_all[4 * L : 4 * L + 2], count
    )
    loss = (jnp.sum(loss) / P_SIZE).reshape(1, 1)

    norm_grads = {}

    def backward_mlp(index, grad):
        x, mid, qkv, pt, ot, act, gp, norms = saved[index]
        dmid, dh, du, c, dm, dn = mlp_bwd(
            place, where, grad, mid, gp, norms, mlp_groups[index]
        )
        norm_grads[index, 1] = dn
        return dmid, dh, du, c, dm

    def backward_attn(index, dmid, dh):
        x, mid, qkv, pt, ot, act, gp, norms = saved[index]
        grad, dqkv, a, dn = attn_bwd(
            place, where, dmid, dh, x, qkv, pt, ot, norms, attn_groups[index]
        )
        norm_grads[index, 0] = dn
        return grad, dqkv, a

    def grads_mlp(index, du, c, dm, dh):
        return grad_mlp(place, where, c, du, saved[index][5], dm, saved[index][4], dh)

    loss = loss + place.to_core(loss)
    dmid, dh, du, c, dm = backward_mlp(1, grad)
    flow_one = Flow(place, where, "sum_one", False)
    token = flow_one.begin(*grads_mlp(1, du, c, dm, dh), (0, 4, 0), (4, 5, 1))
    grad, dqkv_one, a_one = backward_attn(1, gate(dmid, token), dh)
    token = flow_one.advance(grad)
    dmid, dh, du, c, dm = backward_mlp(0, gate(grad, token))
    token = flow_one.advance(dmid)
    flow_two = Flow(place, where, "sum_two", True)
    token = flow_two.begin(*grads_mlp(0, du, gate(c, token), dm, dh), (0, 4, 0), (4, 5, 1))
    token = flow_one.advance(token)
    flow_last = Flow(place, where, "sum_last", False)
    send, keep = grad_qkv(place, where, gate(a_one, token), dqkv_one)
    token = flow_last.begin(send, keep, (0, 3, 0))
    token = flow_two.advance(token)
    grad, dqkv, a = backward_attn(0, gate(dmid, token), dh)
    token = flow_two.advance(grad)
    small = [inputs, grad, g_head]
    small += [norm_grads[i, k] for i in range(L) for k in range(2)] + [dn_final]
    send, keep = grad_qkv(place, where, gate(a, token), dqkv, small)
    token = flow_last.begin(send, keep, (0, 4, 1))
    for bit in bits_of(place.chips):
        loss = loss + place.to_chip(gate(loss, token), 1 << bit)
    token = flow_one.advance(token)
    done_one = None
    while not flow_last.last():
        token = flow_last.advance(token)
        if not flow_two.last():
            token = flow_two.advance(token)
        elif flow_one.last() and done_one is None:
            done_one = flow_one.finish(token)
            token = flow_one.token
        if not flow_one.last():
            token = flow_one.advance(token)
    if done_one is None:
        done_one = flow_one.finish(token)
        token = flow_one.token
    done_two = flow_two.finish(token)
    done_last = flow_last.finish(flow_two.token)
    grads = [
        [(done_last, 3), (done_two, 0)],
        [(done_last, 0), (done_one, 0)],
    ]

    both = jnp.concatenate([loss, square_sum(done_one + done_two + done_last)], 1)
    both = sum([place.to_shard(both, k) for k in range(1, shards)], both)
    loss = both[0, 0] / count
    grad_norm = jnp.sqrt(both[0, 1])
    factor = CLIP / jnp.maximum(grad_norm, CLIP)

    state = [
        (qkv_w, qkv_m, qkv_v),
        (out_w, out_m, out_v),
        (up_w, up_m, up_v),
        (down_w, down_m, down_v),
    ]
    small = [(patch_maps, patch_m, patch_v), (norm_params, norm_m, norm_v)]
    results = adam_step(place, where, factor.reshape(1), state, small, grads, chip)
    news = tuple(r[0] for r in results)
    new_m = tuple(r[1] for r in results)
    new_v = tuple(r[2] for r in results)
    return (loss, grad_norm) + news + new_m + new_v


def solution(mesh):
    batch = P(("shard", "replica"), None)
    stack = P(None, "shard", None)
    flat = P(None, "shard")
    state = (stack, stack, stack, stack, flat, flat)
    return jax.shard_map(
        on_device,
        mesh=mesh,
        in_specs=(batch, batch) + state * 3,
        out_specs=(P(), P()) + state * 3,
        check_vma=False,
    )
```

```python
import jax
import jax.numpy as jnp
from jax import lax
from jax.experimental import pallas as pl
from jax.experimental.pallas import tpu as pltpu
from jax.sharding import PartitionSpec as P

D = 512
H = 8
DH = 64
FF = 2048
P_SIZE = 64
LEN = 256
L = 2
MASKED = 102

EPS = 1e-05
CLIP = 0.001
RATE = 0.05
TABLE_RATE = 0.3
BETA_ONE = 0.9
BETA_TWO = 0.999
ADAM_EPS = 1e-08
DECAY = 0.1
STEP_COUNT = 10

W = 512
SMALL = 512
NORMS_LOW = 2 * P_SIZE + LEN + 16
F32 = jnp.float32
BF16 = jnp.bfloat16


def dense(left, right):
    return jnp.dot(left, right, preferred_element_type=F32)


def dense_tn(left, right):
    return lax.dot_general(left, right, (((0,), (0,)), ((), ())), preferred_element_type=F32)


def dense_nt(left, right):
    return lax.dot_general(left, right, (((1,), (1,)), ((), ())), preferred_element_type=F32)


def layer_norm(x, gain, bias):
    center = x - jnp.mean(x, -1, keepdims=True)
    spread = jnp.mean(center * center, -1, keepdims=True)
    return center * lax.rsqrt(spread + EPS) * gain + bias


def params(**more):
    return pltpu.CompilerParams(vmem_limit_bytes=30 * 2**20, **more)


def cost(flops, data, trans=0):
    return pl.CostEstimate(flops=int(flops), bytes_accessed=int(data), transcendentals=int(trans))


def whole(shape):
    return pl.BlockSpec(shape, lambda *_: (0,) * len(shape))


def in_hbm(x):
    return pltpu.with_memory_space_constraint(x, pltpu.HBM)


ANY = pl.BlockSpec(memory_space=pl.ANY)
SMEM = pl.BlockSpec(memory_space=pltpu.SMEM)


def permute(x, axis, mask, size):
    return lax.ppermute(x, axis, [(i, i ^ mask) for i in range(size)])


def pick(x, index):
    return lax.dynamic_index_in_dim(x, index, 0, keepdims=False)


class Place:
    def __init__(self):
        self.shards = lax.axis_size("shard")
        self.replicas = lax.axis_size("replica")
        self.chips = self.replicas // 2
        self.shard = lax.axis_index("shard")
        replica = lax.axis_index("replica")
        self.core = replica % 2
        self.chip = replica // 2

    def to_core(self, x):
        return permute(x, "replica", 1, self.replicas)

    def to_shard(self, x, mask):
        return permute(x, "shard", mask, self.shards)

    def to_chip(self, x, mask):
        return permute(x, "replica", 2 * mask, self.replicas)


def gate(x, *after):
    return lax.optimization_barrier((x,) + after)[0]


def gather_shards(place, mine):
    return [place.to_shard(mine, mask) for mask in range(1, place.shards)]


def gather_cores(place, ours, *after):
    return place.to_core(jnp.stack(gates(ours, *after)))


def gates(items, *after):
    return list(lax.optimization_barrier(tuple(items) + after)[: len(items)])


def bits_of(size):
    return list(range(size.bit_length() - 1))


def total_of(values):
    total = values[0].astype(F32)
    for value in values[1:]:
        total = total + value.astype(F32)
    return total


def combine(where, jobs, name):
    lanes = W // 2
    arrays, leads, plans, shapes = [], [], [], []

    def number(array, lead):
        for n, known in enumerate(arrays):
            if known is array:
                return n
        arrays.append(array)
        leads.append(lead)
        return len(arrays) - 1

    for segments, lead, cut, bit in jobs:
        plans.append([[(number(a, lead), f, b) for a, f, b in parts] for parts in segments])
        blocks = sum(parts[0][2] for parts in segments)
        rows = segments[0][0][0].shape[-2]
        if cut is None:
            shapes.append(lead + (blocks, rows, W))
        elif cut == "rows":
            shapes += [lead + (blocks, rows // 2, W)] * 2
        else:
            shapes += [lead[:cut] + lead[cut + 1 :] + (blocks, rows, W)] * 2
    arrays = [a.reshape(lead + a.shape[-3:]) for a, lead in zip(arrays, leads)]

    def block(shape):
        zeros = (0,) * (len(shape) - 1)
        return pl.BlockSpec(shape[:-1] + (lanes,), lambda i: zeros + (i,))

    def kernel(where_ref, *refs):
        ins, outs = refs[: len(arrays)], list(refs[len(arrays) :])
        for (segments, lead, cut, bit), plan in zip(jobs, plans):
            some = (slice(None),) * len(lead)
            fewer = (slice(None),) * (len(lead) - (cut is not None and cut != "rows"))
            if cut is None:
                targets = [(outs.pop(0), None)]
            else:
                value = where_ref[bit]
                targets = [(outs.pop(0), 1 - value), (outs.pop(0), value)]
            for out_ref, at in targets:
                start = 0
                for parts in plan:
                    got = []
                    for n, f, b in parts:
                        index = some
                        if cut is not None and cut != "rows":
                            index = some[:cut] + (at,) + some[cut + 1 :]
                        index += (slice(f, f + b),)
                        if cut == "rows":
                            few = ins[n].shape[-2] // 2
                            index += (pl.ds(pl.multiple_of(at * few, few), few),)
                        got.append(ins[n][index])
                    out_ref[fewer + (slice(start, start + parts[0][2]),)] = total_of(got).astype(BF16)
                    start += parts[0][2]

    size = sum(a.size for a in arrays) * 4
    return pl.pallas_call(
        kernel,
        grid=(2,),
        in_specs=[SMEM] + [block(a.shape) for a in arrays],
        out_specs=[block(s) for s in shapes],
        out_shape=[jax.ShapeDtypeStruct(s, BF16) for s in shapes],
        compiler_params=params(),
        cost_estimate=cost(size, size),
        name=name,
    )(where, *arrays)


class Flow:
    def __init__(self, place, spread):
        self.place, self.spread = place, spread
        self.bits = bits_of(place.shards)
        self.steps = len(self.bits) + len(bits_of(place.chips))
        self.step = 0
        self.inputs = []
        self.ranges = []

    def begin(self, send, keep, *ranges):
        other = self.place.to_core(send)
        for first, blocks, order in ranges:
            self.ranges.append((len(self.inputs), first, blocks, order))
        self.inputs += [keep, other]
        self.left = [list(reversed(self.bits)) for _ in self.ranges]
        return send

    def last(self):
        return self.step == self.steps

    def plan(self, flat):
        if self.step == 0:
            parts = [[(flat[n], f, b), (flat[n + 1], f, b)] for n, f, b, _ in self.ranges]
        else:
            parts = [
                [(x, 0, x.shape[-3]) for x in flat[2 * n : 2 * n + 2]]
                for n in range(len(flat) // 2)
            ]
        if self.step >= len(self.bits):
            cut = self.spread and self.step == len(self.bits)
            return [(parts, (), "rows", 2 + len(self.bits)) if cut else (parts, (), None, 0)]
        jobs, self.chosen = [], []
        for n, (_, _, _, order) in enumerate(self.ranges):
            bit = (self.bits if order == 0 else self.bits[::-1])[self.step]
            jobs.append(([parts[n]], (2,) * len(self.left[n]), self.left[n].index(bit), 2 + bit))
            self.left[n].remove(bit)
            self.chosen.append(bit)
        return jobs

    def take(self, out):
        if self.step < len(self.bits):
            self.sends, self.stays = out[0::2], out[1::2]
        else:
            self.sends, self.stays = out[:1], out[-1:]
        return self.sends[0]

    def launch(self):
        place = self.place
        if self.step < len(self.bits):
            got = [place.to_shard(x, 1 << bit) for x, bit in zip(self.sends, self.chosen)]
        else:
            got = [place.to_chip(x, 1 << (self.step - len(self.bits))) for x in self.sends]
        self.inputs = [x for pair in zip(self.stays, got) for x in pair]
        self.step += 1

    def to_neighbours(self):
        self.pieces = [self.sends[0], self.place.to_core(self.sends[0])]
        if self.spread:
            self.pieces.append(self.place.to_chip(self.sends[0], 1))

    def to_last(self):
        if self.spread:
            self.pieces.append(self.place.to_core(self.pieces[2]))


def sum_round(where, flows, *after):
    flat = gates([x for flow in flows for x in flow.inputs], *after)
    jobs, counts = [], []
    for flow in flows:
        few = len(flow.inputs)
        some = flow.plan(flat[:few])
        flat = flat[few:]
        jobs += some
        counts.append(sum(1 if cut is None else 2 for _, _, cut, _ in some))
    out = combine(where, jobs, "sum_round")
    for flow, count in zip(flows, counts):
        token = flow.take(out[:count])
        out = out[count:]
    return token


def square_sum(pieces):
    def kernel(*refs):
        total = jnp.zeros((1, W), F32)
        for ref in refs[:-1]:
            for b in range(ref.shape[0]):
                x = ref[b].astype(F32)
                total = total + jnp.sum(x * x, 0, keepdims=True)
        refs[-1][...] = jnp.sum(total, 1, keepdims=True)

    return pl.pallas_call(
        kernel,
        grid=(1,),
        in_specs=[whole(p.shape) for p in pieces],
        out_specs=whole((1, 1)),
        out_shape=jax.ShapeDtypeStruct((1, 1), F32),
        compiler_params=params(),
        name="square_sum",
    )(*pieces)


def fill_weights(step, where_ref, sources, targets, sem):
    shard, core = where_ref[0], where_ref[1]
    count = len(sources) - 2

    @pl.when(step == 0)
    def _():
        made = targets(sources[0], shard, None)
        for k in range(count):
            made += targets(sources[1 + k], shard ^ (k + 1), core)
            made += targets(sources[-1].at[k], shard ^ (k + 1), 1 - core)
        todo = [pltpu.make_async_copy(s, t, sem.at[n]) for n, (s, t) in enumerate(made)]
        for copy in todo:
            copy.start()
        for copy in todo:
            copy.wait()


def attn_targets(w_ref, rows):
    def targets(piece, at, half):
        if half is None:
            return [(piece.at[pl.ds(0, 4)], w_ref.at[:, pl.ds(pl.multiple_of(at * rows, rows), rows)])]
        start = pl.multiple_of(at * rows + half * (rows // 2), rows // 2)
        return [(piece.at[pl.ds(0, 4)], w_ref.at[:, pl.ds(start, rows // 2)])]

    return targets


def mlp_targets(up_ref, down_ref, rows):
    def targets(piece, at, half):
        few = rows if half is None else rows // 2
        skip = 0 if half is None else half * few
        start = pl.multiple_of(at * rows + skip, few)
        skip = pl.multiple_of(skip, few) if half is not None else 0
        return [
            (piece.at[pl.ds(0, 4)], up_ref.at[:, pl.ds(start, few)]),
            (piece.at[pl.ds(4, 4)], down_ref.at[pl.ds(at * 4, 4), pl.ds(skip, few)]),
        ]

    return targets


def pack(place, where, index, tall, wide, small):
    rows = D // place.shards
    half = rows // 2
    wide = [x.reshape(L, 4, rows, W) for x in wide]
    total = sum(x.shape[2] // W for x in tall) + 4 * len(wide) + bool(small)
    count = len(tall) + len(wide)

    def kernel(where_ref, *refs):
        full_ref, mine_ref = refs[count + len(small) : count + len(small) + 2]

        def run(core):
            own = slice(core * half, core * half + half)
            at = 0
            for ref in refs[: len(tall)]:
                for b in range(ref.shape[1] // W):
                    block = ref[:, W * b : W * b + W].astype(BF16)
                    full_ref[at] = block
                    mine_ref[at] = block[own]
                    at += 1
            for ref in refs[len(tall) : count]:
                for b in range(4):
                    block = ref[b].astype(BF16)
                    full_ref[at] = block
                    mine_ref[at] = block[own]
                    at += 1
            if small:
                table_ref = refs[-1]
                start = 0
                for ref in refs[count : count + len(small)]:
                    table_ref[start : start + ref.shape[0]] = ref[...]
                    start += ref.shape[0]
                table_ref[start:] = jnp.zeros((SMALL - start, rows), F32)
                norms = refs[count + 1][...]
                left = norms - norms.astype(BF16).astype(F32)
                table_ref[NORMS_LOW : NORMS_LOW + norms.shape[0]] = left
                for h in range(2):
                    for q in range(W // rows):
                        first = h * (SMALL // 2) + q * half
                        value = table_ref[first : first + half, :].astype(BF16)
                        spot = slice(q * rows, q * rows + rows)
                        full_ref[at, h * half : h * half + half, spot] = value
                        if h == core:
                            mine_ref[at, :, spot] = value

        for core in range(2):

            @pl.when(where_ref[1] == core)
            def _(core=core):
                run(core)

    return pl.pallas_call(
        kernel,
        grid=(1,),
        in_specs=[SMEM]
        + [pl.BlockSpec((None, rows, x.shape[2]), lambda i: (index, 0, 0)) for x in tall]
        + [pl.BlockSpec((None, 4, rows, W), lambda i: (index, 0, 0, 0)) for x in wide]
        + [whole(x.shape) for x in small],
        out_specs=[whole((total, rows, W)), whole((total, half, W))],
        out_shape=[
            pltpu.HBM((total, rows, W), BF16),
            pltpu.HBM((total, half, W), BF16),
        ],
        scratch_shapes=[pltpu.VMEM((SMALL, rows), F32)] * bool(small),
        compiler_params=params(),
        cost_estimate=cost(total * rows * W, total * rows * W * 7),
        name="pack",
    )(where, *map(in_hbm, tall), *map(in_hbm, wide), *map(in_hbm, small))


def embed_step(place, where, target, maskf, group):
    shards = place.shards
    rows = D // shards
    half = rows // 2
    n = target.shape[0]
    sources = len(group)

    def kernel(where_ref, target_ref, mask_ref, *refs):
        pieces, refs = refs[:sources], refs[sources:]
        x_ref, inputs_ref, head_ref, norm_ref, got_ref, table_ref, sem = refs

        def targets(piece, at, part):
            start = 0 if part is None else pl.multiple_of(part * half, half)
            few = rows if part is None else half
            return [(piece.at[4], got_ref.at[at, pl.ds(start, few)])]

        fill_weights(0, where_ref, pieces, targets, sem)
        for j in range(shards):
            for h in range(2):
                for q in range(W // rows):
                    spot = slice(q * rows, q * rows + rows)
                    part = slice(h * half, h * half + half)
                    value = got_ref[j, part, spot].astype(F32)
                    first = h * (SMALL // 2) + q * half
                    table_ref[first : first + half, j * rows : j * rows + rows] = value
        inputs = jnp.where(mask_ref[...] > 0, 0.0, target_ref[...].astype(F32)).astype(BF16)
        inputs_ref[...] = inputs
        embed = table_ref[:P_SIZE].astype(BF16)
        for s in range(n // LEN):
            part = slice(s * LEN, s * LEN + LEN)
            x_ref[part] = dense(inputs[part], embed) + table_ref[2 * P_SIZE : 2 * P_SIZE + LEN]
        head_ref[...] = table_ref[P_SIZE : 2 * P_SIZE].astype(BF16)
        low = table_ref[NORMS_LOW : NORMS_LOW + 16]
        norm_ref[...] = table_ref[NORMS_LOW - 16 : NORMS_LOW] + low

    return pl.pallas_call(
        kernel,
        grid=(1,),
        in_specs=[SMEM, whole((n, P_SIZE)), whole((n, 1))] + [ANY] * sources,
        out_specs=[whole((n, D)), whole((n, P_SIZE)), whole((P_SIZE, D)), whole((16, D))],
        out_shape=[
            jax.ShapeDtypeStruct((n, D), F32),
            jax.ShapeDtypeStruct((n, P_SIZE), BF16),
            jax.ShapeDtypeStruct((P_SIZE, D), BF16),
            jax.ShapeDtypeStruct((16, D), F32),
        ],
        scratch_shapes=[
            pltpu.VMEM((shards, rows, W), BF16),
            pltpu.VMEM((SMALL, D), F32),
            pltpu.SemaphoreType.DMA((copies_of(group),)),
        ],
        compiler_params=params(),
        cost_estimate=cost(2 * n * D * P_SIZE, n * D * 5),
        name="embed_step",
    )(where, target, maskf, *group)


def copies_of(group):
    return 2 * (2 * (len(group) - 2) + 1)


def norm_parts(x):
    center = x - jnp.mean(x, -1, keepdims=True)
    rstd = lax.rsqrt(jnp.mean(center * center, -1, keepdims=True) + EPS)
    return center * rstd, rstd


def norm_back(xhat, rstd, dy, gain):
    dxh = dy * gain
    return rstd * (
        dxh - jnp.mean(dxh, -1, keepdims=True) - xhat * jnp.mean(dxh * xhat, -1, keepdims=True)
    )


def head_lanes(x, h):
    lane = lax.broadcasted_iota(jnp.int32, (x.shape[0], 128), 1)
    own = (lane < DH) if h % 2 == 0 else (lane >= DH)
    return jnp.where(own, x[:, pair_of(h)], 0)


def pair_of(h):
    return slice(128 * (h // 2), 128 * (h // 2) + 128)


def head_of(h):
    return slice(DH * h, DH * h + DH)


SP = 1


def attn_fwd(place, where, x, norms, group):
    rows = D // place.shards
    n = x.shape[0]
    seqs = n // LEN
    sources = len(group)

    def kernel(where_ref, x_ref, norm_ref, *refs):
        pieces, refs = refs[:sources], refs[sources:]
        mid_ref, qkv_ref, pt_ref, ot_ref, w_ref, sem = refs
        fill_weights(pl.program_id(0), where_ref, pieces, attn_targets(w_ref, rows), sem)
        spans = [slice(LEN * s, LEN * s + LEN) for s in range(SP)]
        a, q, k, vt = [], [], [], []
        for s, span in enumerate(spans):
            xhat, _ = norm_parts(x_ref[span])
            a.append((xhat * norm_ref[0:1, :] + norm_ref[1:2, :]).astype(BF16))
            q.append((dense(a[s], w_ref[0]) * DH**-0.5).astype(BF16))
            k.append(dense(a[s], w_ref[1]).astype(BF16))
            qkv_ref[span, :D] = q[s]
            qkv_ref[span, D : 2 * D] = k[s]

        def scores(s, h):
            return dense_nt(k[s][:, pair_of(h)], head_lanes(q[s], h))

        def gather_values(s, h, p):
            ot_ref[s, head_of(h), :] = dense(vt[s][head_of(h), :], p).astype(BF16)

        items = [(s, h) for h in range(H) for s in range(SP)]
        ahead = scores(*items[0])
        for s, span in enumerate(spans):
            v = dense(a[s], w_ref[2]).astype(BF16)
            qkv_ref[span, 2 * D :] = v
            vt.append(v.T)
        last = None
        for at, (s, h) in enumerate(items):
            st = ahead
            if at + 1 < len(items):
                ahead = scores(*items[at + 1])
            if last is not None:
                gather_values(*last)
            e = jnp.exp(st - jnp.max(st, axis=0, keepdims=True))
            p = (e * (1.0 / jnp.sum(e, axis=0, keepdims=True))).astype(BF16)
            pt_ref[s, h] = p
            last = (s, h, p)
        gather_values(*last)
        for s, span in enumerate(spans):
            mid_ref[span] = x_ref[span] + dense_tn(ot_ref[s], w_ref[3])

    return pl.pallas_call(
        kernel,
        grid=(seqs // SP,),
        in_specs=[SMEM, pl.BlockSpec((SP * LEN, D), lambda i: (i, 0)), whole((4, D))]
        + [ANY] * sources,
        out_specs=[
            pl.BlockSpec((SP * LEN, D), lambda i: (i, 0)),
            pl.BlockSpec((SP * LEN, 3 * D), lambda i: (i, 0)),
            pl.BlockSpec((SP, H, LEN, LEN), lambda i: (i, 0, 0, 0)),
            pl.BlockSpec((SP, D, LEN), lambda i: (i, 0, 0)),
        ],
        out_shape=[
            jax.ShapeDtypeStruct((n, D), F32),
            pltpu.HBM((n, 3 * D), BF16),
            pltpu.HBM((seqs, H, LEN, LEN), BF16),
            pltpu.HBM((seqs, D, LEN), BF16),
        ],
        scratch_shapes=[
            pltpu.VMEM((4, D, W), BF16),
            pltpu.SemaphoreType.DMA((copies_of(group),)),
        ],
        compiler_params=params(),
        cost_estimate=cost(2 * n * D * (4 * D + 2 * LEN), n * D * 20, n * H * LEN),
        name="attn_fwd",
    )(where, x, norms, *group)


def gelu_pair(u):
    cdf = 0.5 * lax.erf(u * 0.7071067811865476) + 0.5
    density = jnp.exp(u * u * -0.5) * 0.3989422804014327
    return u * cdf, cdf + u * density


def mlp_fwd(place, where, mid, norms, group):
    rows = D // place.shards
    n = mid.shape[0]
    tall = LEN
    step = W // 2
    sources = len(group)
    per = W // rows

    def kernel(where_ref, mid_ref, norm_ref, *refs):
        pieces, refs = refs[:sources], refs[sources:]
        out_ref, act_ref, gp_ref, up_ref, down_ref, sem = refs
        fill_weights(pl.program_id(0), where_ref, pieces, mlp_targets(up_ref, down_ref, rows), sem)
        mid = mid_ref[...]
        xhat, _ = norm_parts(mid)
        c = (xhat * norm_ref[2:3, :] + norm_ref[3:4, :]).astype(BF16)
        total = mid

        def upper(b):
            cols = slice(step * (b % 2), step * (b % 2) + step)
            return dense(c, up_ref[b // 2, :, cols])

        def lower(act, b):
            few = per // 2
            return dense(act, down_ref[few * b : few * b + few].reshape(step, D))

        ahead = upper(0)
        for b in range(FF // step):
            cols = slice(step * b, step * b + step)
            u = ahead
            if b + 1 < FF // step:
                ahead = upper(b + 1)
            if b > 0:
                total = total + lower(last, b - 1)
            act, slope = gelu_pair(u)
            last = act.astype(BF16)
            act_ref[:, cols] = last
            gp_ref[:, cols] = slope.astype(BF16)
        out_ref[...] = total + lower(last, FF // step - 1)

    def row(width):
        return pl.BlockSpec((tall, width), lambda i: (i, 0))

    return pl.pallas_call(
        kernel,
        grid=(n // tall,),
        in_specs=[SMEM, row(D), whole((4, D))] + [ANY] * sources,
        out_specs=[row(D), row(FF), row(FF)],
        out_shape=[
            jax.ShapeDtypeStruct((n, D), F32),
            pltpu.HBM((n, FF), BF16),
            pltpu.HBM((n, FF), BF16),
        ],
        scratch_shapes=[
            pltpu.VMEM((4, D, W), BF16),
            pltpu.VMEM((FF // rows, rows, D), BF16),
            pltpu.SemaphoreType.DMA((copies_of(group),)),
        ],
        compiler_params=params(),
        cost_estimate=cost(4 * n * D * FF, n * D * 24, n * FF * 2),
        name="mlp_fwd",
    )(where, mid, norms, *group)


def mlp_bwd(place, where, dz, mid, gp, norms, group):
    rows = D // place.shards
    n = mid.shape[0]
    sources = len(group)
    per = W // rows

    def kernel(where_ref, dz_ref, mid_ref, gp_ref, norm_ref, *refs):
        pieces, refs = refs[:sources], refs[sources:]
        dmid_ref, dh_ref, du_ref, c_ref, dm_ref, dn_ref, up_ref, down_ref, sem = refs
        i = pl.program_id(0)
        fill_weights(i, where_ref, pieces, mlp_targets(up_ref, down_ref, rows), sem)
        dm = dz_ref[...].astype(BF16)
        dm_ref[...] = dm

        def upper(b):
            return dense_nt(dm, down_ref[per * b : per * b + per].reshape(W, D))

        dc = jnp.zeros((LEN, D), F32)
        ahead = upper(0)
        for b in range(FF // W):
            cols = slice(W * b, W * b + W)
            da = ahead
            if b + 1 < FF // W:
                ahead = upper(b + 1)
            if b > 0:
                dc = dc + dense_nt(last, up_ref[b - 1])
            last = (gp_ref[:, cols].astype(F32) * da).astype(BF16)
            du_ref[:, cols] = last
        dc = dc + dense_nt(last, up_ref[FF // W - 1])
        xhat, rstd = norm_parts(mid_ref[...])
        gain = norm_ref[2:3, :]
        c_ref[...] = (xhat * gain + norm_ref[3:4, :]).astype(BF16)
        dmid = dz_ref[...] + norm_back(xhat, rstd, dc, gain)
        dmid_ref[...] = dmid
        dh_ref[...] = dmid.astype(BF16)

        @pl.when(i == 0)
        def _():
            dn_ref[...] = jnp.zeros_like(dn_ref)

        dn_ref[0:1, :] += jnp.sum(dc * xhat, 0, keepdims=True)
        dn_ref[1:2, :] += jnp.sum(dc, 0, keepdims=True)

    def row(width):
        return pl.BlockSpec((LEN, width), lambda i: (i, 0))

    return pl.pallas_call(
        kernel,
        grid=(n // LEN,),
        in_specs=[SMEM, row(D), row(D), row(FF), whole((4, D))] + [ANY] * sources,
        out_specs=[row(D), row(D), row(FF), row(D), row(D), whole((8, D))],
        out_shape=[
            jax.ShapeDtypeStruct((n, D), F32),
            jax.ShapeDtypeStruct((n, D), BF16),
            jax.ShapeDtypeStruct((n, FF), BF16),
            jax.ShapeDtypeStruct((n, D), BF16),
            jax.ShapeDtypeStruct((n, D), BF16),
            jax.ShapeDtypeStruct((8, D), F32),
        ],
        scratch_shapes=[
            pltpu.VMEM((4, D, W), BF16),
            pltpu.VMEM((FF // rows, rows, D), BF16),
            pltpu.SemaphoreType.DMA((copies_of(group),)),
        ],
        compiler_params=params(),
        cost_estimate=cost(4 * n * D * FF, n * D * 32),
        name="mlp_bwd",
    )(where, dz, mid, in_hbm(gp), norms, *group)


def attn_bwd(place, where, dmid, dh, x, qkv, pt, ot, norms, group):
    rows = D // place.shards
    n = x.shape[0]
    seqs = n // LEN
    sources = len(group)

    def kernel(where_ref, dmid_ref, dh_ref, x_ref, qkv_ref, pt_ref, ot_ref, norm_ref, *refs):
        pieces, refs = refs[:sources], refs[sources:]
        dx_ref, dqkv_ref, a_ref, dn_ref, w_ref, dqt_ref, sem = refs
        i = pl.program_id(0)
        fill_weights(i, where_ref, pieces, attn_targets(w_ref, rows), sem)
        spans = [slice(None)]
        do, delta, kt = [], [], []
        for s, span in enumerate(spans):
            do.append(dense_nt(dh_ref[span], w_ref[3]).astype(BF16))
            along = do[s].T.astype(F32) * ot_ref[s].astype(F32)
            delta.append([jnp.sum(along[head_of(h), :], axis=0, keepdims=True) for h in range(H)])
            kt.append(qkv_ref[span, D : 2 * D].T)

        def first(s, h):
            doh = head_lanes(do[s], h)
            v = qkv_ref[spans[s], 2 * D + 128 * (h // 2) : 2 * D + 128 * (h // 2) + 128]
            return dense_nt(v, doh), dense(pt_ref[s, h], doh)

        halves = {}

        def second(s, h, dst, dv):
            q = qkv_ref[spans[s], pair_of(h)]
            lane = lax.broadcasted_iota(jnp.int32, (LEN, 128), 1)
            own = (lane < DH) if h % 2 == 0 else (lane >= DH)
            dk = dense(dst, jnp.where(own, q, 0))
            dqt_ref[s, head_of(h), :] = (dense(kt[s][head_of(h), :], dst) * DH**-0.5).astype(BF16)
            if h % 2 == 0:
                halves[s] = (dk, dv)
                return
            at = 128 * (h // 2)
            dk, dv = dk + halves[s][0], dv + halves[s][1]
            dqkv_ref[spans[s], D + at : D + at + 128] = dk.astype(BF16)
            dqkv_ref[spans[s], 2 * D + at : 2 * D + at + 128] = dv.astype(BF16)

        items = [(s, h) for h in range(H) for s in range(1)]
        ahead = first(*items[0])
        last = None
        for at, (s, h) in enumerate(items):
            dpt, dv = ahead
            if at + 1 < len(items):
                ahead = first(*items[at + 1])
            if last is not None:
                second(*last)
            dst = (pt_ref[s, h].astype(F32) * (dpt - delta[s][h])).astype(BF16)
            last = (s, h, dst, dv)
        second(*last)

        @pl.when(i == 0)
        def _():
            dn_ref[...] = jnp.zeros_like(dn_ref)

        gain = norm_ref[0:1, :]
        for s, span in enumerate(spans):
            da = dense_nt(dqkv_ref[span, D : 2 * D], w_ref[1])
            da = da + dense_nt(dqkv_ref[span, 2 * D :], w_ref[2])
            dq = dqt_ref[s].T
            dqkv_ref[span, :D] = dq
            da = da + dense_nt(dq, w_ref[0])
            xhat, rstd = norm_parts(x_ref[span])
            a_ref[span] = (xhat * gain + norm_ref[1:2, :]).astype(BF16)
            dx_ref[span] = dmid_ref[span] + norm_back(xhat, rstd, da, gain)
            dn_ref[0:1, :] += jnp.sum(da * xhat, 0, keepdims=True)
            dn_ref[1:2, :] += jnp.sum(da, 0, keepdims=True)

    def row(width):
        return pl.BlockSpec((LEN, width), lambda i: (i, 0))

    return pl.pallas_call(
        kernel,
        grid=(seqs,),
        in_specs=[
            SMEM,
            row(D),
            row(D),
            row(D),
            row(3 * D),
            pl.BlockSpec((1, H, LEN, LEN), lambda i: (i, 0, 0, 0)),
            pl.BlockSpec((1, D, LEN), lambda i: (i, 0, 0)),
            whole((4, D)),
        ]
        + [ANY] * sources,
        out_specs=[row(D), row(3 * D), row(D), whole((8, D))],
        out_shape=[
            jax.ShapeDtypeStruct((n, D), F32),
            jax.ShapeDtypeStruct((n, 3 * D), BF16),
            jax.ShapeDtypeStruct((n, D), BF16),
            jax.ShapeDtypeStruct((8, D), F32),
        ],
        scratch_shapes=[
            pltpu.VMEM((4, D, W), BF16),
            pltpu.VMEM((1, D, LEN), BF16),
            pltpu.SemaphoreType.DMA((copies_of(group),)),
        ],
        compiler_params=params(),
        cost_estimate=cost(2 * n * D * (4 * D + 5 * LEN), n * D * 32),
        name="attn_bwd",
    )(where, dmid, dh, x, in_hbm(qkv), in_hbm(pt), in_hbm(ot), norms, *group)


def head_step(place, x, target, maskf, head, norms, count):
    n = x.shape[0]

    def kernel(x_ref, target_ref, mask_ref, head_ref, norm_ref, dx_ref, loss_ref, gh_ref, dn_ref):
        i = pl.program_id(0)
        xhat, rstd = norm_parts(x_ref[...])
        gain = norm_ref[0:1, :]
        y = (xhat * gain + norm_ref[1:2, :]).astype(BF16)
        masked = mask_ref[...]
        err = (dense_nt(y, head_ref[...]) - target_ref[...].astype(F32)) * masked
        dpred = (err * (2.0 / (P_SIZE * count))).astype(BF16)
        dy = dense(dpred, head_ref[...])
        dx_ref[...] = norm_back(xhat, rstd, dy, gain)

        @pl.when(i == 0)
        def _():
            loss_ref[...] = jnp.zeros_like(loss_ref)
            gh_ref[...] = jnp.zeros_like(gh_ref)
            dn_ref[...] = jnp.zeros_like(dn_ref)

        loss_ref[...] += jnp.sum(err * err, 0, keepdims=True)
        gh_ref[...] += dense_tn(dpred, y)
        dn_ref[0:1, :] += jnp.sum(dy * xhat, 0, keepdims=True)
        dn_ref[1:2, :] += jnp.sum(dy, 0, keepdims=True)

    def row(width):
        return pl.BlockSpec((LEN, width), lambda i: (i, 0))

    return pl.pallas_call(
        kernel,
        grid=(n // LEN,),
        in_specs=[row(D), row(P_SIZE), row(1), whole((P_SIZE, D)), whole((2, D))],
        out_specs=[row(D), whole((1, P_SIZE)), whole((P_SIZE, D)), whole((8, D))],
        out_shape=[
            jax.ShapeDtypeStruct((n, D), F32),
            jax.ShapeDtypeStruct((1, P_SIZE), F32),
            jax.ShapeDtypeStruct((P_SIZE, D), F32),
            jax.ShapeDtypeStruct((8, D), F32),
        ],
        compiler_params=params(),
        cost_estimate=cost(6 * n * D * P_SIZE, n * D * 8),
        name="head_step",
    )(x, target, maskf, head, norms)


def put_block(core, block, lead, send_ref, keep_ref, at):
    rows = block.shape[0]
    halves = block.reshape(lead + (2, rows // (2 * lead_size(lead)), W))
    first, second = halves[..., 0, :, :], halves[..., 1, :, :]
    keep_ref[at] = jnp.where(core == 0, first, second)
    send_ref[at] = jnp.where(core == 0, second, first)


def lead_size(lead):
    size = 1
    for n in lead:
        size *= n
    return size


def grad_mlp(place, where, c, du, act, dm, ot, dh):
    shards = place.shards
    rows = D // shards
    n = c.shape[0]
    seqs = n // LEN
    wide = 2 * W
    steps = FF // wide
    per = shards // steps
    blocks = 9

    def kernel(where_ref, c_ref, du_ref, act_ref, dm_ref, ot_ref, dh_ref, send_ref, keep_ref, ct_ref):
        i = pl.program_id(0)
        core = where_ref[1]

        @pl.when(i == 0)
        def _():
            ct_ref[...] = c_ref[...].T

        @pl.when(i < steps)
        def _():
            block = dense(ct_ref[...], du_ref[...]).astype(BF16)
            for b in range(wide // W):
                at = (slice(None), i * (wide // W) + b)
                put_block(core, block[:, W * b : W * b + W], (shards,), send_ref, keep_ref, at)

        @pl.when((i >= steps) & (i < 2 * steps))
        def _():
            block = dense_tn(act_ref[...], dm_ref[...]).astype(BF16)
            at = (pl.ds((i - steps) * per, per), slice(4, 8))
            put_block(core, block, (per, 4), send_ref, keep_ref, at)

        @pl.when(i == 2 * steps)
        def _():
            total = dense(ot_ref[0], dh_ref[:LEN, :])
            for s in range(1, seqs):
                total = total + dense(ot_ref[s], dh_ref[LEN * s : LEN * s + LEN, :])
            put_block(core, total.astype(BF16), (shards,), send_ref, keep_ref, (slice(None), 8))

    shape = (shards, blocks, rows // 2, W)
    return pl.pallas_call(
        kernel,
        grid=(2 * steps + 1,),
        in_specs=[
            SMEM,
            whole((n, D)),
            pl.BlockSpec((n, wide), lambda i: (0, jnp.minimum(i, steps - 1))),
            pl.BlockSpec((n, wide), lambda i: (0, jnp.clip(i - steps, 0, steps - 1))),
            whole((n, D)),
            whole((seqs, D, LEN)),
            whole((n, D)),
        ],
        out_specs=[whole(shape), whole(shape)],
        scratch_shapes=[pltpu.VMEM((D, n), BF16)],
        out_shape=[jax.ShapeDtypeStruct(shape, BF16)] * 2,
        compiler_params=params(),
        cost_estimate=cost(4 * n * D * FF, n * (4 * D + 4 * FF) + 4 * D * FF),
        name="grad_mlp",
    )(where, c, du, in_hbm(act), dm, in_hbm(ot), dh)


def grad_qkv(place, where, a, dqkv, small=()):
    shards = place.shards
    rows = D // shards
    half = rows // 2
    n = a.shape[0]
    blocks = 3 + bool(small)
    extra = len(small)

    def kernel(where_ref, a_ref, dqkv_ref, *refs):
        small_refs, refs = refs[:extra], refs[extra:]
        send_ref, keep_ref, at_ref = refs[:3]
        i = pl.program_id(0)

        @pl.when(i == 0)
        def _():
            at_ref[...] = a_ref[...].T

        @pl.when(i < 3)
        def _():
            block = dense(at_ref[...], dqkv_ref[...]).astype(BF16)
            put_block(where_ref[1], block, (shards,), send_ref, keep_ref, (slice(None), i))

        if extra:
            table_ref = refs[3]
            inputs_ref, dx_ref, head_ref = small_refs[:3]

            @pl.when(i == 3)
            def _():
                dx = dx_ref[...]
                table_ref[:P_SIZE] = dense_tn(inputs_ref[...], dx.astype(BF16)).astype(BF16)
                table_ref[P_SIZE : 2 * P_SIZE] = head_ref[...].astype(BF16)
                total = dx[:LEN]
                for s in range(1, n // LEN):
                    total = total + dx[s * LEN : s * LEN + LEN]
                table_ref[2 * P_SIZE : 2 * P_SIZE + LEN] = total.astype(BF16)
                norms = jnp.concatenate(
                    [ref[0:2, :] for ref in small_refs[3:]]
                    + [jnp.zeros((16 - 2 * (extra - 3), D), F32)],
                    0,
                )
                start = 2 * P_SIZE + LEN
                table_ref[start : start + 16] = norms.astype(BF16)
                table_ref[start + 16 :] = jnp.zeros((SMALL - start - 16, D), BF16)
                for core in range(2):

                    @pl.when(where_ref[1] == core)
                    def _(core=core):
                        for h in range(2):
                            out_ref = keep_ref if h == core else send_ref
                            for j in range(shards):
                                for q in range(W // rows):
                                    first = h * (SMALL // 2) + q * half
                                    value = table_ref[first : first + half, j * rows : j * rows + rows]
                                    out_ref[j, 3, :, q * rows : q * rows + rows] = value

    shape = (shards, blocks, half, W)
    return pl.pallas_call(
        kernel,
        grid=(blocks,),
        in_specs=[SMEM, whole((n, D)), pl.BlockSpec((n, W), lambda i: (0, jnp.minimum(i, 2)))]
        + [whole(x.shape) for x in small],
        out_specs=[whole(shape), whole(shape)],
        scratch_shapes=[pltpu.VMEM((D, n), BF16)] + [pltpu.VMEM((SMALL, D), BF16)] * bool(small),
        out_shape=[jax.ShapeDtypeStruct(shape, BF16)] * 2,
        compiler_params=params(),
        cost_estimate=cost(6 * n * D * D, n * 8 * D + 6 * D * D),
        name="grad_qkv",
    )(where, a, dqkv, *small)


def adam(weight, first, second, grad, rate):
    first = BETA_ONE * first + (1 - BETA_ONE) * grad
    second = BETA_TWO * second + (1 - BETA_TWO) * grad * grad
    spread = second * (1 / (1 - BETA_TWO**STEP_COUNT))
    lower = 1.0 / (spread * lax.rsqrt(spread) + ADAM_EPS)
    weight = weight * (1 - rate * DECAY) - first * lower * (rate / (1 - BETA_ONE**STEP_COUNT))
    return (weight, first, second)


def adam_step(place, where, factor, state, small, grads, chip):
    rows = D // place.shards
    half = rows // 2
    few = half // 2
    flat = [x for group in state for x in group]
    tiny = [x for group in small for x in group]

    def spec(x):
        if x.ndim == 4:
            return pl.BlockSpec((None, 4, few, W), lambda i, h, q: (i, 0, 2 * h + q, 0))
        return pl.BlockSpec((None, few, x.shape[2]), lambda i, h, q: (i, 2 * h + q, 0))

    gflat, spots = [], []
    for layer in grads:
        spots.append([])
        for pieces, first in layer:
            known = [n for n, x in enumerate(gflat) if x is pieces[0]]
            spots[-1].append((known[0] if known else len(gflat), len(pieces), first))
            gflat += [] if known else list(pieces)
    total = len(flat) + len(tiny)

    def kernel(where_ref, factor_ref, *refs):
        grad_refs, refs = refs[: len(gflat)], refs[len(gflat) :]
        ins, outs, table_ref = refs[:total], refs[total : 2 * total], refs[-1]
        layer, h, q = pl.program_id(0), pl.program_id(1), pl.program_id(2)
        scale = factor_ref[0]
        own = where_ref[1] == h
        near = where_ref[chip] == q

        def update(n, at, grad, rate):
            got = adam(ins[3 * n][at], ins[3 * n + 1][at], ins[3 * n + 2][at], grad, rate)
            for k in range(3):
                outs[3 * n + k][at] = got[k]

        part = pl.ds(pl.multiple_of(q * few, few), few)

        def run(layer):
            def grad(group, b):
                base, count, first = spots[layer][group]
                refs = grad_refs[base : base + count]
                if count == 2:
                    got = jnp.where(own, refs[0][first + b, part], refs[1][first + b, part])
                else:
                    close = jnp.where(own, refs[0][first + b], refs[1][first + b])
                    away = jnp.where(own, refs[2][first + b], refs[3][first + b])
                    got = jnp.where(near, close, away)
                return got.astype(F32) * scale

            for b in range(3):
                update(0, (slice(None), slice(W * b, W * b + W)), grad(0, b), RATE)
            update(1, (slice(None), slice(None)), grad(1, 8), RATE)
            for b in range(4):
                update(2, (slice(None), slice(W * b, W * b + W)), grad(1, b), RATE)
                update(3, (b,), grad(1, 4 + b), RATE)

        for i in range(L):

            @pl.when(layer == i)
            def _(i=i):
                run(i)

        @pl.when((layer == 0) & (h == 0) & (q == 0))
        def _():
            base, _, at = spots[0][0]
            mine, other = grad_refs[base][at + 3], grad_refs[base + 1][at + 3]
            first = where_ref[1] == 0
            for n, block in enumerate((jnp.where(first, mine, other), jnp.where(first, other, mine))):
                for k in range(W // rows):
                    start = n * (SMALL // 2) + k * half
                    table_ref[start : start + half] = (
                        block[:, k * rows : k * rows + rows].astype(F32) * scale
                    )
            count = 2 * P_SIZE + LEN
            update(4, (slice(None), slice(None)), table_ref[:count], TABLE_RATE)
            norms = small[1][0].shape[0]
            update(5, (slice(None), slice(None)), table_ref[count : count + norms], TABLE_RATE)

    out = pl.pallas_call(
        kernel,
        grid=(L, 2, 2),
        in_specs=[SMEM, SMEM]
        + [whole(g.shape) for g in gflat]
        + [spec(x) for x in flat]
        + [whole(x.shape) for x in tiny],
        out_specs=[spec(x) for x in flat] + [whole(x.shape) for x in tiny],
        out_shape=[pltpu.HBM(x.shape, F32) for x in flat + tiny],
        scratch_shapes=[pltpu.VMEM((SMALL, rows), F32)],
        compiler_params=params(),
        cost_estimate=cost(20 * L * 12 * rows * W, 24 * L * 12 * rows * W),
        name="adam_step",
    )(where, factor, *gflat, *map(in_hbm, flat), *map(in_hbm, tiny))
    return [tuple(out[3 * n : 3 * n + 3]) for n in range(len(state) + len(small))]


def on_device(
    series,
    mask,
    qkv_w,
    out_w,
    up_w,
    down_w,
    patch_maps,
    norm_params,
    qkv_m,
    out_m,
    up_m,
    down_m,
    patch_m,
    norm_m,
    qkv_v,
    out_v,
    up_v,
    down_v,
    patch_v,
    norm_v,
):
    place = Place()
    shards = place.shards
    rows = D // shards
    half = rows // 2
    seqs = series.shape[0]
    count = MASKED * seqs * shards * place.replicas
    shard_bits = [(place.shard >> bit) & 1 for bit in bits_of(shards)]
    where = jnp.stack([place.shard, place.core] + shard_bits + [place.chip & 1]).astype(jnp.int32)
    chip = 2 + len(shard_bits)

    small_now = [patch_maps, norm_params]
    packs = [
        (
            pack(place, where, i, [qkv_w, out_w], [], small_now if i == 0 else []),
            pack(place, where, i, [up_w], [down_w], []),
        )
        for i in range(L)
    ]

    def group_of(packed, ours, theirs):
        return [packed[0]] + ours + [theirs]

    attn_groups = [None] * L
    mlp_groups = [None] * L
    target = series.reshape(seqs * LEN, P_SIZE)
    maskf = mask.reshape(seqs * LEN, 1).astype(F32)
    ours = gather_shards(place, packs[0][0][1])
    theirs = gather_cores(place, ours, *[p[1] for pair in packs for p in pair], target, maskf)
    attn_groups[0] = group_of(packs[0][0], ours, theirs)
    mine = gate(packs[0][1][1], *ours)
    ours_mlp = gather_shards(place, mine)

    x, inputs, head, norms_all = embed_step(place, where, target, gate(maskf, mine), attn_groups[0])
    saved = []
    for index in range(L):
        norms = norms_all[4 * index : 4 * index + 4]
        mid, qkv, pt, ot = attn_fwd(place, where, x, norms, attn_groups[index])
        held = mid
        if index + 1 < L:
            got = gates(ours_mlp, mid)
            mine = gate(packs[index + 1][0][1], *got)
            ours_attn = gather_shards(place, mine)
            held = gate(mid, mine)
        theirs = gather_cores(place, ours_mlp, mid)
        mlp_groups[index] = group_of(packs[index][1], ours_mlp, theirs)
        pieces = mlp_groups[index] if index == 0 else [in_hbm(x) for x in mlp_groups[index]]
        y, act, gp = mlp_fwd(place, where, held, norms, pieces)
        if index + 1 < L:
            got = gates(ours_attn, y)
            theirs = gather_cores(place, got)
            attn_groups[index + 1] = group_of(packs[index + 1][0], ours_attn, theirs)
            mine = gate(packs[index + 1][1][1], *got)
            ours_mlp = gather_shards(place, mine)
            y = gate(y, mine)
        saved.append((x, mid, qkv, pt, ot, act, gp, norms))
        x = y

    grad, loss, g_head, dn_final = head_step(
        place, x, target, maskf, head, norms_all[4 * L : 4 * L + 2], count
    )
    loss = (jnp.sum(loss) / P_SIZE).reshape(1, 1)

    norm_grads = {}

    def backward_mlp(index, grad):
        x, mid, qkv, pt, ot, act, gp, norms = saved[index]
        dmid, dh, du, c, dm, dn = mlp_bwd(
            place, where, grad, mid, gp, norms, mlp_groups[index]
        )
        norm_grads[index, 1] = dn
        return dmid, dh, du, c, dm

    def backward_attn(index, dmid, dh):
        x, mid, qkv, pt, ot, act, gp, norms = saved[index]
        grad, dqkv, a, dn = attn_bwd(
            place, where, dmid, dh, x, qkv, pt, ot, norms, attn_groups[index]
        )
        norm_grads[index, 0] = dn
        return grad, dqkv, a

    def grads_mlp(index, du, c, dm, dh):
        return grad_mlp(place, where, c, du, saved[index][5], dm, saved[index][4], dh)

    one, two, end = Flow(place, True), Flow(place, True), Flow(place, False)

    def advance(flows, *after):
        token = sum_round(where, flows, *after)
        for flow in flows:
            flow.launch()
        return token

    loss = loss + place.to_core(loss)
    dmid, dh, du, c, dm = backward_mlp(1, grad)
    token = one.begin(*grads_mlp(1, du, c, dm, dh), (0, 4, 0), (4, 5, 1))
    grad, dqkv_one, a_one = backward_attn(1, gate(dmid, token), dh)
    token = advance([one], grad)
    dmid, dh, du, c, dm = backward_mlp(0, gate(grad, token))
    token = advance([one], dmid)
    token = two.begin(*grads_mlp(0, du, gate(c, token), dm, dh), (0, 4, 0), (4, 5, 1))
    token = advance([one], token)
    token = end.begin(*grad_qkv(place, where, gate(a_one, token), dqkv_one), (0, 3, 0))
    token = advance([two], token)
    grad, dqkv, a = backward_attn(0, gate(dmid, token), dh)
    token = sum_round(where, [one, two], grad)
    small = [inputs, grad, g_head]
    small += [norm_grads[i, k] for i in range(L) for k in range(2)] + [dn_final]
    token = end.begin(*grad_qkv(place, where, gate(a, token), dqkv, small), (0, 4, 1))
    one.launch()
    two.launch()
    while not one.last():
        token = advance([one], token)
    token = sum_round(where, [one, two, end], token)
    end.launch()
    two.launch()
    one.to_neighbours()
    hops = bits_of(place.chips)

    def pass_loss(loss, token):
        if not hops:
            return loss
        return loss + place.to_chip(gate(loss, token), 1 << hops.pop(0))

    while end.step < end.steps - 2:
        loss = pass_loss(loss, token)
        token = sum_round(where, [end] + ([two] if not two.last() else []), token, *one.pieces, loss)
        end.launch()
        if two.step == two.steps - 1:
            break
        if not two.last():
            two.launch()
    one.to_last()
    behind = not two.last()
    while end.step < end.steps - 1:
        loss = pass_loss(loss, token)
        token = advance([end], token, *one.pieces, loss)
    if behind:
        two.launch()
    while hops:
        loss = pass_loss(loss, token)
    state = [(qkv_w, qkv_m, qkv_v), (out_w, out_m, out_v), (up_w, up_m, up_v)]
    state.append(tuple(x.reshape(L, 4, rows, W) for x in (down_w, down_m, down_v)))
    token = sum_round(where, [end, two], token, loss)
    end.launch()
    two.to_neighbours()
    token = sum_round(where, [end], token, *two.pieces)
    end.to_neighbours()
    two.to_last()
    grads = [
        [(end.pieces, 3), (two.pieces, 0)],
        [(end.pieces, 0), (one.pieces, 0)],
    ]
    done_one, done_two, done_last = one.pieces, two.pieces, end.pieces

    both = jnp.concatenate([loss, square_sum(done_one + done_two + done_last)], 1)
    both = sum([place.to_shard(both, k) for k in range(1, shards)], both)
    loss = both[0, 0] / count
    grad_norm = jnp.sqrt(both[0, 1])
    factor = CLIP / jnp.maximum(grad_norm, CLIP)

    small = [(patch_maps, patch_m, patch_v), (norm_params, norm_m, norm_v)]
    results = adam_step(place, where, factor.reshape(1), state, small, grads, chip)
    results[3] = tuple(x.reshape(down_w.shape) for x in results[3])
    news = tuple(r[0] for r in results)
    new_m = tuple(r[1] for r in results)
    new_v = tuple(r[2] for r in results)
    return (loss, grad_norm) + news + new_m + new_v


def solution(mesh):
    batch = P(("shard", "replica"), None)
    stack = P(None, "shard", None)
    flat = P(None, "shard")
    state = (stack, stack, stack, stack, flat, flat)
    return jax.shard_map(
        on_device,
        mesh=mesh,
        in_specs=(batch, batch) + state * 3,
        out_specs=(P(), P()) + state * 3,
        check_vma=False,
    )
```

```python
import jax
import jax.numpy as jnp
from jax import lax
from jax.experimental import pallas as pl
from jax.experimental.pallas import tpu as pltpu
from jax.sharding import PartitionSpec as P

D = 512
H = 8
DH = 64
FF = 2048
P_SIZE = 64
LEN = 256
L = 2
MASKED = 102

EPS = 1e-05
CLIP = 0.001
RATE = 0.05
TABLE_RATE = 0.3
BETA_ONE = 0.9
BETA_TWO = 0.999
ADAM_EPS = 1e-08
DECAY = 0.1
STEP_COUNT = 10

W = 512
SMALL = 512
NORMS_LOW = 2 * P_SIZE + LEN + 16
F32 = jnp.float32
BF16 = jnp.bfloat16


def dense(left, right):
    return jnp.dot(left, right, preferred_element_type=F32)


def dense_tn(left, right):
    return lax.dot_general(left, right, (((0,), (0,)), ((), ())), preferred_element_type=F32)


def dense_nt(left, right):
    return lax.dot_general(left, right, (((1,), (1,)), ((), ())), preferred_element_type=F32)


def layer_norm(x, gain, bias):
    center = x - jnp.mean(x, -1, keepdims=True)
    spread = jnp.mean(center * center, -1, keepdims=True)
    return center * lax.rsqrt(spread + EPS) * gain + bias


def params(mib=30):
    return pltpu.CompilerParams(vmem_limit_bytes=mib * 2**20)


def cost(flops, data, trans=0):
    return pl.CostEstimate(
        flops=int(30 * flops), bytes_accessed=int(30 * data), transcendentals=int(30 * trans)
    )


def whole(shape):
    return pl.BlockSpec(shape, lambda *_: (0,) * len(shape))


def in_hbm(x):
    return pltpu.with_memory_space_constraint(x, pltpu.HBM)


ANY = pl.BlockSpec(memory_space=pl.ANY)
SMEM = pl.BlockSpec(memory_space=pltpu.SMEM)


def permute(x, axis, mask, size):
    return lax.ppermute(x, axis, [(i, i ^ mask) for i in range(size)])


def pick(x, index):
    return lax.dynamic_index_in_dim(x, index, 0, keepdims=False)


class Place:
    def __init__(self):
        self.shards = lax.axis_size("shard")
        self.replicas = lax.axis_size("replica")
        self.chips = self.replicas // 2
        self.shard = lax.axis_index("shard")
        replica = lax.axis_index("replica")
        self.core = replica % 2
        self.chip = replica // 2

    def to_core(self, x):
        return permute(x, "replica", 1, self.replicas)

    def to_shard(self, x, mask):
        return permute(x, "shard", mask, self.shards)

    def to_chip(self, x, mask):
        return permute(x, "replica", 2 * mask, self.replicas)


def gate(x, *after):
    return lax.optimization_barrier((x,) + after)[0]


def gather_shards(place, mine):
    return [place.to_shard(mine, mask) for mask in range(1, place.shards)]


def gather_cores(place, ours, *after):
    return place.to_core(jnp.stack(gates(ours, *after)))


def gates(items, *after):
    return list(lax.optimization_barrier(tuple(items) + after)[: len(items)])


def select_of(items, index):
    out = items[0]
    for k in range(1, len(items)):
        out = jnp.where(index == k, items[k], out)
    return out


def bits_of(size):
    return list(range(size.bit_length() - 1))


def total_of(values):
    total = values[0].astype(F32)
    for value in values[1:]:
        total = total + value.astype(F32)
    return total


def combine(where, jobs, name):
    lanes = W // 2
    arrays, leads, plans, shapes = [], [], [], []

    def number(array, lead):
        for n, known in enumerate(arrays):
            if known is array:
                return n
        arrays.append(array)
        leads.append(lead)
        return len(arrays) - 1

    for segments, lead, cut, bit in jobs:
        plans.append([[(number(a, lead), f, b) for a, f, b in parts] for parts in segments])
        blocks = sum(parts[0][2] for parts in segments)
        rows = segments[0][0][0].shape[-2]
        if cut is None:
            shapes.append(lead + (blocks, rows, W))
        elif cut == "rows":
            shapes += [lead + (blocks, rows // 2, W)] * 2
        else:
            shapes += [lead[:cut] + lead[cut + 1 :] + (blocks, rows, W)] * 2
    arrays = [a.reshape(lead + a.shape[-3:]) for a, lead in zip(arrays, leads)]

    def block(shape):
        zeros = (0,) * (len(shape) - 1)
        return pl.BlockSpec(shape[:-1] + (lanes,), lambda i: zeros + (i,))

    def kernel(where_ref, *refs):
        ins, outs = refs[: len(arrays)], list(refs[len(arrays) :])
        for (segments, lead, cut, bit), plan in zip(jobs, plans):
            some = (slice(None),) * len(lead)
            fewer = (slice(None),) * (len(lead) - (cut is not None and cut != "rows"))
            if cut is None:
                targets = [(outs.pop(0), None)]
            else:
                value = where_ref[bit]
                targets = [(outs.pop(0), 1 - value), (outs.pop(0), value)]
            for out_ref, at in targets:
                start = 0
                for parts in plan:
                    got = []
                    for n, f, b in parts:
                        index = some
                        if cut is not None and cut != "rows":
                            index = some[:cut] + (at,) + some[cut + 1 :]
                        index += (slice(f, f + b),)
                        if cut == "rows":
                            few = ins[n].shape[-2] // 2
                            index += (pl.ds(pl.multiple_of(at * few, few), few),)
                        got.append(ins[n][index])
                    out_ref[fewer + (slice(start, start + parts[0][2]),)] = total_of(got).astype(BF16)
                    start += parts[0][2]

    size = sum(a.size for a in arrays) * 4
    return pl.pallas_call(
        kernel,
        grid=(2,),
        in_specs=[SMEM] + [block(a.shape) for a in arrays],
        out_specs=[block(s) for s in shapes],
        out_shape=[jax.ShapeDtypeStruct(s, BF16) for s in shapes],
        compiler_params=params(12),
        cost_estimate=cost(size, size),
        name=name,
    )(where, *arrays)


class Flow:
    def __init__(self, place, spread, far_first=False):
        self.place, self.spread = place, spread
        self.chip_bits = bits_of(place.chips)[:: -1 if far_first else 1]
        self.bits = bits_of(place.shards)
        self.steps = len(self.bits) + len(bits_of(place.chips))
        self.step = 0
        self.inputs = []
        self.ranges = []

    def begin(self, send, keep, *ranges):
        other = self.place.to_core(send)
        for first, blocks, order in ranges:
            self.ranges.append((len(self.inputs), first, blocks, order))
        self.inputs += [keep, other]
        self.left = [list(reversed(self.bits)) for _ in self.ranges]
        return send

    def join(self, other):
        self.inputs = other.inputs + self.inputs
        self.ranges = other.ranges + self.ranges
        self.left = other.left + self.left

    def last(self):
        return self.step == self.steps

    def plan(self, flat):
        if self.step == 0:
            parts = [[(flat[n], f, b), (flat[n + 1], f, b)] for n, f, b, _ in self.ranges]
        else:
            parts = [
                [(x, 0, x.shape[-3]) for x in flat[2 * n : 2 * n + 2]]
                for n in range(len(flat) // 2)
            ]
        if self.step >= len(self.bits):
            cut = self.spread and self.step == len(self.bits)
            bit = 2 + len(self.bits) + self.chip_bits[0]
            return [(parts, (), "rows", bit) if cut else (parts, (), None, 0)]
        jobs, self.chosen = [], []
        for n, (_, _, _, order) in enumerate(self.ranges):
            bit = (self.bits if order == 0 else self.bits[::-1])[self.step]
            jobs.append(([parts[n]], (2,) * len(self.left[n]), self.left[n].index(bit), 2 + bit))
            self.left[n].remove(bit)
            self.chosen.append(bit)
        return jobs

    def take(self, out):
        if self.step < len(self.bits):
            self.sends, self.stays = out[0::2], out[1::2]
        else:
            self.sends, self.stays = out[:1], out[-1:]
        return self.sends[0]

    def launch(self):
        place = self.place
        if self.step < len(self.bits):
            got = [place.to_shard(x, 1 << bit) for x, bit in zip(self.sends, self.chosen)]
        else:
            bit = self.chip_bits[self.step - len(self.bits)]
            got = [place.to_chip(x, 1 << bit) for x in self.sends]
        self.inputs = [x for pair in zip(self.stays, got) for x in pair]
        self.step += 1

    def to_neighbours(self):
        self.pieces = [self.sends[0], self.place.to_core(self.sends[0])]
        if self.spread:
            self.pieces.append(self.place.to_chip(self.sends[0], 1 << self.chip_bits[0]))

    def to_last(self):
        if self.spread:
            self.pieces.append(self.place.to_core(self.pieces[2]))


def sum_round(where, flows, *after):
    flat = gates([x for flow in flows for x in flow.inputs], *after)
    jobs, counts = [], []
    for flow in flows:
        few = len(flow.inputs)
        some = flow.plan(flat[:few])
        flat = flat[few:]
        jobs += some
        counts.append(sum(1 if cut is None else 2 for _, _, cut, _ in some))
    out = combine(where, jobs, "sum_round")
    for flow, count in zip(flows, counts):
        token = flow.take(out[:count])
        out = out[count:]
    return token


def square_sum(pieces, loss):
    def kernel(loss_ref, *refs):
        total = jnp.zeros((1, W), F32)
        for ref in refs[:-1]:
            for b in range(ref.shape[0]):
                x = ref[b].astype(F32)
                total = total + jnp.sum(x * x, 0, keepdims=True)
        refs[-1][:, 0:1] = loss_ref[...]
        refs[-1][:, 1:2] = jnp.sum(total, 1, keepdims=True)

    return pl.pallas_call(
        kernel,
        grid=(1,),
        in_specs=[whole((1, 1))] + [whole(p.shape) for p in pieces],
        out_specs=whole((1, 2)),
        out_shape=jax.ShapeDtypeStruct((1, 2), F32),
        compiler_params=params(8),
        cost_estimate=cost(10**6, 10**6),
        name="square_sum",
    )(loss, *pieces)


def fill_weights(step, where_ref, sources, targets, sem):
    shard, core = where_ref[0], where_ref[1]
    count = len(sources) - 2

    @pl.when(step == 0)
    def _():
        made = targets(sources[0], shard, None)
        for k in range(count):
            made += targets(sources[1 + k], shard ^ (k + 1), core)
            made += targets(sources[-1].at[k], shard ^ (k + 1), 1 - core)
        todo = [pltpu.make_async_copy(s, t, sem.at[n]) for n, (s, t) in enumerate(made)]
        for copy in todo:
            copy.start()
        for copy in todo:
            copy.wait()


def attn_targets(w_ref, rows):
    def targets(piece, at, half):
        if half is None:
            return [(piece.at[pl.ds(0, 4)], w_ref.at[:, pl.ds(pl.multiple_of(at * rows, rows), rows)])]
        start = pl.multiple_of(at * rows + half * (rows // 2), rows // 2)
        return [(piece.at[pl.ds(0, 4)], w_ref.at[:, pl.ds(start, rows // 2)])]

    return targets


def mlp_targets(up_ref, down_ref, rows):
    def targets(piece, at, half):
        few = rows if half is None else rows // 2
        skip = 0 if half is None else half * few
        start = pl.multiple_of(at * rows + skip, few)
        skip = pl.multiple_of(skip, few) if half is not None else 0
        return [
            (piece.at[pl.ds(0, 4)], up_ref.at[:, pl.ds(start, few)]),
            (piece.at[pl.ds(4, 4)], down_ref.at[pl.ds(at * 4, 4), pl.ds(skip, few)]),
        ]

    return targets


def pack(place, where, index, tall, wide, small):
    rows = D // place.shards
    half = rows // 2
    wide = [x.reshape(L, 4, rows, W) for x in wide]
    total = sum(x.shape[2] // W for x in tall) + 4 * len(wide) + bool(small)
    count = len(tall) + len(wide)

    def kernel(where_ref, *refs):
        full_ref, mine_ref = refs[count + len(small) : count + len(small) + 2]

        def run(core):
            own = slice(core * half, core * half + half)
            at = 0
            for ref in refs[: len(tall)]:
                for b in range(ref.shape[1] // W):
                    block = ref[:, W * b : W * b + W].astype(BF16)
                    full_ref[at] = block
                    mine_ref[at] = block[own]
                    at += 1
            for ref in refs[len(tall) : count]:
                for b in range(4):
                    block = ref[b].astype(BF16)
                    full_ref[at] = block
                    mine_ref[at] = block[own]
                    at += 1
            if small:
                table_ref = refs[-1]
                start = 0
                for ref in refs[count : count + len(small)]:
                    table_ref[start : start + ref.shape[0]] = ref[...]
                    start += ref.shape[0]
                table_ref[start:] = jnp.zeros((SMALL - start, rows), F32)
                norms = refs[count + 1][...]
                left = norms - norms.astype(BF16).astype(F32)
                table_ref[NORMS_LOW : NORMS_LOW + norms.shape[0]] = left
                for h in range(2):
                    for q in range(W // rows):
                        first = h * (SMALL // 2) + q * half
                        value = table_ref[first : first + half, :].astype(BF16)
                        spot = slice(q * rows, q * rows + rows)
                        full_ref[at, h * half : h * half + half, spot] = value
                        if h == core:
                            mine_ref[at, :, spot] = value

        for core in range(2):

            @pl.when(where_ref[1] == core)
            def _(core=core):
                run(core)

    return pl.pallas_call(
        kernel,
        grid=(1,),
        in_specs=[SMEM]
        + [pl.BlockSpec((None, rows, x.shape[2]), lambda i: (index, 0, 0)) for x in tall]
        + [pl.BlockSpec((None, 4, rows, W), lambda i: (index, 0, 0, 0)) for x in wide]
        + [whole(x.shape) for x in small],
        out_specs=[whole((total, rows, W)), whole((total, half, W))],
        out_shape=[
            pltpu.HBM((total, rows, W), BF16),
            pltpu.HBM((total, half, W), BF16),
        ],
        scratch_shapes=[pltpu.VMEM((SMALL, rows), F32)] * bool(small),
        compiler_params=params(),
        cost_estimate=cost(total * rows * W, total * rows * W * 7),
        name="pack",
    )(where, *map(in_hbm, tall), *map(in_hbm, wide), *map(in_hbm, small))


def embed_step(place, where, target, maskf, group):
    shards = place.shards
    rows = D // shards
    half = rows // 2
    n = target.shape[0]
    sources = len(group)

    def kernel(where_ref, target_ref, mask_ref, *refs):
        pieces, refs = refs[:sources], refs[sources:]
        x_ref, inputs_ref, head_ref, norm_ref, got_ref, table_ref, sem = refs

        def targets(piece, at, part):
            start = 0 if part is None else pl.multiple_of(part * half, half)
            few = rows if part is None else half
            return [(piece.at[4], got_ref.at[at, pl.ds(start, few)])]

        fill_weights(0, where_ref, pieces, targets, sem)
        for j in range(shards):
            for h in range(2):
                for q in range(W // rows):
                    spot = slice(q * rows, q * rows + rows)
                    part = slice(h * half, h * half + half)
                    value = got_ref[j, part, spot].astype(F32)
                    first = h * (SMALL // 2) + q * half
                    table_ref[first : first + half, j * rows : j * rows + rows] = value
        inputs = jnp.where(mask_ref[...] > 0, 0.0, target_ref[...].astype(F32)).astype(BF16)
        inputs_ref[...] = inputs
        embed = table_ref[:P_SIZE].astype(BF16)
        for s in range(n // LEN):
            part = slice(s * LEN, s * LEN + LEN)
            x_ref[part] = dense(inputs[part], embed) + table_ref[2 * P_SIZE : 2 * P_SIZE + LEN]
        head_ref[...] = table_ref[P_SIZE : 2 * P_SIZE].astype(BF16)
        low = table_ref[NORMS_LOW : NORMS_LOW + 16]
        norm_ref[...] = table_ref[NORMS_LOW - 16 : NORMS_LOW] + low

    return pl.pallas_call(
        kernel,
        grid=(1,),
        in_specs=[SMEM, whole((n, P_SIZE)), whole((n, 1))] + [ANY] * sources,
        out_specs=[whole((n, D)), whole((n, P_SIZE)), whole((P_SIZE, D)), whole((16, D))],
        out_shape=[
            jax.ShapeDtypeStruct((n, D), F32),
            jax.ShapeDtypeStruct((n, P_SIZE), BF16),
            jax.ShapeDtypeStruct((P_SIZE, D), BF16),
            jax.ShapeDtypeStruct((16, D), F32),
        ],
        scratch_shapes=[
            pltpu.VMEM((shards, rows, W), BF16),
            pltpu.VMEM((SMALL, D), F32),
            pltpu.SemaphoreType.DMA((copies_of(group),)),
        ],
        compiler_params=params(),
        cost_estimate=cost(2 * n * D * P_SIZE, n * D * 5),
        name="embed_step",
    )(where, target, maskf, *group)


def copies_of(group):
    return 2 * (2 * (len(group) - 2) + 1)


def norm_parts(x):
    center = x - jnp.mean(x, -1, keepdims=True)
    rstd = lax.rsqrt(jnp.mean(center * center, -1, keepdims=True) + EPS)
    return center * rstd, rstd


def norm_back(xhat, rstd, dy, gain):
    dxh = dy * gain
    return rstd * (
        dxh - jnp.mean(dxh, -1, keepdims=True) - xhat * jnp.mean(dxh * xhat, -1, keepdims=True)
    )


def head_lanes(x, h):
    lane = lax.broadcasted_iota(jnp.int32, (x.shape[0], 128), 1)
    own = (lane < DH) if h % 2 == 0 else (lane >= DH)
    return jnp.where(own, x[:, pair_of(h)], 0)


def pair_of(h):
    return slice(128 * (h // 2), 128 * (h // 2) + 128)


def head_of(h):
    return slice(DH * h, DH * h + DH)


SP = 1


def attn_fwd(place, where, x, norms, group):
    rows = D // place.shards
    n = x.shape[0]
    seqs = n // LEN
    sources = len(group)

    def kernel(where_ref, x_ref, norm_ref, *refs):
        pieces, refs = refs[:sources], refs[sources:]
        mid_ref, qkv_ref, pt_ref, ot_ref, w_ref, sem = refs
        fill_weights(pl.program_id(0), where_ref, pieces, attn_targets(w_ref, rows), sem)
        spans = [slice(LEN * s, LEN * s + LEN) for s in range(SP)]
        a, q, k, vt = [], [], [], []
        for s, span in enumerate(spans):
            xhat, _ = norm_parts(x_ref[span])
            a.append((xhat * norm_ref[0:1, :] + norm_ref[1:2, :]).astype(BF16))
            q.append((dense(a[s], w_ref[0]) * DH**-0.5).astype(BF16))
            k.append(dense(a[s], w_ref[1]).astype(BF16))
            qkv_ref[span, :D] = q[s]
            qkv_ref[span, D : 2 * D] = k[s]

        def scores(s, h):
            return dense_nt(k[s][:, pair_of(h)], head_lanes(q[s], h))

        def gather_values(s, h, p):
            ot_ref[s, head_of(h), :] = dense(vt[s][head_of(h), :], p).astype(BF16)

        items = [(s, h) for h in range(H) for s in range(SP)]
        ahead = scores(*items[0])
        for s, span in enumerate(spans):
            v = dense(a[s], w_ref[2]).astype(BF16)
            qkv_ref[span, 2 * D :] = v
            vt.append(v.T)
        last = None
        for at, (s, h) in enumerate(items):
            st = ahead
            if at + 1 < len(items):
                ahead = scores(*items[at + 1])
            if last is not None:
                gather_values(*last)
            e = jnp.exp(st - jnp.max(st, axis=0, keepdims=True))
            p = (e * (1.0 / jnp.sum(e, axis=0, keepdims=True))).astype(BF16)
            pt_ref[s, h] = p
            last = (s, h, p)
        gather_values(*last)
        for s, span in enumerate(spans):
            mid_ref[span] = x_ref[span] + dense_tn(ot_ref[s], w_ref[3])

    return pl.pallas_call(
        kernel,
        grid=(seqs // SP,),
        in_specs=[SMEM, pl.BlockSpec((SP * LEN, D), lambda i: (i, 0)), whole((4, D))]
        + [ANY] * sources,
        out_specs=[
            pl.BlockSpec((SP * LEN, D), lambda i: (i, 0)),
            pl.BlockSpec((SP * LEN, 3 * D), lambda i: (i, 0)),
            pl.BlockSpec((SP, H, LEN, LEN), lambda i: (i, 0, 0, 0)),
            pl.BlockSpec((SP, D, LEN), lambda i: (i, 0, 0)),
        ],
        out_shape=[
            pltpu.HBM((n, D), F32),
            pltpu.HBM((n, 3 * D), BF16),
            pltpu.HBM((seqs, H, LEN, LEN), BF16),
            pltpu.HBM((seqs, D, LEN), BF16),
        ],
        scratch_shapes=[
            pltpu.VMEM((4, D, W), BF16),
            pltpu.SemaphoreType.DMA((copies_of(group),)),
        ],
        compiler_params=params(),
        cost_estimate=cost(2 * n * D * (4 * D + 2 * LEN), n * D * 20, n * H * LEN),
        name="attn_fwd",
    )(where, x, norms, *group)


def gelu_pair(u):
    cdf = 0.5 * lax.erf(u * 0.7071067811865476) + 0.5
    density = jnp.exp(u * u * -0.5) * 0.3989422804014327
    return u * cdf, cdf + u * density


def mlp_fwd(place, where, mid, norms, group):
    rows = D // place.shards
    n = mid.shape[0]
    tall = LEN
    step = W // 2
    sources = len(group)
    per = W // rows

    def kernel(where_ref, mid_ref, norm_ref, *refs):
        pieces, refs = refs[:sources], refs[sources:]
        out_ref, act_ref, gp_ref, up_ref, down_ref, sem = refs
        fill_weights(pl.program_id(0), where_ref, pieces, mlp_targets(up_ref, down_ref, rows), sem)
        mid = mid_ref[...]
        xhat, _ = norm_parts(mid)
        c = (xhat * norm_ref[2:3, :] + norm_ref[3:4, :]).astype(BF16)
        total = mid

        def upper(b):
            cols = slice(step * (b % 2), step * (b % 2) + step)
            return dense(c, up_ref[b // 2, :, cols])

        def lower(act, b):
            few = per // 2
            return dense(act, down_ref[few * b : few * b + few].reshape(step, D))

        ahead = upper(0)
        for b in range(FF // step):
            cols = slice(step * b, step * b + step)
            u = ahead
            if b + 1 < FF // step:
                ahead = upper(b + 1)
            if b > 0:
                total = total + lower(last, b - 1)
            act, slope = gelu_pair(u)
            last = act.astype(BF16)
            act_ref[:, cols] = last
            gp_ref[:, cols] = slope.astype(BF16)
        out_ref[...] = total + lower(last, FF // step - 1)

    def row(width):
        return pl.BlockSpec((tall, width), lambda i: (i, 0))

    return pl.pallas_call(
        kernel,
        grid=(n // tall,),
        in_specs=[SMEM, row(D), whole((4, D))] + [ANY] * sources,
        out_specs=[row(D), row(FF), row(FF)],
        out_shape=[
            jax.ShapeDtypeStruct((n, D), F32),
            pltpu.HBM((n, FF), BF16),
            pltpu.HBM((n, FF), BF16),
        ],
        scratch_shapes=[
            pltpu.VMEM((4, D, W), BF16),
            pltpu.VMEM((FF // rows, rows, D), BF16),
            pltpu.SemaphoreType.DMA((copies_of(group),)),
        ],
        compiler_params=params(),
        cost_estimate=cost(4 * n * D * FF, n * D * 24, n * FF * 2),
        name="mlp_fwd",
    )(where, in_hbm(mid), norms, *group)


def mlp_bwd(place, where, dz, mid, gp, norms, group):
    rows = D // place.shards
    n = mid.shape[0]
    sources = len(group)
    per = W // rows

    def kernel(where_ref, dz_ref, mid_ref, gp_ref, norm_ref, *refs):
        pieces, refs = refs[:sources], refs[sources:]
        dmid_ref, dh_ref, du_ref, c_ref, dm_ref, dn_ref, up_ref, down_ref, sem = refs
        i = pl.program_id(0)
        fill_weights(i, where_ref, pieces, mlp_targets(up_ref, down_ref, rows), sem)
        dm = dz_ref[...].astype(BF16)
        dm_ref[...] = dm

        def upper(b):
            return dense_nt(dm, down_ref[per * b : per * b + per].reshape(W, D))

        dc = jnp.zeros((LEN, D), F32)
        ahead = upper(0)
        for b in range(FF // W):
            cols = slice(W * b, W * b + W)
            da = ahead
            if b + 1 < FF // W:
                ahead = upper(b + 1)
            if b > 0:
                dc = dc + dense_nt(last, up_ref[b - 1])
            last = (gp_ref[:, cols].astype(F32) * da).astype(BF16)
            du_ref[:, cols] = last
        dc = dc + dense_nt(last, up_ref[FF // W - 1])
        xhat, rstd = norm_parts(mid_ref[...])
        gain = norm_ref[2:3, :]
        c_ref[...] = (xhat * gain + norm_ref[3:4, :]).astype(BF16)
        dmid = dz_ref[...] + norm_back(xhat, rstd, dc, gain)
        dmid_ref[...] = dmid
        dh_ref[...] = dmid.astype(BF16)

        @pl.when(i == 0)
        def _():
            dn_ref[...] = jnp.zeros_like(dn_ref)

        dn_ref[0:1, :] += jnp.sum(dc * xhat, 0, keepdims=True)
        dn_ref[1:2, :] += jnp.sum(dc, 0, keepdims=True)

    def row(width):
        return pl.BlockSpec((LEN, width), lambda i: (i, 0))

    return pl.pallas_call(
        kernel,
        grid=(n // LEN,),
        in_specs=[SMEM, row(D), row(D), row(FF), whole((4, D))] + [ANY] * sources,
        out_specs=[row(D), row(D), row(FF), row(D), row(D), whole((8, D))],
        out_shape=[
            jax.ShapeDtypeStruct((n, D), F32),
            jax.ShapeDtypeStruct((n, D), BF16),
            pltpu.HBM((n, FF), BF16),
            jax.ShapeDtypeStruct((n, D), BF16),
            jax.ShapeDtypeStruct((n, D), BF16),
            jax.ShapeDtypeStruct((8, D), F32),
        ],
        scratch_shapes=[
            pltpu.VMEM((4, D, W), BF16),
            pltpu.VMEM((FF // rows, rows, D), BF16),
            pltpu.SemaphoreType.DMA((copies_of(group),)),
        ],
        compiler_params=params(),
        cost_estimate=cost(4 * n * D * FF, n * D * 32),
        name="mlp_bwd",
    )(where, dz, in_hbm(mid), in_hbm(gp), norms, *group)


def attn_bwd(place, where, dmid, dh, x, qkv, pt, ot, norms, group):
    rows = D // place.shards
    n = x.shape[0]
    seqs = n // LEN
    sources = len(group)

    def kernel(where_ref, dmid_ref, dh_ref, x_ref, qkv_ref, pt_ref, ot_ref, norm_ref, *refs):
        pieces, refs = refs[:sources], refs[sources:]
        dx_ref, dqkv_ref, a_ref, dn_ref, w_ref, dqt_ref, sem = refs
        i = pl.program_id(0)
        fill_weights(i, where_ref, pieces, attn_targets(w_ref, rows), sem)
        spans = [slice(None)]
        do, delta, kt = [], [], []
        for s, span in enumerate(spans):
            do.append(dense_nt(dh_ref[span], w_ref[3]).astype(BF16))
            along = do[s].T.astype(F32) * ot_ref[s].astype(F32)
            delta.append([jnp.sum(along[head_of(h), :], axis=0, keepdims=True) for h in range(H)])
            kt.append(qkv_ref[span, D : 2 * D].T)

        def first(s, h):
            doh = head_lanes(do[s], h)
            v = qkv_ref[spans[s], 2 * D + 128 * (h // 2) : 2 * D + 128 * (h // 2) + 128]
            return dense_nt(v, doh), dense(pt_ref[s, h], doh)

        halves = {}

        def second(s, h, dst, dv):
            q = qkv_ref[spans[s], pair_of(h)]
            lane = lax.broadcasted_iota(jnp.int32, (LEN, 128), 1)
            own = (lane < DH) if h % 2 == 0 else (lane >= DH)
            dk = dense(dst, jnp.where(own, q, 0))
            dqt_ref[s, head_of(h), :] = (dense(kt[s][head_of(h), :], dst) * DH**-0.5).astype(BF16)
            if h % 2 == 0:
                halves[s] = (dk, dv)
                return
            at = 128 * (h // 2)
            dk, dv = dk + halves[s][0], dv + halves[s][1]
            dqkv_ref[spans[s], D + at : D + at + 128] = dk.astype(BF16)
            dqkv_ref[spans[s], 2 * D + at : 2 * D + at + 128] = dv.astype(BF16)

        items = [(s, h) for h in range(H) for s in range(1)]
        ahead = first(*items[0])
        last = None
        for at, (s, h) in enumerate(items):
            dpt, dv = ahead
            if at + 1 < len(items):
                ahead = first(*items[at + 1])
            if last is not None:
                second(*last)
            dst = (pt_ref[s, h].astype(F32) * (dpt - delta[s][h])).astype(BF16)
            last = (s, h, dst, dv)
        second(*last)

        @pl.when(i == 0)
        def _():
            dn_ref[...] = jnp.zeros_like(dn_ref)

        gain = norm_ref[0:1, :]
        for s, span in enumerate(spans):
            da = dense_nt(dqkv_ref[span, D : 2 * D], w_ref[1])
            da = da + dense_nt(dqkv_ref[span, 2 * D :], w_ref[2])
            dq = dqt_ref[s].T
            dqkv_ref[span, :D] = dq
            da = da + dense_nt(dq, w_ref[0])
            xhat, rstd = norm_parts(x_ref[span])
            a_ref[span] = (xhat * gain + norm_ref[1:2, :]).astype(BF16)
            dx_ref[span] = dmid_ref[span] + norm_back(xhat, rstd, da, gain)
            dn_ref[0:1, :] += jnp.sum(da * xhat, 0, keepdims=True)
            dn_ref[1:2, :] += jnp.sum(da, 0, keepdims=True)

    def row(width):
        return pl.BlockSpec((LEN, width), lambda i: (i, 0))

    return pl.pallas_call(
        kernel,
        grid=(seqs,),
        in_specs=[
            SMEM,
            row(D),
            row(D),
            row(D),
            row(3 * D),
            pl.BlockSpec((1, H, LEN, LEN), lambda i: (i, 0, 0, 0)),
            pl.BlockSpec((1, D, LEN), lambda i: (i, 0, 0)),
            whole((4, D)),
        ]
        + [ANY] * sources,
        out_specs=[row(D), row(3 * D), row(D), whole((8, D))],
        out_shape=[
            jax.ShapeDtypeStruct((n, D), F32),
            jax.ShapeDtypeStruct((n, 3 * D), BF16),
            jax.ShapeDtypeStruct((n, D), BF16),
            jax.ShapeDtypeStruct((8, D), F32),
        ],
        scratch_shapes=[
            pltpu.VMEM((4, D, W), BF16),
            pltpu.VMEM((1, D, LEN), BF16),
            pltpu.SemaphoreType.DMA((copies_of(group),)),
        ],
        compiler_params=params(),
        cost_estimate=cost(2 * n * D * (4 * D + 5 * LEN), n * D * 32),
        name="attn_bwd",
    )(where, dmid, dh, x, in_hbm(qkv), in_hbm(pt), in_hbm(ot), norms, *group)


def head_step(place, x, target, maskf, head, norms, count):
    n = x.shape[0]

    def kernel(x_ref, target_ref, mask_ref, head_ref, norm_ref, dx_ref, loss_ref, gh_ref, dn_ref):
        i = pl.program_id(0)
        xhat, rstd = norm_parts(x_ref[...])
        gain = norm_ref[0:1, :]
        y = (xhat * gain + norm_ref[1:2, :]).astype(BF16)
        masked = mask_ref[...]
        err = (dense_nt(y, head_ref[...]) - target_ref[...].astype(F32)) * masked
        dpred = (err * (2.0 / (P_SIZE * count))).astype(BF16)
        dy = dense(dpred, head_ref[...])
        dx_ref[...] = norm_back(xhat, rstd, dy, gain)

        @pl.when(i == 0)
        def _():
            loss_ref[...] = jnp.zeros_like(loss_ref)
            gh_ref[...] = jnp.zeros_like(gh_ref)
            dn_ref[...] = jnp.zeros_like(dn_ref)

        loss_ref[...] += jnp.sum(err * err, 0, keepdims=True)
        gh_ref[...] += dense_tn(dpred, y)
        dn_ref[0:1, :] += jnp.sum(dy * xhat, 0, keepdims=True)
        dn_ref[1:2, :] += jnp.sum(dy, 0, keepdims=True)

    def row(width):
        return pl.BlockSpec((LEN, width), lambda i: (i, 0))

    return pl.pallas_call(
        kernel,
        grid=(n // LEN,),
        in_specs=[row(D), row(P_SIZE), row(1), whole((P_SIZE, D)), whole((2, D))],
        out_specs=[row(D), whole((1, P_SIZE)), whole((P_SIZE, D)), whole((8, D))],
        out_shape=[
            jax.ShapeDtypeStruct((n, D), F32),
            jax.ShapeDtypeStruct((1, P_SIZE), F32),
            jax.ShapeDtypeStruct((P_SIZE, D), F32),
            jax.ShapeDtypeStruct((8, D), F32),
        ],
        compiler_params=params(),
        cost_estimate=cost(6 * n * D * P_SIZE, n * D * 8),
        name="head_step",
    )(x, target, maskf, head, norms)


def put_block(core, block, lead, send_ref, keep_ref, at):
    rows = block.shape[0]
    halves = block.reshape(lead + (2, rows // (2 * lead_size(lead)), W))
    first, second = halves[..., 0, :, :], halves[..., 1, :, :]
    keep_ref[at] = jnp.where(core == 0, first, second)
    send_ref[at] = jnp.where(core == 0, second, first)


def lead_size(lead):
    size = 1
    for n in lead:
        size *= n
    return size


def grad_mlp(place, where, c, du, act, dm, ot, dh):
    shards = place.shards
    rows = D // shards
    n = c.shape[0]
    seqs = n // LEN
    wide = 2 * W
    steps = FF // wide
    per = shards // steps
    blocks = 9

    def kernel(where_ref, c_ref, du_ref, act_ref, dm_ref, ot_ref, dh_ref, send_ref, keep_ref, ct_ref):
        i = pl.program_id(0)
        core = where_ref[1]

        @pl.when(i == 0)
        def _():
            ct_ref[...] = c_ref[...].T

        @pl.when(i < steps)
        def _():
            block = dense(ct_ref[...], du_ref[...]).astype(BF16)
            for b in range(wide // W):
                at = (slice(None), i * (wide // W) + b)
                put_block(core, block[:, W * b : W * b + W], (shards,), send_ref, keep_ref, at)

        @pl.when((i >= steps) & (i < 2 * steps))
        def _():
            block = dense_tn(act_ref[...], dm_ref[...]).astype(BF16)
            at = (pl.ds((i - steps) * per, per), slice(4, 8))
            put_block(core, block, (per, 4), send_ref, keep_ref, at)

        @pl.when(i == 2 * steps)
        def _():
            total = dense(ot_ref[0], dh_ref[:LEN, :])
            for s in range(1, seqs):
                total = total + dense(ot_ref[s], dh_ref[LEN * s : LEN * s + LEN, :])
            put_block(core, total.astype(BF16), (shards,), send_ref, keep_ref, (slice(None), 8))

    shape = (shards, blocks, rows // 2, W)
    return pl.pallas_call(
        kernel,
        grid=(2 * steps + 1,),
        in_specs=[
            SMEM,
            whole((n, D)),
            pl.BlockSpec((n, wide), lambda i: (0, jnp.minimum(i, steps - 1))),
            pl.BlockSpec((n, wide), lambda i: (0, jnp.clip(i - steps, 0, steps - 1))),
            whole((n, D)),
            whole((seqs, D, LEN)),
            whole((n, D)),
        ],
        out_specs=[whole(shape), whole(shape)],
        scratch_shapes=[pltpu.VMEM((D, n), BF16)],
        out_shape=[jax.ShapeDtypeStruct(shape, BF16)] * 2,
        compiler_params=params(),
        cost_estimate=cost(4 * n * D * FF, n * (4 * D + 4 * FF) + 4 * D * FF),
        name="grad_mlp",
    )(where, c, in_hbm(du), in_hbm(act), dm, in_hbm(ot), dh)


def grad_qkv(place, where, a, dqkv, small=()):
    shards = place.shards
    rows = D // shards
    half = rows // 2
    n = a.shape[0]
    blocks = 3 + bool(small)
    extra = len(small)

    def kernel(where_ref, a_ref, dqkv_ref, *refs):
        small_refs, refs = refs[:extra], refs[extra:]
        send_ref, keep_ref, at_ref = refs[:3]
        i = pl.program_id(0)

        @pl.when(i == 0)
        def _():
            at_ref[...] = a_ref[...].T

        @pl.when(i < 3)
        def _():
            block = dense(at_ref[...], dqkv_ref[...]).astype(BF16)
            put_block(where_ref[1], block, (shards,), send_ref, keep_ref, (slice(None), i))

        if extra:
            table_ref = refs[3]
            inputs_ref, dx_ref, head_ref = small_refs[:3]

            @pl.when(i == 3)
            def _():
                dx = dx_ref[...]
                table_ref[:P_SIZE] = dense_tn(inputs_ref[...], dx.astype(BF16)).astype(BF16)
                table_ref[P_SIZE : 2 * P_SIZE] = head_ref[...].astype(BF16)
                total = dx[:LEN]
                for s in range(1, n // LEN):
                    total = total + dx[s * LEN : s * LEN + LEN]
                table_ref[2 * P_SIZE : 2 * P_SIZE + LEN] = total.astype(BF16)
                norms = jnp.concatenate(
                    [ref[0:2, :] for ref in small_refs[3:]]
                    + [jnp.zeros((16 - 2 * (extra - 3), D), F32)],
                    0,
                )
                start = 2 * P_SIZE + LEN
                table_ref[start : start + 16] = norms.astype(BF16)
                table_ref[start + 16 :] = jnp.zeros((SMALL - start - 16, D), BF16)
                for core in range(2):

                    @pl.when(where_ref[1] == core)
                    def _(core=core):
                        for h in range(2):
                            out_ref = keep_ref if h == core else send_ref
                            for j in range(shards):
                                for q in range(W // rows):
                                    first = h * (SMALL // 2) + q * half
                                    value = table_ref[first : first + half, j * rows : j * rows + rows]
                                    out_ref[j, 3, :, q * rows : q * rows + rows] = value

    shape = (shards, blocks, half, W)
    return pl.pallas_call(
        kernel,
        grid=(blocks,),
        in_specs=[SMEM, whole((n, D)), pl.BlockSpec((n, W), lambda i: (0, jnp.minimum(i, 2)))]
        + [whole(x.shape) for x in small],
        out_specs=[whole(shape), whole(shape)],
        scratch_shapes=[pltpu.VMEM((D, n), BF16)] + [pltpu.VMEM((SMALL, D), BF16)] * bool(small),
        out_shape=[jax.ShapeDtypeStruct(shape, BF16)] * 2,
        compiler_params=params(),
        cost_estimate=cost(6 * n * D * D, n * 8 * D + 6 * D * D),
        name="grad_qkv",
    )(where, a, dqkv, *small)


def adam(weight, first, second, grad, rate):
    first = BETA_ONE * first + (1 - BETA_ONE) * grad
    second = BETA_TWO * second + (1 - BETA_TWO) * grad * grad
    spread = second * (1 / (1 - BETA_TWO**STEP_COUNT))
    lower = 1.0 / (spread * lax.rsqrt(spread) + ADAM_EPS)
    weight = weight * (1 - rate * DECAY) - first * lower * (rate / (1 - BETA_ONE**STEP_COUNT))
    return (weight, first, second)


def fetch(arrays, where):
    def kernel(where_ref, *refs):
        sem = refs[-1]
        count = len(arrays)
        copies = [
            pltpu.make_async_copy(refs[n], refs[count + n], sem.at[n]) for n in range(count)
        ]
        for copy in copies:
            copy.start()
        for copy in copies:
            copy.wait()

    return pl.pallas_call(
        kernel,
        in_specs=[SMEM] + [pl.BlockSpec(memory_space=pltpu.HBM)] * len(arrays),
        out_specs=[pl.BlockSpec(memory_space=pltpu.VMEM)] * len(arrays),
        out_shape=[pltpu.VMEM(x.shape, x.dtype) for x in arrays],
        scratch_shapes=[pltpu.SemaphoreType.DMA((len(arrays),))],
        compiler_params=params(4),
        name="fetch",
    )(where, *map(in_hbm, arrays))


def adam_step(place, where, both, count, state, small, grads):
    rows = D // place.shards
    half = rows // 2
    few = half // 2
    flat = [x for group in state for x in group]
    tiny = [x for group in small for x in group]

    def spec(x):
        if x.ndim == 4:
            return pl.BlockSpec((None, 4, few, W), lambda i, h, q: (i, 0, 2 * h + q, 0))
        return pl.BlockSpec((None, few, x.shape[2]), lambda i, h, q: (i, 2 * h + q, 0))

    gflat, spots = [], []
    for layer in grads:
        spots.append([])
        for pieces, first, bit in layer:
            known = [n for n, x in enumerate(gflat) if x is pieces[0]]
            spots[-1].append((known[0] if known else len(gflat), len(pieces), first, bit))
            gflat += [] if known else list(pieces)
    total = len(flat) + len(tiny)

    def kernel(where_ref, *refs):
        both_refs, refs = refs[: len(both)], refs[len(both) :]
        grad_refs, refs = refs[: len(gflat)], refs[len(gflat) :]
        ins, outs, table_ref = refs[:total], refs[total : 2 * total], refs[-1]
        loss_ref, norm_ref = refs[2 * total : 2 * total + 2]
        layer, h, q = pl.program_id(0), pl.program_id(1), pl.program_id(2)
        values = [ref[...] for ref in both_refs]
        sums = jnp.zeros((1, 2), F32)
        for j in range(len(values)):
            sums = sums + select_of(values, where_ref[0] ^ j)
        norm = jnp.sqrt(sums[:, 1:2])
        loss_ref[...] = sums[:, 0:1] / count
        norm_ref[...] = norm
        scale = CLIP / jnp.maximum(norm, CLIP)
        own = where_ref[1] == h

        def update(n, at, grad, rate):
            got = adam(ins[3 * n][at], ins[3 * n + 1][at], ins[3 * n + 2][at], grad, rate)
            for k in range(3):
                outs[3 * n + k][at] = got[k]

        part = pl.ds(pl.multiple_of(q * few, few), few)

        def run(layer):
            def grad(group, b):
                base, count, first, bit = spots[layer][group]
                refs = grad_refs[base : base + count]
                if count == 2:
                    got = jnp.where(own, refs[0][first + b, part], refs[1][first + b, part])
                else:
                    close = jnp.where(own, refs[0][first + b], refs[1][first + b])
                    away = jnp.where(own, refs[2][first + b], refs[3][first + b])
                    got = jnp.where(where_ref[bit] == q, close, away)
                return got.astype(F32) * scale

            for b in range(3):
                update(0, (slice(None), slice(W * b, W * b + W)), grad(0, b), RATE)
            update(1, (slice(None), slice(None)), grad(1, 8), RATE)
            for b in range(4):
                update(2, (slice(None), slice(W * b, W * b + W)), grad(1, b), RATE)
                update(3, (b,), grad(1, 4 + b), RATE)

        for i in range(L):

            @pl.when(layer == i)
            def _(i=i):
                run(i)

        @pl.when((layer == 0) & (h == 0) & (q == 0))
        def _():
            base, _, at, _ = spots[0][0]
            mine, other = grad_refs[base][at + 3], grad_refs[base + 1][at + 3]
            first = where_ref[1] == 0
            for n, block in enumerate((jnp.where(first, mine, other), jnp.where(first, other, mine))):
                for k in range(W // rows):
                    start = n * (SMALL // 2) + k * half
                    table_ref[start : start + half] = (
                        block[:, k * rows : k * rows + rows].astype(F32) * scale
                    )
            count = 2 * P_SIZE + LEN
            update(4, (slice(None), slice(None)), table_ref[:count], TABLE_RATE)
            norms = small[1][0].shape[0]
            update(5, (slice(None), slice(None)), table_ref[count : count + norms], TABLE_RATE)

    out = pl.pallas_call(
        kernel,
        grid=(L, 2, 2),
        in_specs=[SMEM]
        + [whole((1, 2)) for _ in both]
        + [whole(g.shape) for g in gflat]
        + [spec(x) for x in flat]
        + [whole(x.shape) for x in tiny],
        out_specs=[spec(x) for x in flat] + [whole(x.shape) for x in tiny] + [whole((1, 1))] * 2,
        out_shape=[pltpu.HBM(x.shape, F32) for x in flat + tiny]
        + [jax.ShapeDtypeStruct((1, 1), F32)] * 2,
        scratch_shapes=[pltpu.VMEM((SMALL, rows), F32)],
        compiler_params=params(20),
        cost_estimate=cost(20 * L * 12 * rows * W, 24 * L * 12 * rows * W),
        name="adam_step",
    )(where, *both, *gflat, *flat, *map(in_hbm, tiny))
    news = [tuple(out[3 * n : 3 * n + 3]) for n in range(len(state) + len(small))]
    return out[-2].reshape(()), out[-1].reshape(()), news


def on_device(
    series,
    mask,
    qkv_w,
    out_w,
    up_w,
    down_w,
    patch_maps,
    norm_params,
    qkv_m,
    out_m,
    up_m,
    down_m,
    patch_m,
    norm_m,
    qkv_v,
    out_v,
    up_v,
    down_v,
    patch_v,
    norm_v,
):
    place = Place()
    shards = place.shards
    rows = D // shards
    half = rows // 2
    seqs = series.shape[0]
    count = MASKED * seqs * shards * place.replicas
    shard_bits = [(place.shard >> bit) & 1 for bit in bits_of(shards)]
    chip_bits = [(place.chip >> bit) & 1 for bit in bits_of(place.chips)]
    where = jnp.stack([place.shard, place.core] + shard_bits + chip_bits).astype(jnp.int32)
    chip = 2 + len(shard_bits)

    small_now = [patch_maps, norm_params]
    packs = [
        (
            pack(place, where, i, [qkv_w, out_w], [], small_now if i == 0 else []),
            pack(place, where, i, [up_w], [down_w], []),
        )
        for i in range(L)
    ]

    def group_of(packed, ours, theirs):
        return [packed[0]] + ours + [theirs]

    attn_groups = [None] * L
    mlp_groups = [None] * L
    target = series.reshape(seqs * LEN, P_SIZE)
    maskf = mask.reshape(seqs * LEN, 1).astype(F32)
    ours = gather_shards(place, packs[0][0][1])
    theirs = gather_cores(place, ours, *[p[1] for pair in packs for p in pair], target, maskf)
    attn_groups[0] = group_of(packs[0][0], ours, theirs)
    mine = gate(packs[0][1][1], *ours)
    ours_mlp = gather_shards(place, mine)

    x, inputs, head, norms_all = embed_step(place, where, target, gate(maskf, mine), attn_groups[0])
    saved = []
    for index in range(L):
        norms = norms_all[4 * index : 4 * index + 4]
        mid, qkv, pt, ot = attn_fwd(place, where, x, norms, attn_groups[index])
        held = mid
        if index + 1 < L:
            got = gates(ours_mlp, mid)
            mine = gate(packs[index + 1][0][1], *got)
            ours_attn = gather_shards(place, mine)
            held = gate(mid, mine)
        theirs = gather_cores(place, ours_mlp, mid)
        mlp_groups[index] = group_of(packs[index][1], ours_mlp, theirs)
        pieces = mlp_groups[index] if index == 0 else [in_hbm(x) for x in mlp_groups[index]]
        y, act, gp = mlp_fwd(place, where, held, norms, pieces)
        if index + 1 < L:
            got = gates(ours_attn, y)
            theirs = gather_cores(place, got)
            attn_groups[index + 1] = group_of(packs[index + 1][0], ours_attn, theirs)
            mine = gate(packs[index + 1][1][1], *got)
            ours_mlp = gather_shards(place, mine)
            y = gate(y, mine)
        saved.append((x, mid, qkv, pt, ot, act, gp, norms))
        x = y

    grad, loss, g_head, dn_final = head_step(
        place, x, target, maskf, head, norms_all[4 * L : 4 * L + 2], count
    )
    loss = (jnp.sum(loss) / P_SIZE).reshape(1, 1)

    norm_grads = {}

    def backward_mlp(index, grad):
        x, mid, qkv, pt, ot, act, gp, norms = saved[index]
        dmid, dh, du, c, dm, dn = mlp_bwd(
            place, where, grad, mid, gp, norms, mlp_groups[index]
        )
        norm_grads[index, 1] = dn
        return dmid, dh, du, c, dm

    def backward_attn(index, dmid, dh):
        x, mid, qkv, pt, ot, act, gp, norms = saved[index]
        grad, dqkv, a, dn = attn_bwd(
            place, where, dmid, dh, x, qkv, pt, ot, norms, attn_groups[index]
        )
        norm_grads[index, 0] = dn
        return grad, dqkv, a

    def grads_mlp(index, du, c, dm, dh):
        return grad_mlp(place, where, c, du, saved[index][5], dm, saved[index][4], dh)

    one, two = Flow(place, True, True), Flow(place, True)
    ahead, end = Flow(place, False), Flow(place, False)

    def advance(flows, *after):
        token = sum_round(where, flows, *after)
        for flow in flows:
            flow.launch()
        return token

    loss = loss + place.to_core(loss)
    dmid, dh, du, c, dm = backward_mlp(1, grad)
    token = one.begin(*grads_mlp(1, du, c, dm, dh), (0, 4, 0), (4, 5, 1))
    grad, dqkv_one, a_one = backward_attn(1, gate(dmid, token), dh)
    token = advance([one], grad)
    dmid, dh, du, c, dm = backward_mlp(0, gate(grad, token))
    token = advance([one], dmid)
    token = two.begin(*grads_mlp(0, du, gate(c, token), dm, dh), (0, 4, 0), (4, 5, 1))
    token = advance([one], token)
    token = ahead.begin(*grad_qkv(place, where, gate(a_one, token), dqkv_one), (0, 3, 0))
    token = advance([two], token)
    grad, dqkv, a = backward_attn(0, gate(dmid, token), dh)
    token = sum_round(where, [one, two, ahead], grad)
    small = [inputs, grad, g_head]
    small += [norm_grads[i, k] for i in range(L) for k in range(2)] + [dn_final]
    token = end.begin(*grad_qkv(place, where, gate(a, token), dqkv, small), (0, 4, 1))
    one.launch()
    two.launch()
    ahead.launch()
    while not one.last():
        token = advance([one], token)
    token = sum_round(where, [one, two, end], token)
    end.launch()
    end.join(ahead)
    two.launch()
    one.to_neighbours()
    hops = bits_of(place.chips)

    def pass_loss(loss, token):
        if not hops:
            return loss
        return loss + place.to_chip(gate(loss, token), 1 << hops.pop(0))

    while end.step < end.steps - 2:
        loss = pass_loss(loss, token)
        token = sum_round(where, [end] + ([two] if not two.last() else []), token, loss)
        end.launch()
        if two.step == two.steps - 1:
            break
        if not two.last():
            two.launch()
    behind = not two.last()
    while end.step < end.steps - 1:
        loss = pass_loss(loss, token)
        token = advance([end], token, *one.pieces, loss)
    one.to_last()
    if behind:
        two.launch()
    while hops:
        loss = pass_loss(loss, token)
    state = [(qkv_w, qkv_m, qkv_v), (out_w, out_m, out_v), (up_w, up_m, up_v)]
    state.append(tuple(x.reshape(L, 4, rows, W) for x in (down_w, down_m, down_v)))
    token = sum_round(where, [end, two], token, loss)
    end.launch()
    two.to_neighbours()
    near = fetch([x for group in state for x in group], gate(where, token))
    state = [tuple(near[3 * n : 3 * n + 3]) for n in range(len(state))]
    token = sum_round(where, [end], token, *two.pieces, near[0])
    end.to_neighbours()
    two.to_last()
    grads = [
        [(end.pieces, 3, 0), (two.pieces, 0, chip + two.chip_bits[0])],
        [(end.pieces, 0, 0), (one.pieces, 0, chip + one.chip_bits[0])],
    ]
    done_one, done_two, done_last = one.pieces, two.pieces, end.pieces

    both = square_sum(done_one + done_two + done_last, loss)
    both = [both] + [place.to_shard(both, k) for k in range(1, shards)]

    small = [(patch_maps, patch_m, patch_v), (norm_params, norm_m, norm_v)]
    loss, grad_norm, results = adam_step(place, where, both, count, state, small, grads)
    results[3] = tuple(x.reshape(down_w.shape) for x in results[3])
    news = tuple(r[0] for r in results)
    new_m = tuple(r[1] for r in results)
    new_v = tuple(r[2] for r in results)
    return (loss, grad_norm) + news + new_m + new_v


def solution(mesh):
    batch = P(("shard", "replica"), None)
    stack = P(None, "shard", None)
    flat = P(None, "shard")
    state = (stack, stack, stack, stack, flat, flat)
    return jax.shard_map(
        on_device,
        mesh=mesh,
        in_specs=(batch, batch) + state * 3,
        out_specs=(P(), P()) + state * 3,
        check_vma=False,
    )
```

```python
import jax
import jax.numpy as jnp
from jax import lax
from jax.experimental import pallas as pl
from jax.experimental.pallas import tpu as pltpu
from jax.sharding import PartitionSpec as P

D = 512
H = 8
DH = 64
FF = 2048
P_SIZE = 64
LEN = 256
L = 2
MASKED = 102

EPS = 1e-05
CLIP = 0.001
RATE = 0.05
TABLE_RATE = 0.3
BETA_ONE = 0.9
BETA_TWO = 0.999
ADAM_EPS = 1e-08
DECAY = 0.1
STEP_COUNT = 10

W = 512
SMALL = 512
NORMS_LOW = 2 * P_SIZE + LEN + 16
F32 = jnp.float32
BF16 = jnp.bfloat16


def dense(left, right):
    return jnp.dot(left, right, preferred_element_type=F32)


def dense_tn(left, right):
    return lax.dot_general(left, right, (((0,), (0,)), ((), ())), preferred_element_type=F32)


def dense_nt(left, right):
    return lax.dot_general(left, right, (((1,), (1,)), ((), ())), preferred_element_type=F32)


def layer_norm(x, gain, bias):
    center = x - jnp.mean(x, -1, keepdims=True)
    spread = jnp.mean(center * center, -1, keepdims=True)
    return center * lax.rsqrt(spread + EPS) * gain + bias


def params(mib=30):
    return pltpu.CompilerParams(vmem_limit_bytes=mib * 2**20)


def cost(flops, data, trans=0):
    return pl.CostEstimate(
        flops=int(30 * flops), bytes_accessed=int(30 * data), transcendentals=int(30 * trans)
    )


def whole(shape):
    return pl.BlockSpec(shape, lambda *_: (0,) * len(shape))


def in_hbm(x):
    return pltpu.with_memory_space_constraint(x, pltpu.HBM)


ANY = pl.BlockSpec(memory_space=pl.ANY)
SMEM = pl.BlockSpec(memory_space=pltpu.SMEM)


def permute(x, axis, mask, size):
    return lax.ppermute(x, axis, [(i, i ^ mask) for i in range(size)])


def pick(x, index):
    return lax.dynamic_index_in_dim(x, index, 0, keepdims=False)


class Place:
    def __init__(self):
        self.shards = lax.axis_size("shard")
        self.replicas = lax.axis_size("replica")
        self.chips = self.replicas // 2
        self.shard = lax.axis_index("shard")
        replica = lax.axis_index("replica")
        self.core = replica % 2
        self.chip = replica // 2

    def to_core(self, x):
        return permute(x, "replica", 1, self.replicas)

    def to_shard(self, x, mask):
        return permute(x, "shard", mask, self.shards)

    def to_chip(self, x, mask):
        return permute(x, "replica", 2 * mask, self.replicas)


def gate(x, *after):
    return lax.optimization_barrier((x,) + after)[0]


def gather_shards(place, mine):
    return [place.to_shard(mine, mask) for mask in range(1, place.shards)]


def gather_cores(place, ours, *after):
    items = gates(ours, *after)
    return place.to_core(stack(items) if items[0].shape[0] % 4 == 0 else jnp.stack(items))


def stack(items):
    def kernel(*refs):
        for n, ref in enumerate(refs[:-1]):
            refs[-1][n] = ref[...]

    few, rows, width = items[0].shape
    part = pl.BlockSpec((few // 2, rows, width), lambda i: (i, 0, 0))
    return pl.pallas_call(
        kernel,
        grid=(2,),
        in_specs=[part] * len(items),
        out_specs=pl.BlockSpec((len(items), few // 2, rows, width), lambda i: (0, i, 0, 0)),
        out_shape=jax.ShapeDtypeStruct((len(items), few, rows, width), items[0].dtype),
        compiler_params=params(12),
        cost_estimate=cost(10**5, 10**5),
        name="stack",
    )(*items)


def gates(items, *after):
    return list(lax.optimization_barrier(tuple(items) + after)[: len(items)])


def select_of(items, index):
    out = items[0]
    for k in range(1, len(items)):
        out = jnp.where(index == k, items[k], out)
    return out


def bits_of(size):
    return list(range(size.bit_length() - 1))


def total_of(values):
    total = values[0].astype(F32)
    for value in values[1:]:
        total = total + value.astype(F32)
    return total


def combine(where, jobs, name):
    lanes = W // 2
    arrays, leads, plans, shapes = [], [], [], []

    def number(array, lead):
        for n, known in enumerate(arrays):
            if known is array:
                return n
        arrays.append(array)
        leads.append(lead)
        return len(arrays) - 1

    for segments, lead, cut, bit in jobs:
        plans.append([[(number(a, lead), f, b) for a, f, b in parts] for parts in segments])
        blocks = sum(parts[0][2] for parts in segments)
        rows = segments[0][0][0].shape[-2]
        if cut is None:
            shapes.append(lead + (blocks, rows, W))
        elif cut == "rows":
            shapes += [lead + (blocks, rows // 2, W)] * 2
        else:
            shapes += [lead[:cut] + lead[cut + 1 :] + (blocks, rows, W)] * 2
    arrays = [a.reshape(lead + a.shape[-3:]) for a, lead in zip(arrays, leads)]

    def block(shape):
        zeros = (0,) * (len(shape) - 1)
        return pl.BlockSpec(shape[:-1] + (lanes,), lambda i: zeros + (i,))

    def kernel(where_ref, *refs):
        ins, outs = refs[: len(arrays)], list(refs[len(arrays) :])
        for (segments, lead, cut, bit), plan in zip(jobs, plans):
            some = (slice(None),) * len(lead)
            fewer = (slice(None),) * (len(lead) - (cut is not None and cut != "rows"))
            if cut is None:
                targets = [(outs.pop(0), None)]
            else:
                value = where_ref[bit]
                targets = [(outs.pop(0), 1 - value), (outs.pop(0), value)]
            for out_ref, at in targets:
                start = 0
                for parts in plan:
                    got = []
                    for n, f, b in parts:
                        index = some
                        if cut is not None and cut != "rows":
                            index = some[:cut] + (at,) + some[cut + 1 :]
                        index += (slice(f, f + b),)
                        if cut == "rows":
                            few = ins[n].shape[-2] // 2
                            index += (pl.ds(pl.multiple_of(at * few, few), few),)
                        got.append(ins[n][index])
                    out_ref[fewer + (slice(start, start + parts[0][2]),)] = total_of(got).astype(BF16)
                    start += parts[0][2]

    size = sum(a.size for a in arrays) * 4
    return pl.pallas_call(
        kernel,
        grid=(2,),
        in_specs=[SMEM] + [block(a.shape) for a in arrays],
        out_specs=[block(s) for s in shapes],
        out_shape=[jax.ShapeDtypeStruct(s, BF16) for s in shapes],
        compiler_params=params(12),
        cost_estimate=cost(size, size),
        name=name,
    )(where, *arrays)


class Flow:
    def __init__(self, place, spread, far_first=False):
        self.place, self.spread = place, spread
        self.chip_bits = bits_of(place.chips)[:: -1 if far_first else 1]
        self.bits = bits_of(place.shards)
        self.steps = len(self.bits) + len(bits_of(place.chips))
        self.step = 0
        self.inputs = []
        self.ranges = []

    def begin(self, send, keep, *ranges):
        other = self.place.to_core(send)
        for first, blocks, order in ranges:
            self.ranges.append((len(self.inputs), first, blocks, order))
        self.inputs += [keep, other]
        self.left = [list(reversed(self.bits)) for _ in self.ranges]
        return send

    def join(self, other):
        self.inputs = other.inputs + self.inputs
        self.ranges = other.ranges + self.ranges
        self.left = other.left + self.left

    def last(self):
        return self.step == self.steps

    def plan(self, flat):
        if self.step == 0:
            parts = [[(flat[n], f, b), (flat[n + 1], f, b)] for n, f, b, _ in self.ranges]
        else:
            parts = [
                [(x, 0, x.shape[-3]) for x in flat[2 * n : 2 * n + 2]]
                for n in range(len(flat) // 2)
            ]
        if self.step >= len(self.bits):
            cut = self.spread and self.step == len(self.bits)
            bit = 2 + len(self.bits) + self.chip_bits[0]
            return [(parts, (), "rows", bit) if cut else (parts, (), None, 0)]
        jobs, self.chosen = [], []
        for n, (_, _, _, order) in enumerate(self.ranges):
            bit = (self.bits if order == 0 else self.bits[::-1])[self.step]
            jobs.append(([parts[n]], (2,) * len(self.left[n]), self.left[n].index(bit), 2 + bit))
            self.left[n].remove(bit)
            self.chosen.append(bit)
        return jobs

    def take(self, out):
        if self.step < len(self.bits):
            self.sends, self.stays = out[0::2], out[1::2]
        else:
            self.sends, self.stays = out[:1], out[-1:]
        return self.sends[0]

    def launch(self):
        place = self.place
        if self.step < len(self.bits):
            got = [place.to_shard(x, 1 << bit) for x, bit in zip(self.sends, self.chosen)]
        else:
            bit = self.chip_bits[self.step - len(self.bits)]
            got = [place.to_chip(x, 1 << bit) for x in self.sends]
        self.inputs = [x for pair in zip(self.stays, got) for x in pair]
        self.step += 1

    def to_neighbours(self):
        self.pieces = [self.sends[0], self.place.to_core(self.sends[0])]
        if self.spread:
            self.pieces.append(self.place.to_chip(self.sends[0], 1 << self.chip_bits[0]))

    def to_last(self):
        if self.spread:
            self.pieces.append(self.place.to_core(self.pieces[2]))


def sum_round(where, flows, *after):
    flat = gates([x for flow in flows for x in flow.inputs], *after)
    jobs, counts = [], []
    for flow in flows:
        few = len(flow.inputs)
        some = flow.plan(flat[:few])
        flat = flat[few:]
        jobs += some
        counts.append(sum(1 if cut is None else 2 for _, _, cut, _ in some))
    out = combine(where, jobs, "sum_round")
    for flow, count in zip(flows, counts):
        token = flow.take(out[:count])
        out = out[count:]
    return token


def square_sum(pieces, loss):
    def kernel(loss_ref, *refs):
        total = jnp.zeros((1, W), F32)
        for ref in refs[:-1]:
            for b in range(ref.shape[0]):
                x = ref[b].astype(F32)
                total = total + jnp.sum(x * x, 0, keepdims=True)
        refs[-1][:, 0:1] = loss_ref[...]
        refs[-1][:, 1:2] = jnp.sum(total, 1, keepdims=True)

    return pl.pallas_call(
        kernel,
        grid=(1,),
        in_specs=[whole((1, 1))] + [whole(p.shape) for p in pieces],
        out_specs=whole((1, 2)),
        out_shape=jax.ShapeDtypeStruct((1, 2), F32),
        compiler_params=params(8),
        cost_estimate=cost(10**6, 10**6),
        name="square_sum",
    )(loss, *pieces)


def fill_weights(step, where_ref, sources, targets, sem):
    shard, core = where_ref[0], where_ref[1]
    count = len(sources) - 2

    @pl.when(step == 0)
    def _():
        made = targets(sources[0], shard, None)
        for k in range(count):
            made += targets(sources[1 + k], shard ^ (k + 1), core)
            made += targets(sources[-1].at[k], shard ^ (k + 1), 1 - core)
        todo = [pltpu.make_async_copy(s, t, sem.at[n]) for n, (s, t) in enumerate(made)]
        for copy in todo:
            copy.start()
        for copy in todo:
            copy.wait()


def attn_targets(w_ref, rows):
    def targets(piece, at, half):
        if half is None:
            return [(piece.at[pl.ds(0, 4)], w_ref.at[:, pl.ds(pl.multiple_of(at * rows, rows), rows)])]
        start = pl.multiple_of(at * rows + half * (rows // 2), rows // 2)
        return [(piece.at[pl.ds(0, 4)], w_ref.at[:, pl.ds(start, rows // 2)])]

    return targets


def mlp_targets(up_ref, down_ref, rows):
    def targets(piece, at, half):
        few = rows if half is None else rows // 2
        skip = 0 if half is None else half * few
        start = pl.multiple_of(at * rows + skip, few)
        skip = pl.multiple_of(skip, few) if half is not None else 0
        return [
            (piece.at[pl.ds(0, 4)], up_ref.at[:, pl.ds(start, few)]),
            (piece.at[pl.ds(4, 4)], down_ref.at[pl.ds(at * 4, 4), pl.ds(skip, few)]),
        ]

    return targets


def pack(place, where, index, tall, wide, small):
    rows = D // place.shards
    half = rows // 2
    wide = [x.reshape(L, 4, rows, W) for x in wide]
    total = sum(x.shape[2] // W for x in tall) + 4 * len(wide) + bool(small)
    count = len(tall) + len(wide)

    def kernel(where_ref, *refs):
        full_ref, mine_ref = refs[count + len(small) : count + len(small) + 2]

        def run(core):
            own = slice(core * half, core * half + half)
            at = 0
            for ref in refs[: len(tall)]:
                for b in range(ref.shape[1] // W):
                    block = ref[:, W * b : W * b + W].astype(BF16)
                    full_ref[at] = block
                    mine_ref[at] = block[own]
                    at += 1
            for ref in refs[len(tall) : count]:
                for b in range(4):
                    block = ref[b].astype(BF16)
                    full_ref[at] = block
                    mine_ref[at] = block[own]
                    at += 1
            if small:
                table_ref = refs[-1]
                start = 0
                for ref in refs[count : count + len(small)]:
                    table_ref[start : start + ref.shape[0]] = ref[...]
                    start += ref.shape[0]
                table_ref[start:] = jnp.zeros((SMALL - start, rows), F32)
                norms = refs[count + 1][...]
                left = norms - norms.astype(BF16).astype(F32)
                table_ref[NORMS_LOW : NORMS_LOW + norms.shape[0]] = left
                for h in range(2):
                    for q in range(W // rows):
                        first = h * (SMALL // 2) + q * half
                        value = table_ref[first : first + half, :].astype(BF16)
                        spot = slice(q * rows, q * rows + rows)
                        full_ref[at, h * half : h * half + half, spot] = value
                        if h == core:
                            mine_ref[at, :, spot] = value

        for core in range(2):

            @pl.when(where_ref[1] == core)
            def _(core=core):
                run(core)

    return pl.pallas_call(
        kernel,
        grid=(1,),
        in_specs=[SMEM]
        + [pl.BlockSpec((None, rows, x.shape[2]), lambda i: (index, 0, 0)) for x in tall]
        + [pl.BlockSpec((None, 4, rows, W), lambda i: (index, 0, 0, 0)) for x in wide]
        + [whole(x.shape) for x in small],
        out_specs=[whole((total, rows, W)), whole((total, half, W))],
        out_shape=[
            pltpu.HBM((total, rows, W), BF16),
            pltpu.HBM((total, half, W), BF16),
        ],
        scratch_shapes=[pltpu.VMEM((SMALL, rows), F32)] * bool(small),
        compiler_params=params(),
        cost_estimate=cost(total * rows * W, total * rows * W * 7),
        name="pack",
    )(where, *map(in_hbm, tall), *map(in_hbm, wide), *map(in_hbm, small))


def embed_step(place, where, target, maskf, group):
    shards = place.shards
    rows = D // shards
    half = rows // 2
    n = target.shape[0]
    sources = len(group)

    def kernel(where_ref, target_ref, mask_ref, *refs):
        pieces, refs = refs[:sources], refs[sources:]
        x_ref, inputs_ref, head_ref, norm_ref, got_ref, table_ref, sem = refs

        def targets(piece, at, part):
            start = 0 if part is None else pl.multiple_of(part * half, half)
            few = rows if part is None else half
            return [(piece.at[4], got_ref.at[at, pl.ds(start, few)])]

        fill_weights(0, where_ref, pieces, targets, sem)
        for j in range(shards):
            for h in range(2):
                for q in range(W // rows):
                    spot = slice(q * rows, q * rows + rows)
                    part = slice(h * half, h * half + half)
                    value = got_ref[j, part, spot].astype(F32)
                    first = h * (SMALL // 2) + q * half
                    table_ref[first : first + half, j * rows : j * rows + rows] = value
        inputs = jnp.where(mask_ref[...] > 0, 0.0, target_ref[...].astype(F32)).astype(BF16)
        inputs_ref[...] = inputs
        embed = table_ref[:P_SIZE].astype(BF16)
        for s in range(n // LEN):
            part = slice(s * LEN, s * LEN + LEN)
            x_ref[part] = dense(inputs[part], embed) + table_ref[2 * P_SIZE : 2 * P_SIZE + LEN]
        head_ref[...] = table_ref[P_SIZE : 2 * P_SIZE].astype(BF16)
        low = table_ref[NORMS_LOW : NORMS_LOW + 16]
        norm_ref[...] = table_ref[NORMS_LOW - 16 : NORMS_LOW] + low

    return pl.pallas_call(
        kernel,
        grid=(1,),
        in_specs=[SMEM, whole((n, P_SIZE)), whole((n, 1))] + [ANY] * sources,
        out_specs=[whole((n, D)), whole((n, P_SIZE)), whole((P_SIZE, D)), whole((16, D))],
        out_shape=[
            pltpu.HBM((n, D), F32),
            jax.ShapeDtypeStruct((n, P_SIZE), BF16),
            jax.ShapeDtypeStruct((P_SIZE, D), BF16),
            jax.ShapeDtypeStruct((16, D), F32),
        ],
        scratch_shapes=[
            pltpu.VMEM((shards, rows, W), BF16),
            pltpu.VMEM((SMALL, D), F32),
            pltpu.SemaphoreType.DMA((copies_of(group),)),
        ],
        compiler_params=params(),
        cost_estimate=cost(2 * n * D * P_SIZE, n * D * 5),
        name="embed_step",
    )(where, target, maskf, in_hbm(group[0]), *group[1:])


def copies_of(group):
    return 2 * (2 * (len(group) - 2) + 1)


def norm_parts(x):
    center = x - jnp.mean(x, -1, keepdims=True)
    rstd = lax.rsqrt(jnp.mean(center * center, -1, keepdims=True) + EPS)
    return center * rstd, rstd


def norm_back(xhat, rstd, dy, gain):
    dxh = dy * gain
    return rstd * (
        dxh - jnp.mean(dxh, -1, keepdims=True) - xhat * jnp.mean(dxh * xhat, -1, keepdims=True)
    )


def head_lanes(x, h):
    lane = lax.broadcasted_iota(jnp.int32, (x.shape[0], 128), 1)
    own = (lane < DH) if h % 2 == 0 else (lane >= DH)
    return jnp.where(own, x[:, pair_of(h)], 0)


def pair_of(h):
    return slice(128 * (h // 2), 128 * (h // 2) + 128)


def head_of(h):
    return slice(DH * h, DH * h + DH)


SP = 1


def attn_fwd(place, where, x, norms, group):
    rows = D // place.shards
    n = x.shape[0]
    seqs = n // LEN
    sources = len(group)

    def kernel(where_ref, x_ref, norm_ref, *refs):
        pieces, refs = refs[:sources], refs[sources:]
        mid_ref, qkv_ref, pt_ref, ot_ref, w_ref, sem = refs
        fill_weights(pl.program_id(0), where_ref, pieces, attn_targets(w_ref, rows), sem)
        spans = [slice(LEN * s, LEN * s + LEN) for s in range(SP)]
        a, q, k, vt = [], [], [], []
        for s, span in enumerate(spans):
            xhat, _ = norm_parts(x_ref[span])
            a.append((xhat * norm_ref[0:1, :] + norm_ref[1:2, :]).astype(BF16))
            q.append((dense(a[s], w_ref[0]) * DH**-0.5).astype(BF16))
            k.append(dense(a[s], w_ref[1]).astype(BF16))
            qkv_ref[span, :D] = q[s]
            qkv_ref[span, D : 2 * D] = k[s]

        def scores(s, h):
            return dense_nt(k[s][:, pair_of(h)], head_lanes(q[s], h))

        def gather_values(s, h, p):
            ot_ref[s, head_of(h), :] = dense(vt[s][head_of(h), :], p).astype(BF16)

        items = [(s, h) for h in range(H) for s in range(SP)]
        ahead = scores(*items[0])
        for s, span in enumerate(spans):
            v = dense(a[s], w_ref[2]).astype(BF16)
            qkv_ref[span, 2 * D :] = v
            vt.append(v.T)
        last = None
        for at, (s, h) in enumerate(items):
            st = ahead
            if at + 1 < len(items):
                ahead = scores(*items[at + 1])
            if last is not None:
                gather_values(*last)
            e = jnp.exp(st - jnp.max(st, axis=0, keepdims=True))
            p = (e * (1.0 / jnp.sum(e, axis=0, keepdims=True))).astype(BF16)
            pt_ref[s, h] = p
            last = (s, h, p)
        gather_values(*last)
        for s, span in enumerate(spans):
            mid_ref[span] = x_ref[span] + dense_tn(ot_ref[s], w_ref[3])

    return pl.pallas_call(
        kernel,
        grid=(seqs // SP,),
        in_specs=[SMEM, pl.BlockSpec((SP * LEN, D), lambda i: (i, 0)), whole((4, D))]
        + [ANY] * sources,
        out_specs=[
            pl.BlockSpec((SP * LEN, D), lambda i: (i, 0)),
            pl.BlockSpec((SP * LEN, 3 * D), lambda i: (i, 0)),
            pl.BlockSpec((SP, H, LEN, LEN), lambda i: (i, 0, 0, 0)),
            pl.BlockSpec((SP, D, LEN), lambda i: (i, 0, 0)),
        ],
        out_shape=[
            pltpu.HBM((n, D), F32),
            pltpu.HBM((n, 3 * D), BF16),
            pltpu.HBM((seqs, H, LEN, LEN), BF16),
            pltpu.HBM((seqs, D, LEN), BF16),
        ],
        scratch_shapes=[
            pltpu.VMEM((4, D, W), BF16),
            pltpu.SemaphoreType.DMA((copies_of(group),)),
        ],
        compiler_params=params(),
        cost_estimate=cost(2 * n * D * (4 * D + 2 * LEN), n * D * 20, n * H * LEN),
        name="attn_fwd",
    )(where, x, norms, in_hbm(group[0]), *group[1:])


def gelu_pair(u):
    cdf = 0.5 * lax.erf(u * 0.7071067811865476) + 0.5
    density = jnp.exp(u * u * -0.5) * 0.3989422804014327
    return u * cdf, cdf + u * density


def mlp_fwd(place, where, mid, norms, group):
    rows = D // place.shards
    n = mid.shape[0]
    tall = LEN
    step = W // 2
    sources = len(group)
    per = W // rows

    def kernel(where_ref, mid_ref, norm_ref, *refs):
        pieces, refs = refs[:sources], refs[sources:]
        out_ref, act_ref, gp_ref, up_ref, down_ref, sem = refs
        fill_weights(pl.program_id(0), where_ref, pieces, mlp_targets(up_ref, down_ref, rows), sem)
        mid = mid_ref[...]
        xhat, _ = norm_parts(mid)
        c = (xhat * norm_ref[2:3, :] + norm_ref[3:4, :]).astype(BF16)
        total = mid

        def upper(b):
            cols = slice(step * (b % 2), step * (b % 2) + step)
            return dense(c, up_ref[b // 2, :, cols])

        def lower(act, b):
            few = per // 2
            return dense(act, down_ref[few * b : few * b + few].reshape(step, D))

        ahead = upper(0)
        for b in range(FF // step):
            cols = slice(step * b, step * b + step)
            u = ahead
            if b + 1 < FF // step:
                ahead = upper(b + 1)
            if b > 0:
                total = total + lower(last, b - 1)
            act, slope = gelu_pair(u)
            last = act.astype(BF16)
            act_ref[:, cols] = last
            gp_ref[:, cols] = slope.astype(BF16)
        out_ref[...] = total + lower(last, FF // step - 1)

    def row(width):
        return pl.BlockSpec((tall, width), lambda i: (i, 0))

    return pl.pallas_call(
        kernel,
        grid=(n // tall,),
        in_specs=[SMEM, row(D), whole((4, D))] + [ANY] * sources,
        out_specs=[row(D), row(FF), row(FF)],
        out_shape=[
            jax.ShapeDtypeStruct((n, D), F32),
            pltpu.HBM((n, FF), BF16),
            pltpu.HBM((n, FF), BF16),
        ],
        scratch_shapes=[
            pltpu.VMEM((4, D, W), BF16),
            pltpu.VMEM((FF // rows, rows, D), BF16),
            pltpu.SemaphoreType.DMA((copies_of(group),)),
        ],
        compiler_params=params(),
        cost_estimate=cost(4 * n * D * FF, n * D * 24, n * FF * 2),
        name="mlp_fwd",
    )(where, in_hbm(mid), norms, *group)


def mlp_bwd(place, where, dz, mid, gp, norms, group):
    rows = D // place.shards
    n = mid.shape[0]
    sources = len(group)
    per = W // rows

    def kernel(where_ref, dz_ref, mid_ref, gp_ref, norm_ref, *refs):
        pieces, refs = refs[:sources], refs[sources:]
        dmid_ref, dh_ref, du_ref, c_ref, dm_ref, dn_ref, up_ref, down_ref, sem = refs
        i = pl.program_id(0)
        fill_weights(i, where_ref, pieces, mlp_targets(up_ref, down_ref, rows), sem)
        dm = dz_ref[...].astype(BF16)
        dm_ref[...] = dm

        def upper(b):
            return dense_nt(dm, down_ref[per * b : per * b + per].reshape(W, D))

        dc = jnp.zeros((LEN, D), F32)
        ahead = upper(0)
        for b in range(FF // W):
            cols = slice(W * b, W * b + W)
            da = ahead
            if b + 1 < FF // W:
                ahead = upper(b + 1)
            if b > 0:
                dc = dc + dense_nt(last, up_ref[b - 1])
            last = (gp_ref[:, cols].astype(F32) * da).astype(BF16)
            du_ref[:, cols] = last
        dc = dc + dense_nt(last, up_ref[FF // W - 1])
        xhat, rstd = norm_parts(mid_ref[...])
        gain = norm_ref[2:3, :]
        c_ref[...] = (xhat * gain + norm_ref[3:4, :]).astype(BF16)
        dmid = dz_ref[...] + norm_back(xhat, rstd, dc, gain)
        dmid_ref[...] = dmid
        dh_ref[...] = dmid.astype(BF16)

        @pl.when(i == 0)
        def _():
            dn_ref[...] = jnp.zeros_like(dn_ref)

        dn_ref[0:1, :] += jnp.sum(dc * xhat, 0, keepdims=True)
        dn_ref[1:2, :] += jnp.sum(dc, 0, keepdims=True)

    def row(width):
        return pl.BlockSpec((LEN, width), lambda i: (i, 0))

    return pl.pallas_call(
        kernel,
        grid=(n // LEN,),
        in_specs=[SMEM, row(D), row(D), row(FF), whole((4, D))] + [ANY] * sources,
        out_specs=[row(D), row(D), row(FF), row(D), row(D), whole((8, D))],
        out_shape=[
            jax.ShapeDtypeStruct((n, D), F32),
            jax.ShapeDtypeStruct((n, D), BF16),
            pltpu.HBM((n, FF), BF16),
            jax.ShapeDtypeStruct((n, D), BF16),
            jax.ShapeDtypeStruct((n, D), BF16),
            jax.ShapeDtypeStruct((8, D), F32),
        ],
        scratch_shapes=[
            pltpu.VMEM((4, D, W), BF16),
            pltpu.VMEM((FF // rows, rows, D), BF16),
            pltpu.SemaphoreType.DMA((copies_of(group),)),
        ],
        compiler_params=params(),
        cost_estimate=cost(4 * n * D * FF, n * D * 32),
        name="mlp_bwd",
    )(where, dz, in_hbm(mid), in_hbm(gp), norms, *group)


def attn_bwd(place, where, dmid, dh, x, qkv, pt, ot, norms, group):
    rows = D // place.shards
    n = x.shape[0]
    seqs = n // LEN
    sources = len(group)

    def kernel(where_ref, dmid_ref, dh_ref, x_ref, qkv_ref, pt_ref, ot_ref, norm_ref, *refs):
        pieces, refs = refs[:sources], refs[sources:]
        dx_ref, dqkv_ref, a_ref, dn_ref, w_ref, dqt_ref, sem = refs
        i = pl.program_id(0)
        fill_weights(i, where_ref, pieces, attn_targets(w_ref, rows), sem)
        spans = [slice(None)]
        do, delta, kt = [], [], []
        for s, span in enumerate(spans):
            do.append(dense_nt(dh_ref[span], w_ref[3]).astype(BF16))
            along = do[s].T.astype(F32) * ot_ref[s].astype(F32)
            delta.append([jnp.sum(along[head_of(h), :], axis=0, keepdims=True) for h in range(H)])
            kt.append(qkv_ref[span, D : 2 * D].T)

        def first(s, h):
            doh = head_lanes(do[s], h)
            v = qkv_ref[spans[s], 2 * D + 128 * (h // 2) : 2 * D + 128 * (h // 2) + 128]
            return dense_nt(v, doh), dense(pt_ref[s, h], doh)

        halves = {}

        def second(s, h, dst, dv):
            q = qkv_ref[spans[s], pair_of(h)]
            lane = lax.broadcasted_iota(jnp.int32, (LEN, 128), 1)
            own = (lane < DH) if h % 2 == 0 else (lane >= DH)
            dk = dense(dst, jnp.where(own, q, 0))
            dqt_ref[s, head_of(h), :] = (dense(kt[s][head_of(h), :], dst) * DH**-0.5).astype(BF16)
            if h % 2 == 0:
                halves[s] = (dk, dv)
                return
            at = 128 * (h // 2)
            dk, dv = dk + halves[s][0], dv + halves[s][1]
            dqkv_ref[spans[s], D + at : D + at + 128] = dk.astype(BF16)
            dqkv_ref[spans[s], 2 * D + at : 2 * D + at + 128] = dv.astype(BF16)

        items = [(s, h) for h in range(H) for s in range(1)]
        ahead = first(*items[0])
        last = None
        for at, (s, h) in enumerate(items):
            dpt, dv = ahead
            if at + 1 < len(items):
                ahead = first(*items[at + 1])
            if last is not None:
                second(*last)
            dst = (pt_ref[s, h].astype(F32) * (dpt - delta[s][h])).astype(BF16)
            last = (s, h, dst, dv)
        second(*last)

        @pl.when(i == 0)
        def _():
            dn_ref[...] = jnp.zeros_like(dn_ref)

        gain = norm_ref[0:1, :]
        for s, span in enumerate(spans):
            da = dense_nt(dqkv_ref[span, D : 2 * D], w_ref[1])
            da = da + dense_nt(dqkv_ref[span, 2 * D :], w_ref[2])
            dq = dqt_ref[s].T
            dqkv_ref[span, :D] = dq
            da = da + dense_nt(dq, w_ref[0])
            xhat, rstd = norm_parts(x_ref[span])
            a_ref[span] = (xhat * gain + norm_ref[1:2, :]).astype(BF16)
            dx_ref[span] = dmid_ref[span] + norm_back(xhat, rstd, da, gain)
            dn_ref[0:1, :] += jnp.sum(da * xhat, 0, keepdims=True)
            dn_ref[1:2, :] += jnp.sum(da, 0, keepdims=True)

    def row(width):
        return pl.BlockSpec((LEN, width), lambda i: (i, 0))

    return pl.pallas_call(
        kernel,
        grid=(seqs,),
        in_specs=[
            SMEM,
            row(D),
            row(D),
            row(D),
            row(3 * D),
            pl.BlockSpec((1, H, LEN, LEN), lambda i: (i, 0, 0, 0)),
            pl.BlockSpec((1, D, LEN), lambda i: (i, 0, 0)),
            whole((4, D)),
        ]
        + [ANY] * sources,
        out_specs=[row(D), row(3 * D), row(D), whole((8, D))],
        out_shape=[
            jax.ShapeDtypeStruct((n, D), F32),
            jax.ShapeDtypeStruct((n, 3 * D), BF16),
            jax.ShapeDtypeStruct((n, D), BF16),
            jax.ShapeDtypeStruct((8, D), F32),
        ],
        scratch_shapes=[
            pltpu.VMEM((4, D, W), BF16),
            pltpu.VMEM((1, D, LEN), BF16),
            pltpu.SemaphoreType.DMA((copies_of(group),)),
        ],
        compiler_params=params(),
        cost_estimate=cost(2 * n * D * (4 * D + 5 * LEN), n * D * 32),
        name="attn_bwd",
    )(where, dmid, dh, x, in_hbm(qkv), in_hbm(pt), in_hbm(ot), norms, *group)


def head_step(place, x, target, maskf, head, norms, count):
    n = x.shape[0]

    def kernel(x_ref, target_ref, mask_ref, head_ref, norm_ref, dx_ref, loss_ref, gh_ref, dn_ref):
        i = pl.program_id(0)
        xhat, rstd = norm_parts(x_ref[...])
        gain = norm_ref[0:1, :]
        y = (xhat * gain + norm_ref[1:2, :]).astype(BF16)
        masked = mask_ref[...]
        err = (dense_nt(y, head_ref[...]) - target_ref[...].astype(F32)) * masked
        dpred = (err * (2.0 / (P_SIZE * count))).astype(BF16)
        dy = dense(dpred, head_ref[...])
        dx_ref[...] = norm_back(xhat, rstd, dy, gain)

        @pl.when(i == 0)
        def _():
            loss_ref[...] = jnp.zeros_like(loss_ref)
            gh_ref[...] = jnp.zeros_like(gh_ref)
            dn_ref[...] = jnp.zeros_like(dn_ref)

        loss_ref[...] += jnp.sum(err * err, 0, keepdims=True)
        gh_ref[...] += dense_tn(dpred, y)
        dn_ref[0:1, :] += jnp.sum(dy * xhat, 0, keepdims=True)
        dn_ref[1:2, :] += jnp.sum(dy, 0, keepdims=True)

    def row(width):
        return pl.BlockSpec((LEN, width), lambda i: (i, 0))

    return pl.pallas_call(
        kernel,
        grid=(n // LEN,),
        in_specs=[row(D), row(P_SIZE), row(1), whole((P_SIZE, D)), whole((2, D))],
        out_specs=[row(D), whole((1, P_SIZE)), whole((P_SIZE, D)), whole((8, D))],
        out_shape=[
            jax.ShapeDtypeStruct((n, D), F32),
            jax.ShapeDtypeStruct((1, P_SIZE), F32),
            jax.ShapeDtypeStruct((P_SIZE, D), F32),
            jax.ShapeDtypeStruct((8, D), F32),
        ],
        compiler_params=params(),
        cost_estimate=cost(6 * n * D * P_SIZE, n * D * 8),
        name="head_step",
    )(x, target, maskf, head, norms)


def put_block(core, block, lead, send_ref, keep_ref, at):
    rows = block.shape[0]
    halves = block.reshape(lead + (2, rows // (2 * lead_size(lead)), W))
    first, second = halves[..., 0, :, :], halves[..., 1, :, :]
    keep_ref[at] = jnp.where(core == 0, first, second)
    send_ref[at] = jnp.where(core == 0, second, first)


def lead_size(lead):
    size = 1
    for n in lead:
        size *= n
    return size


def grad_mlp(place, where, c, du, act, dm, ot, dh):
    shards = place.shards
    rows = D // shards
    n = c.shape[0]
    seqs = n // LEN
    wide = 2 * W
    steps = FF // wide
    per = shards // steps
    blocks = 9

    def kernel(where_ref, c_ref, du_ref, act_ref, dm_ref, ot_ref, dh_ref, send_ref, keep_ref, ct_ref):
        i = pl.program_id(0)
        core = where_ref[1]

        @pl.when(i == 0)
        def _():
            ct_ref[...] = c_ref[...].T

        @pl.when(i < steps)
        def _():
            block = dense(ct_ref[...], du_ref[...]).astype(BF16)
            for b in range(wide // W):
                at = (slice(None), i * (wide // W) + b)
                put_block(core, block[:, W * b : W * b + W], (shards,), send_ref, keep_ref, at)

        @pl.when((i >= steps) & (i < 2 * steps))
        def _():
            block = dense_tn(act_ref[...], dm_ref[...]).astype(BF16)
            at = (pl.ds((i - steps) * per, per), slice(4, 8))
            put_block(core, block, (per, 4), send_ref, keep_ref, at)

        @pl.when(i == 2 * steps)
        def _():
            total = dense(ot_ref[0], dh_ref[:LEN, :])
            for s in range(1, seqs):
                total = total + dense(ot_ref[s], dh_ref[LEN * s : LEN * s + LEN, :])
            put_block(core, total.astype(BF16), (shards,), send_ref, keep_ref, (slice(None), 8))

    shape = (shards, blocks, rows // 2, W)
    return pl.pallas_call(
        kernel,
        grid=(2 * steps + 1,),
        in_specs=[
            SMEM,
            whole((n, D)),
            pl.BlockSpec((n, wide), lambda i: (0, jnp.minimum(i, steps - 1))),
            pl.BlockSpec((n, wide), lambda i: (0, jnp.clip(i - steps, 0, steps - 1))),
            whole((n, D)),
            whole((seqs, D, LEN)),
            whole((n, D)),
        ],
        out_specs=[whole(shape), whole(shape)],
        scratch_shapes=[pltpu.VMEM((D, n), BF16)],
        out_shape=[jax.ShapeDtypeStruct(shape, BF16)] * 2,
        compiler_params=params(),
        cost_estimate=cost(4 * n * D * FF, n * (4 * D + 4 * FF) + 4 * D * FF),
        name="grad_mlp",
    )(where, c, in_hbm(du), in_hbm(act), dm, in_hbm(ot), dh)


def grad_qkv(place, where, a, dqkv, small=()):
    shards = place.shards
    rows = D // shards
    half = rows // 2
    n = a.shape[0]
    blocks = 3 + bool(small)
    extra = len(small)

    def kernel(where_ref, a_ref, dqkv_ref, *refs):
        small_refs, refs = refs[:extra], refs[extra:]
        send_ref, keep_ref, at_ref = refs[:3]
        i = pl.program_id(0)

        @pl.when(i == 0)
        def _():
            at_ref[...] = a_ref[...].T

        @pl.when(i < 3)
        def _():
            block = dense(at_ref[...], dqkv_ref[...]).astype(BF16)
            put_block(where_ref[1], block, (shards,), send_ref, keep_ref, (slice(None), i))

        if extra:
            table_ref = refs[3]
            inputs_ref, dx_ref, head_ref = small_refs[:3]

            @pl.when(i == 3)
            def _():
                dx = dx_ref[...]
                table_ref[:P_SIZE] = dense_tn(inputs_ref[...], dx.astype(BF16)).astype(BF16)
                table_ref[P_SIZE : 2 * P_SIZE] = head_ref[...].astype(BF16)
                total = dx[:LEN]
                for s in range(1, n // LEN):
                    total = total + dx[s * LEN : s * LEN + LEN]
                table_ref[2 * P_SIZE : 2 * P_SIZE + LEN] = total.astype(BF16)
                norms = jnp.concatenate(
                    [ref[0:2, :] for ref in small_refs[3:]]
                    + [jnp.zeros((16 - 2 * (extra - 3), D), F32)],
                    0,
                )
                start = 2 * P_SIZE + LEN
                table_ref[start : start + 16] = norms.astype(BF16)
                table_ref[start + 16 :] = jnp.zeros((SMALL - start - 16, D), BF16)
                for core in range(2):

                    @pl.when(where_ref[1] == core)
                    def _(core=core):
                        for h in range(2):
                            out_ref = keep_ref if h == core else send_ref
                            for j in range(shards):
                                for q in range(W // rows):
                                    first = h * (SMALL // 2) + q * half
                                    value = table_ref[first : first + half, j * rows : j * rows + rows]
                                    out_ref[j, 3, :, q * rows : q * rows + rows] = value

    shape = (shards, blocks, half, W)
    return pl.pallas_call(
        kernel,
        grid=(blocks,),
        in_specs=[SMEM, whole((n, D)), pl.BlockSpec((n, W), lambda i: (0, jnp.minimum(i, 2)))]
        + [whole(x.shape) for x in small],
        out_specs=[whole(shape), whole(shape)],
        scratch_shapes=[pltpu.VMEM((D, n), BF16)] + [pltpu.VMEM((SMALL, D), BF16)] * bool(small),
        out_shape=[jax.ShapeDtypeStruct(shape, BF16)] * 2,
        compiler_params=params(),
        cost_estimate=cost(6 * n * D * D, n * 8 * D + 6 * D * D),
        name="grad_qkv",
    )(where, a, dqkv, *small)


def adam(weight, first, second, tenth, rate):
    scale = (1 - BETA_ONE**STEP_COUNT) / rate
    first = BETA_ONE * first + tenth
    second = BETA_TWO * second + tenth * ((1 - BETA_TWO) / (1 - BETA_ONE) ** 2) * tenth
    spread = second * (scale * scale / (1 - BETA_TWO**STEP_COUNT))
    step = first * (1.0 / (spread * lax.rsqrt(spread) + ADAM_EPS * scale))
    return (weight * (1 - rate * DECAY) - step, first, second)


def fetch(arrays, where):
    def kernel(where_ref, *refs):
        sem = refs[-1]
        count = len(arrays)
        copies = [
            pltpu.make_async_copy(refs[n], refs[count + n], sem.at[n]) for n in range(count)
        ]
        for copy in copies:
            copy.start()
        for copy in copies:
            copy.wait()

    return pl.pallas_call(
        kernel,
        in_specs=[SMEM] + [pl.BlockSpec(memory_space=pltpu.HBM)] * len(arrays),
        out_specs=[pl.BlockSpec(memory_space=pltpu.VMEM)] * len(arrays),
        out_shape=[pltpu.VMEM(x.shape, x.dtype) for x in arrays],
        scratch_shapes=[pltpu.SemaphoreType.DMA((len(arrays),))],
        compiler_params=params(4),
        name="fetch",
    )(where, *map(in_hbm, arrays))


def adam_step(place, where, both, count, state, small, grads):
    rows = D // place.shards
    half = rows // 2
    few = half // 2
    flat = [x for group in state for x in group]
    tiny = [x for group in small for x in group]

    def spec(x):
        if x.ndim == 4:
            return pl.BlockSpec((None, 4, few, W), lambda i, h, q: (i, 0, 2 * h + q, 0))
        return pl.BlockSpec((None, few, x.shape[2]), lambda i, h, q: (i, 2 * h + q, 0))

    gflat, spots = [], []
    for layer in grads:
        spots.append([])
        for pieces, first, bit in layer:
            known = [n for n, x in enumerate(gflat) if x is pieces[0]]
            spots[-1].append((known[0] if known else len(gflat), len(pieces), first, bit))
            gflat += [] if known else list(pieces)
    total = len(flat) + len(tiny)

    def kernel(where_ref, *refs):
        both_refs, refs = refs[: len(both)], refs[len(both) :]
        grad_refs, refs = refs[: len(gflat)], refs[len(gflat) :]
        ins, outs, table_ref = refs[:total], refs[total : 2 * total], refs[-1]
        loss_ref, norm_ref = refs[2 * total : 2 * total + 2]
        layer, h, q = pl.program_id(0), pl.program_id(1), pl.program_id(2)
        values = [ref[...] for ref in both_refs]
        sums = jnp.zeros((1, 2), F32)
        for j in range(len(values)):
            sums = sums + select_of(values, where_ref[0] ^ j)
        norm = jnp.sqrt(sums[:, 1:2])
        loss_ref[...] = sums[:, 0:1] / count
        norm_ref[...] = norm
        scale = (1 - BETA_ONE) * CLIP / jnp.maximum(norm, CLIP)
        own = where_ref[1] == h

        def update(n, at, grad, rate):
            got = adam(ins[3 * n][at], ins[3 * n + 1][at], ins[3 * n + 2][at], grad, rate)
            for k in range(3):
                outs[3 * n + k][at] = got[k]

        part = pl.ds(pl.multiple_of(q * few, few), few)

        def run(layer):
            def grad(group, b):
                base, count, first, bit = spots[layer][group]
                refs = grad_refs[base : base + count]
                if count == 2:
                    got = jnp.where(own, refs[0][first + b, part], refs[1][first + b, part])
                else:
                    close = jnp.where(own, refs[0][first + b], refs[1][first + b])
                    away = jnp.where(own, refs[2][first + b], refs[3][first + b])
                    got = jnp.where(where_ref[bit] == q, close, away)
                return got.astype(F32) * scale

            for b in range(3):
                update(0, (slice(None), slice(W * b, W * b + W)), grad(0, b), RATE)
            update(1, (slice(None), slice(None)), grad(1, 8), RATE)
            for b in range(4):
                update(2, (slice(None), slice(W * b, W * b + W)), grad(1, b), RATE)
                update(3, (b,), grad(1, 4 + b), RATE)

        for i in range(L):

            @pl.when(layer == i)
            def _(i=i):
                run(i)

        @pl.when((layer == 0) & (h == 0) & (q == 0))
        def _():
            base, _, at, _ = spots[0][0]
            mine, other = grad_refs[base][at + 3], grad_refs[base + 1][at + 3]
            first = where_ref[1] == 0
            for n, block in enumerate((jnp.where(first, mine, other), jnp.where(first, other, mine))):
                for k in range(W // rows):
                    start = n * (SMALL // 2) + k * half
                    table_ref[start : start + half] = (
                        block[:, k * rows : k * rows + rows].astype(F32) * scale
                    )
            count = 2 * P_SIZE + LEN
            update(4, (slice(None), slice(None)), table_ref[:count], TABLE_RATE)
            norms = small[1][0].shape[0]
            update(5, (slice(None), slice(None)), table_ref[count : count + norms], TABLE_RATE)

    out = pl.pallas_call(
        kernel,
        grid=(L, 2, 2),
        in_specs=[SMEM]
        + [whole((1, 2)) for _ in both]
        + [whole(g.shape) for g in gflat]
        + [spec(x) for x in flat]
        + [whole(x.shape) for x in tiny],
        out_specs=[spec(x) for x in flat] + [whole(x.shape) for x in tiny] + [whole((1, 1))] * 2,
        out_shape=[pltpu.HBM(x.shape, F32) for x in flat + tiny]
        + [jax.ShapeDtypeStruct((1, 1), F32)] * 2,
        scratch_shapes=[pltpu.VMEM((SMALL, rows), F32)],
        compiler_params=params(20),
        cost_estimate=cost(20 * L * 12 * rows * W, 24 * L * 12 * rows * W),
        name="adam_step",
    )(where, *both, *gflat, *flat, *map(in_hbm, tiny))
    news = [tuple(out[3 * n : 3 * n + 3]) for n in range(len(state) + len(small))]
    return out[-2].reshape(()), out[-1].reshape(()), news


def on_device(
    series,
    mask,
    qkv_w,
    out_w,
    up_w,
    down_w,
    patch_maps,
    norm_params,
    qkv_m,
    out_m,
    up_m,
    down_m,
    patch_m,
    norm_m,
    qkv_v,
    out_v,
    up_v,
    down_v,
    patch_v,
    norm_v,
):
    place = Place()
    shards = place.shards
    rows = D // shards
    half = rows // 2
    seqs = series.shape[0]
    count = MASKED * seqs * shards * place.replicas
    shard_bits = [(place.shard >> bit) & 1 for bit in bits_of(shards)]
    chip_bits = [(place.chip >> bit) & 1 for bit in bits_of(place.chips)]
    where = jnp.stack([place.shard, place.core] + shard_bits + chip_bits).astype(jnp.int32)
    chip = 2 + len(shard_bits)

    small_now = [patch_maps, norm_params]
    packs = [
        (
            pack(place, where, i, [qkv_w, out_w], [], small_now if i == 0 else []),
            pack(place, where, i, [up_w], [down_w], []),
        )
        for i in range(L)
    ]

    def group_of(packed, ours, theirs):
        return [packed[0]] + ours + [theirs]

    attn_groups = [None] * L
    mlp_groups = [None] * L
    target = series.reshape(seqs * LEN, P_SIZE)
    maskf = mask.reshape(seqs * LEN, 1).astype(F32)
    ours = gather_shards(place, packs[0][0][1])
    theirs = gather_cores(place, ours, *[p[1] for pair in packs for p in pair], target, maskf)
    attn_groups[0] = group_of(packs[0][0], ours, theirs)
    mine = gate(packs[0][1][1], *ours)
    ours_mlp = gather_shards(place, mine)

    x, inputs, head, norms_all = embed_step(place, where, target, gate(maskf, mine), attn_groups[0])
    saved = []
    for index in range(L):
        norms = norms_all[4 * index : 4 * index + 4]
        held = in_hbm(x) if index == 0 else x
        mid, qkv, pt, ot = attn_fwd(place, where, held, norms, attn_groups[index])
        held = mid
        if index + 1 < L:
            got = gates(ours_mlp, mid)
            mine = gate(packs[index + 1][0][1], *got)
            ours_attn = gather_shards(place, mine)
            held = gate(mid, mine)
        theirs = gather_cores(place, ours_mlp, mid)
        mlp_groups[index] = group_of(packs[index][1], ours_mlp, theirs)
        pieces = mlp_groups[index] if index == 0 else [in_hbm(x) for x in mlp_groups[index]]
        y, act, gp = mlp_fwd(place, where, held, norms, pieces)
        if index + 1 < L:
            got = gates(ours_attn, y)
            theirs = gather_cores(place, got)
            attn_groups[index + 1] = group_of(packs[index + 1][0], ours_attn, theirs)
            mine = gate(packs[index + 1][1][1], *got)
            ours_mlp = gather_shards(place, mine)
            y = gate(y, mine)
        saved.append((x, mid, qkv, pt, ot, act, gp, norms))
        x = y

    grad, loss, g_head, dn_final = head_step(
        place, x, target, maskf, head, norms_all[4 * L : 4 * L + 2], count
    )
    loss = (jnp.sum(loss) / P_SIZE).reshape(1, 1)

    norm_grads = {}

    def backward_mlp(index, grad):
        x, mid, qkv, pt, ot, act, gp, norms = saved[index]
        dmid, dh, du, c, dm, dn = mlp_bwd(
            place, where, grad, mid, gp, norms, mlp_groups[index]
        )
        norm_grads[index, 1] = dn
        return dmid, dh, du, c, dm

    def backward_attn(index, dmid, dh):
        x, mid, qkv, pt, ot, act, gp, norms = saved[index]
        grad, dqkv, a, dn = attn_bwd(
            place, where, dmid, dh, x, qkv, pt, ot, norms, attn_groups[index]
        )
        norm_grads[index, 0] = dn
        return grad, dqkv, a

    def grads_mlp(index, du, c, dm, dh):
        return grad_mlp(place, where, c, du, saved[index][5], dm, saved[index][4], dh)

    one, two = Flow(place, True, True), Flow(place, True)
    ahead, end = Flow(place, False), Flow(place, False)

    def advance(flows, *after):
        token = sum_round(where, flows, *after)
        for flow in flows:
            flow.launch()
        return token

    loss = loss + place.to_core(loss)
    dmid, dh, du, c, dm = backward_mlp(1, grad)
    token = one.begin(*grads_mlp(1, du, c, dm, dh), (0, 4, 0), (4, 5, 1))
    grad, dqkv_one, a_one = backward_attn(1, gate(dmid, token), dh)
    token = advance([one], grad)
    dmid, dh, du, c, dm = backward_mlp(0, gate(grad, token))
    token = advance([one], dmid)
    token = two.begin(*grads_mlp(0, du, gate(c, token), dm, dh), (0, 4, 0), (4, 5, 1))
    token = advance([one], token)
    token = ahead.begin(*grad_qkv(place, where, gate(a_one, token), dqkv_one), (0, 3, 1))
    token = advance([two], token)
    grad, dqkv, a = backward_attn(0, gate(dmid, token), dh)
    token = sum_round(where, [one, two, ahead], grad)
    small = [inputs, grad, g_head]
    small += [norm_grads[i, k] for i in range(L) for k in range(2)] + [dn_final]
    token = end.begin(*grad_qkv(place, where, gate(a, token), dqkv, small), (0, 4, 0))
    one.launch()
    two.launch()
    ahead.launch()
    while not one.last():
        token = advance([one], token)
    token = sum_round(where, [one, two, end], token)
    end.launch()
    end.join(ahead)
    two.launch()
    one.to_neighbours()
    hops = bits_of(place.chips)

    def pass_loss(loss, token):
        if not hops:
            return loss
        return loss + place.to_chip(gate(loss, token), 1 << hops.pop(0))

    while end.step < end.steps - 2:
        loss = pass_loss(loss, token)
        token = sum_round(where, [end] + ([two] if not two.last() else []), token, loss)
        end.launch()
        if two.step == two.steps - 1:
            break
        if not two.last():
            two.launch()
    behind = not two.last()
    while end.step < end.steps - 1:
        loss = pass_loss(loss, token)
        token = advance([end], token, *one.pieces, loss)
    one.to_last()
    if behind:
        two.launch()
    while hops:
        loss = pass_loss(loss, token)
    state = [(qkv_w, qkv_m, qkv_v), (out_w, out_m, out_v), (up_w, up_m, up_v)]
    state.append(tuple(x.reshape(L, 4, rows, W) for x in (down_w, down_m, down_v)))
    token = sum_round(where, [end, two], token, loss)
    end.launch()
    two.to_neighbours()
    near = fetch([x for group in state for x in group], gate(where, token))
    state = [tuple(near[3 * n : 3 * n + 3]) for n in range(len(state))]
    token = sum_round(where, [end], token, *two.pieces, near[0])
    end.to_neighbours()
    two.to_last()
    grads = [
        [(end.pieces, 3, 0), (two.pieces, 0, chip + two.chip_bits[0])],
        [(end.pieces, 0, 0), (one.pieces, 0, chip + one.chip_bits[0])],
    ]
    done_one, done_two, done_last = one.pieces, two.pieces, end.pieces

    both = square_sum(done_one + done_two + done_last, loss)
    both = [both] + [place.to_shard(both, k) for k in range(1, shards)]

    small = [(patch_maps, patch_m, patch_v), (norm_params, norm_m, norm_v)]
    loss, grad_norm, results = adam_step(place, where, both, count, state, small, grads)
    results[3] = tuple(x.reshape(down_w.shape) for x in results[3])
    news = tuple(r[0] for r in results)
    new_m = tuple(r[1] for r in results)
    new_v = tuple(r[2] for r in results)
    return (loss, grad_norm) + news + new_m + new_v


def solution(mesh):
    batch = P(("shard", "replica"), None)
    stack = P(None, "shard", None)
    flat = P(None, "shard")
    state = (stack, stack, stack, stack, flat, flat)
    return jax.shard_map(
        on_device,
        mesh=mesh,
        in_specs=(batch, batch) + state * 3,
        out_specs=(P(), P()) + state * 3,
        check_vma=False,
    )
```

```python
import jax
import jax.numpy as jnp
from jax import lax
from jax.experimental import pallas as pl
from jax.experimental.pallas import tpu as pltpu
from jax.sharding import PartitionSpec as P

D = 512
H = 8
DH = 64
FF = 2048
P_SIZE = 64
LEN = 256
L = 2
MASKED = 102

EPS = 1e-05
CLIP = 0.001
RATE = 0.05
TABLE_RATE = 0.3
BETA_ONE = 0.9
BETA_TWO = 0.999
ADAM_EPS = 1e-08
DECAY = 0.1
STEP_COUNT = 10

W = 512
SMALL = 512
NORMS_LOW = 2 * P_SIZE + LEN + 16
F32 = jnp.float32
BF16 = jnp.bfloat16


def dense(left, right):
    return jnp.dot(left, right, preferred_element_type=F32)


def dense_tn(left, right):
    return lax.dot_general(left, right, (((0,), (0,)), ((), ())), preferred_element_type=F32)


def dense_nt(left, right):
    return lax.dot_general(left, right, (((1,), (1,)), ((), ())), preferred_element_type=F32)


def layer_norm(x, gain, bias):
    center = x - jnp.mean(x, -1, keepdims=True)
    spread = jnp.mean(center * center, -1, keepdims=True)
    return center * lax.rsqrt(spread + EPS) * gain + bias


def params(mib=30):
    return pltpu.CompilerParams(vmem_limit_bytes=mib * 2**20)


def cost(flops, data, trans=0):
    return pl.CostEstimate(
        flops=int(30 * flops), bytes_accessed=int(30 * data), transcendentals=int(30 * trans)
    )


def whole(shape):
    return pl.BlockSpec(shape, lambda *_: (0,) * len(shape))


def in_hbm(x):
    return pltpu.with_memory_space_constraint(x, pltpu.HBM)


ANY = pl.BlockSpec(memory_space=pl.ANY)
SMEM = pl.BlockSpec(memory_space=pltpu.SMEM)


def permute(x, axis, mask, size):
    return lax.ppermute(x, axis, [(i, i ^ mask) for i in range(size)])


def pick(x, index):
    return lax.dynamic_index_in_dim(x, index, 0, keepdims=False)


class Place:
    def __init__(self):
        self.shards = lax.axis_size("shard")
        self.replicas = lax.axis_size("replica")
        self.chips = self.replicas // 2
        self.shard = lax.axis_index("shard")
        replica = lax.axis_index("replica")
        self.core = replica % 2
        self.chip = replica // 2

    def to_core(self, x):
        return permute(x, "replica", 1, self.replicas)

    def to_shard(self, x, mask):
        return permute(x, "shard", mask, self.shards)

    def to_chip(self, x, mask):
        return permute(x, "replica", 2 * mask, self.replicas)


def gate(x, *after):
    return lax.optimization_barrier((x,) + after)[0]


def gather_shards(place, mine):
    return [place.to_shard(mine, mask) for mask in range(1, place.shards)]


def gather_cores(place, ours, *after):
    items = gates(ours, *after)
    return place.to_core(stack(items) if items[0].shape[0] % 4 == 0 else jnp.stack(items))


def stack(items):
    def kernel(*refs):
        for n, ref in enumerate(refs[:-1]):
            refs[-1][n] = ref[...]

    few, rows, width = items[0].shape
    part = pl.BlockSpec((few // 2, rows, width), lambda i: (i, 0, 0))
    return pl.pallas_call(
        kernel,
        grid=(2,),
        in_specs=[part] * len(items),
        out_specs=pl.BlockSpec((len(items), few // 2, rows, width), lambda i: (0, i, 0, 0)),
        out_shape=jax.ShapeDtypeStruct((len(items), few, rows, width), items[0].dtype),
        compiler_params=params(12),
        cost_estimate=cost(10**5, 10**5),
        name="stack",
    )(*items)


def gates(items, *after):
    return list(lax.optimization_barrier(tuple(items) + after)[: len(items)])


def select_of(items, index):
    out = items[0]
    for k in range(1, len(items)):
        out = jnp.where(index == k, items[k], out)
    return out


def bits_of(size):
    return list(range(size.bit_length() - 1))


def total_of(values):
    total = values[0].astype(F32)
    for value in values[1:]:
        total = total + value.astype(F32)
    return total


def combine(where, jobs, name):
    lanes = W // 2
    arrays, leads, plans, shapes = [], [], [], []

    def number(array, lead):
        for n, known in enumerate(arrays):
            if known is array:
                return n
        arrays.append(array)
        leads.append(lead)
        return len(arrays) - 1

    for segments, lead, cut, bit in jobs:
        plans.append([[(number(a, lead), f, b) for a, f, b in parts] for parts in segments])
        blocks = sum(parts[0][2] for parts in segments)
        rows = segments[0][0][0].shape[-2]
        if cut is None:
            shapes.append(lead + (blocks, rows, W))
        elif cut == "rows":
            shapes += [lead + (blocks, rows // 2, W)] * 2
        else:
            shapes += [lead[:cut] + lead[cut + 1 :] + (blocks, rows, W)] * 2
    arrays = [a.reshape(lead + a.shape[-3:]) for a, lead in zip(arrays, leads)]

    def block(shape):
        zeros = (0,) * (len(shape) - 1)
        return pl.BlockSpec(shape[:-1] + (lanes,), lambda i: zeros + (i,))

    def kernel(where_ref, *refs):
        ins, outs = refs[: len(arrays)], list(refs[len(arrays) :])
        for (segments, lead, cut, bit), plan in zip(jobs, plans):
            some = (slice(None),) * len(lead)
            fewer = (slice(None),) * (len(lead) - (cut is not None and cut != "rows"))
            if cut is None:
                targets = [(outs.pop(0), None)]
            else:
                value = where_ref[bit]
                targets = [(outs.pop(0), 1 - value), (outs.pop(0), value)]
            for out_ref, at in targets:
                start = 0
                for parts in plan:
                    got = []
                    for n, f, b in parts:
                        index = some
                        if cut is not None and cut != "rows":
                            index = some[:cut] + (at,) + some[cut + 1 :]
                        index += (slice(f, f + b),)
                        if cut == "rows":
                            few = ins[n].shape[-2] // 2
                            index += (pl.ds(pl.multiple_of(at * few, few), few),)
                        got.append(ins[n][index])
                    out_ref[fewer + (slice(start, start + parts[0][2]),)] = total_of(got).astype(BF16)
                    start += parts[0][2]

    size = sum(a.size for a in arrays) * 4
    return pl.pallas_call(
        kernel,
        grid=(2,),
        in_specs=[SMEM] + [block(a.shape) for a in arrays],
        out_specs=[block(s) for s in shapes],
        out_shape=[jax.ShapeDtypeStruct(s, BF16) for s in shapes],
        compiler_params=params(12),
        cost_estimate=cost(size, size),
        name=name,
    )(where, *arrays)


class Flow:
    def __init__(self, place, spread, far_first=False):
        self.place, self.spread = place, spread
        self.chip_bits = bits_of(place.chips)[:: -1 if far_first else 1]
        self.bits = bits_of(place.shards)
        self.steps = len(self.bits) + len(bits_of(place.chips))
        self.step = 0
        self.inputs = []
        self.ranges = []

    def begin(self, send, keep, *ranges):
        other = self.place.to_core(send)
        for first, blocks, order in ranges:
            self.ranges.append((len(self.inputs), first, blocks, order))
        self.inputs += [keep, other]
        self.left = [list(reversed(self.bits)) for _ in self.ranges]
        return send

    def join(self, other):
        self.inputs = other.inputs + self.inputs
        self.ranges = other.ranges + self.ranges
        self.left = other.left + self.left

    def last(self):
        return self.step == self.steps

    def plan(self, flat):
        if self.step == 0:
            parts = [[(flat[n], f, b), (flat[n + 1], f, b)] for n, f, b, _ in self.ranges]
        else:
            parts = [
                [(x, 0, x.shape[-3]) for x in flat[2 * n : 2 * n + 2]]
                for n in range(len(flat) // 2)
            ]
        if self.step >= len(self.bits):
            cut = self.spread and self.step == len(self.bits)
            bit = 2 + len(self.bits) + self.chip_bits[0]
            return [(parts, (), "rows", bit) if cut else (parts, (), None, 0)]
        jobs, self.chosen = [], []
        for n, (_, _, _, order) in enumerate(self.ranges):
            bit = (self.bits if order == 0 else self.bits[::-1])[self.step]
            jobs.append(([parts[n]], (2,) * len(self.left[n]), self.left[n].index(bit), 2 + bit))
            self.left[n].remove(bit)
            self.chosen.append(bit)
        return jobs

    def take(self, out):
        if self.step < len(self.bits):
            self.sends, self.stays = out[0::2], out[1::2]
        else:
            self.sends, self.stays = out[:1], out[-1:]
        return self.sends[0]

    def launch(self):
        place = self.place
        if self.step < len(self.bits):
            got = [place.to_shard(x, 1 << bit) for x, bit in zip(self.sends, self.chosen)]
        else:
            bit = self.chip_bits[self.step - len(self.bits)]
            got = [place.to_chip(x, 1 << bit) for x in self.sends]
        self.inputs = [x for pair in zip(self.stays, got) for x in pair]
        self.step += 1

    def to_neighbours(self):
        self.pieces = [self.sends[0], self.place.to_core(self.sends[0])]
        if self.spread:
            self.pieces.append(self.place.to_chip(self.sends[0], 1 << self.chip_bits[0]))

    def to_last(self):
        if self.spread:
            self.pieces.append(self.place.to_core(self.pieces[2]))


def sum_round(where, flows, *after):
    flat = gates([x for flow in flows for x in flow.inputs], *after)
    jobs, counts = [], []
    for flow in flows:
        few = len(flow.inputs)
        some = flow.plan(flat[:few])
        flat = flat[few:]
        jobs += some
        counts.append(sum(1 if cut is None else 2 for _, _, cut, _ in some))
    out = combine(where, jobs, "sum_round")
    for flow, count in zip(flows, counts):
        token = flow.take(out[:count])
        out = out[count:]
    return token


def square_sum(pieces, loss):
    def kernel(loss_ref, *refs):
        total = jnp.zeros((1, W), F32)
        for ref in refs[:-1]:
            for b in range(ref.shape[0]):
                x = ref[b].astype(F32)
                total = total + jnp.sum(x * x, 0, keepdims=True)
        refs[-1][:, 0:1] = loss_ref[...]
        refs[-1][:, 1:2] = jnp.sum(total, 1, keepdims=True)

    return pl.pallas_call(
        kernel,
        grid=(1,),
        in_specs=[whole((1, 1))] + [whole(p.shape) for p in pieces],
        out_specs=whole((1, 2)),
        out_shape=jax.ShapeDtypeStruct((1, 2), F32),
        compiler_params=params(8),
        cost_estimate=cost(10**6, 10**6),
        name="square_sum",
    )(loss, *pieces)


def fill_weights(step, where_ref, sources, targets, sem):
    shard, core = where_ref[0], where_ref[1]
    count = len(sources) - 2

    @pl.when(step == 0)
    def _():
        made = targets(sources[0], shard, None)
        for k in range(count):
            made += targets(sources[1 + k], shard ^ (k + 1), core)
            made += targets(sources[-1].at[k], shard ^ (k + 1), 1 - core)
        todo = [pltpu.make_async_copy(s, t, sem.at[n]) for n, (s, t) in enumerate(made)]
        for copy in todo:
            copy.start()
        for copy in todo:
            copy.wait()


def attn_targets(w_ref, rows):
    def targets(piece, at, half):
        if half is None:
            return [(piece.at[pl.ds(0, 4)], w_ref.at[:, pl.ds(pl.multiple_of(at * rows, rows), rows)])]
        start = pl.multiple_of(at * rows + half * (rows // 2), rows // 2)
        return [(piece.at[pl.ds(0, 4)], w_ref.at[:, pl.ds(start, rows // 2)])]

    return targets


def mlp_targets(up_ref, down_ref, rows):
    def targets(piece, at, half):
        few = rows if half is None else rows // 2
        skip = 0 if half is None else half * few
        start = pl.multiple_of(at * rows + skip, few)
        skip = pl.multiple_of(skip, few) if half is not None else 0
        return [
            (piece.at[pl.ds(0, 4)], up_ref.at[:, pl.ds(start, few)]),
            (piece.at[pl.ds(4, 4)], down_ref.at[pl.ds(at * 4, 4), pl.ds(skip, few)]),
        ]

    return targets


def pack(place, where, index, tall, wide, small):
    rows = D // place.shards
    half = rows // 2
    wide = [x.reshape(L, 4, rows, W) for x in wide]
    total = sum(x.shape[2] // W for x in tall) + 4 * len(wide) + bool(small)
    count = len(tall) + len(wide)

    def kernel(where_ref, *refs):
        full_ref, mine_ref = refs[count + len(small) : count + len(small) + 2]

        def run(core):
            own = slice(core * half, core * half + half)
            at = 0
            for ref in refs[: len(tall)]:
                for b in range(ref.shape[1] // W):
                    block = ref[:, W * b : W * b + W].astype(BF16)
                    full_ref[at] = block
                    mine_ref[at] = block[own]
                    at += 1
            for ref in refs[len(tall) : count]:
                for b in range(4):
                    block = ref[b].astype(BF16)
                    full_ref[at] = block
                    mine_ref[at] = block[own]
                    at += 1
            if small:
                table_ref = refs[-1]
                start = 0
                for ref in refs[count : count + len(small)]:
                    table_ref[start : start + ref.shape[0]] = ref[...]
                    start += ref.shape[0]
                table_ref[start:] = jnp.zeros((SMALL - start, rows), F32)
                norms = refs[count + 1][...]
                left = norms - norms.astype(BF16).astype(F32)
                table_ref[NORMS_LOW : NORMS_LOW + norms.shape[0]] = left
                for h in range(2):
                    for q in range(W // rows):
                        first = h * (SMALL // 2) + q * half
                        value = table_ref[first : first + half, :].astype(BF16)
                        spot = slice(q * rows, q * rows + rows)
                        full_ref[at, h * half : h * half + half, spot] = value
                        if h == core:
                            mine_ref[at, :, spot] = value

        for core in range(2):

            @pl.when(where_ref[1] == core)
            def _(core=core):
                run(core)

    return pl.pallas_call(
        kernel,
        grid=(1,),
        in_specs=[SMEM]
        + [pl.BlockSpec((None, rows, x.shape[2]), lambda i: (index, 0, 0)) for x in tall]
        + [pl.BlockSpec((None, 4, rows, W), lambda i: (index, 0, 0, 0)) for x in wide]
        + [whole(x.shape) for x in small],
        out_specs=[whole((total, rows, W)), whole((total, half, W))],
        out_shape=[
            pltpu.HBM((total, rows, W), BF16),
            pltpu.HBM((total, half, W), BF16),
        ],
        scratch_shapes=[pltpu.VMEM((SMALL, rows), F32)] * bool(small),
        compiler_params=params(),
        cost_estimate=cost(total * rows * W, total * rows * W * 7),
        name="pack",
    )(where, *map(in_hbm, tall), *map(in_hbm, wide), *map(in_hbm, small))


def embed_step(place, where, target, maskf, group):
    shards = place.shards
    rows = D // shards
    half = rows // 2
    n = target.shape[0]
    sources = len(group)

    def kernel(where_ref, target_ref, mask_ref, *refs):
        pieces, refs = refs[:sources], refs[sources:]
        x_ref, inputs_ref, head_ref, norm_ref, got_ref, table_ref, sem = refs

        def targets(piece, at, part):
            start = 0 if part is None else pl.multiple_of(part * half, half)
            few = rows if part is None else half
            return [(piece.at[4], got_ref.at[at, pl.ds(start, few)])]

        fill_weights(0, where_ref, pieces, targets, sem)
        for j in range(shards):
            for h in range(2):
                for q in range(W // rows):
                    spot = slice(q * rows, q * rows + rows)
                    part = slice(h * half, h * half + half)
                    value = got_ref[j, part, spot].astype(F32)
                    first = h * (SMALL // 2) + q * half
                    table_ref[first : first + half, j * rows : j * rows + rows] = value
        inputs = jnp.where(mask_ref[...] > 0, 0.0, target_ref[...].astype(F32)).astype(BF16)
        inputs_ref[...] = inputs
        embed = table_ref[:P_SIZE].astype(BF16)
        for s in range(n // LEN):
            part = slice(s * LEN, s * LEN + LEN)
            x_ref[part] = dense(inputs[part], embed) + table_ref[2 * P_SIZE : 2 * P_SIZE + LEN]
        head_ref[...] = table_ref[P_SIZE : 2 * P_SIZE].astype(BF16)
        low = table_ref[NORMS_LOW : NORMS_LOW + 16]
        norm_ref[...] = table_ref[NORMS_LOW - 16 : NORMS_LOW] + low

    return pl.pallas_call(
        kernel,
        grid=(1,),
        in_specs=[SMEM, whole((n, P_SIZE)), whole((n, 1))] + [ANY] * sources,
        out_specs=[whole((n, D)), whole((n, P_SIZE)), whole((P_SIZE, D)), whole((16, D))],
        out_shape=[
            pltpu.HBM((n, D), F32),
            jax.ShapeDtypeStruct((n, P_SIZE), BF16),
            jax.ShapeDtypeStruct((P_SIZE, D), BF16),
            jax.ShapeDtypeStruct((16, D), F32),
        ],
        scratch_shapes=[
            pltpu.VMEM((shards, rows, W), BF16),
            pltpu.VMEM((SMALL, D), F32),
            pltpu.SemaphoreType.DMA((copies_of(group),)),
        ],
        compiler_params=params(),
        cost_estimate=cost(2 * n * D * P_SIZE, n * D * 5),
        name="embed_step",
    )(where, target, maskf, in_hbm(group[0]), *group[1:])


def copies_of(group):
    return 2 * (2 * (len(group) - 2) + 1)


def norm_parts(x):
    center = x - jnp.mean(x, -1, keepdims=True)
    rstd = lax.rsqrt(jnp.mean(center * center, -1, keepdims=True) + EPS)
    return center * rstd, rstd


def norm_back(xhat, rstd, dy, gain):
    dxh = dy * gain
    return rstd * (
        dxh - jnp.mean(dxh, -1, keepdims=True) - xhat * jnp.mean(dxh * xhat, -1, keepdims=True)
    )


def head_lanes(x, h):
    lane = lax.broadcasted_iota(jnp.int32, (x.shape[0], 128), 1)
    own = (lane < DH) if h % 2 == 0 else (lane >= DH)
    return jnp.where(own, x[:, pair_of(h)], 0)


def pair_of(h):
    return slice(128 * (h // 2), 128 * (h // 2) + 128)


def head_of(h):
    return slice(DH * h, DH * h + DH)


SP = 1


def attn_fwd(place, where, x, norms, group):
    rows = D // place.shards
    n = x.shape[0]
    seqs = n // LEN
    sources = len(group)

    def kernel(where_ref, x_ref, norm_ref, *refs):
        pieces, refs = refs[:sources], refs[sources:]
        mid_ref, qkv_ref, pt_ref, ot_ref, w_ref, sem = refs
        fill_weights(pl.program_id(0), where_ref, pieces, attn_targets(w_ref, rows), sem)
        spans = [slice(LEN * s, LEN * s + LEN) for s in range(SP)]
        a, q, k, vt = [], [], [], []
        for s, span in enumerate(spans):
            xhat, _ = norm_parts(x_ref[span])
            a.append((xhat * norm_ref[0:1, :] + norm_ref[1:2, :]).astype(BF16))
            q.append((dense(a[s], w_ref[0]) * DH**-0.5).astype(BF16))
            k.append(dense(a[s], w_ref[1]).astype(BF16))
            qkv_ref[span, :D] = q[s]
            qkv_ref[span, D : 2 * D] = k[s]

        def scores(s, h):
            return dense_nt(k[s][:, pair_of(h)], head_lanes(q[s], h))

        def gather_values(s, h, p):
            ot_ref[s, head_of(h), :] = dense(vt[s][head_of(h), :], p).astype(BF16)

        items = [(s, h) for h in range(H) for s in range(SP)]
        ahead = scores(*items[0])
        for s, span in enumerate(spans):
            v = dense(a[s], w_ref[2]).astype(BF16)
            qkv_ref[span, 2 * D :] = v
            vt.append(v.T)
        last = None
        for at, (s, h) in enumerate(items):
            st = ahead
            if at + 1 < len(items):
                ahead = scores(*items[at + 1])
            if last is not None:
                gather_values(*last)
            e = jnp.exp(st - jnp.max(st, axis=0, keepdims=True))
            p = (e * (1.0 / jnp.sum(e, axis=0, keepdims=True))).astype(BF16)
            pt_ref[s, h] = p
            last = (s, h, p)
        gather_values(*last)
        for s, span in enumerate(spans):
            mid_ref[span] = x_ref[span] + dense_tn(ot_ref[s], w_ref[3])

    return pl.pallas_call(
        kernel,
        grid=(seqs // SP,),
        in_specs=[SMEM, pl.BlockSpec((SP * LEN, D), lambda i: (i, 0)), whole((4, D))]
        + [ANY] * sources,
        out_specs=[
            pl.BlockSpec((SP * LEN, D), lambda i: (i, 0)),
            pl.BlockSpec((SP * LEN, 3 * D), lambda i: (i, 0)),
            pl.BlockSpec((SP, H, LEN, LEN), lambda i: (i, 0, 0, 0)),
            pl.BlockSpec((SP, D, LEN), lambda i: (i, 0, 0)),
        ],
        out_shape=[
            pltpu.HBM((n, D), F32),
            pltpu.HBM((n, 3 * D), BF16),
            pltpu.HBM((seqs, H, LEN, LEN), BF16),
            pltpu.HBM((seqs, D, LEN), BF16),
        ],
        scratch_shapes=[
            pltpu.VMEM((4, D, W), BF16),
            pltpu.SemaphoreType.DMA((copies_of(group),)),
        ],
        compiler_params=params(),
        cost_estimate=cost(2 * n * D * (4 * D + 2 * LEN), n * D * 20, n * H * LEN),
        name="attn_fwd",
    )(where, x, norms, in_hbm(group[0]), *group[1:])


def gelu_pair(u):
    cdf = 0.5 * lax.erf(u * 0.7071067811865476) + 0.5
    density = jnp.exp(u * u * -0.5) * 0.3989422804014327
    return u * cdf, cdf + u * density


def mlp_fwd(place, where, mid, norms, group):
    rows = D // place.shards
    n = mid.shape[0]
    tall = LEN
    step = W // 2
    sources = len(group)
    per = W // rows

    def kernel(where_ref, mid_ref, norm_ref, *refs):
        pieces, refs = refs[:sources], refs[sources:]
        out_ref, act_ref, gp_ref, up_ref, down_ref, sem = refs
        fill_weights(pl.program_id(0), where_ref, pieces, mlp_targets(up_ref, down_ref, rows), sem)
        mid = mid_ref[...]
        xhat, _ = norm_parts(mid)
        c = (xhat * norm_ref[2:3, :] + norm_ref[3:4, :]).astype(BF16)
        total = mid

        def upper(b):
            cols = slice(step * (b % 2), step * (b % 2) + step)
            return dense(c, up_ref[b // 2, :, cols])

        def lower(act, b):
            few = per // 2
            return dense(act, down_ref[few * b : few * b + few].reshape(step, D))

        ahead = upper(0)
        for b in range(FF // step):
            cols = slice(step * b, step * b + step)
            u = ahead
            if b + 1 < FF // step:
                ahead = upper(b + 1)
            if b > 0:
                total = total + lower(last, b - 1)
            act, slope = gelu_pair(u)
            last = act.astype(BF16)
            act_ref[:, cols] = last
            gp_ref[:, cols] = slope.astype(BF16)
        out_ref[...] = total + lower(last, FF // step - 1)

    def row(width):
        return pl.BlockSpec((tall, width), lambda i: (i, 0))

    return pl.pallas_call(
        kernel,
        grid=(n // tall,),
        in_specs=[SMEM, row(D), whole((4, D))] + [ANY] * sources,
        out_specs=[row(D), row(FF), row(FF)],
        out_shape=[
            jax.ShapeDtypeStruct((n, D), F32),
            pltpu.HBM((n, FF), BF16),
            pltpu.HBM((n, FF), BF16),
        ],
        scratch_shapes=[
            pltpu.VMEM((4, D, W), BF16),
            pltpu.VMEM((FF // rows, rows, D), BF16),
            pltpu.SemaphoreType.DMA((copies_of(group),)),
        ],
        compiler_params=params(),
        cost_estimate=cost(4 * n * D * FF, n * D * 24, n * FF * 2),
        name="mlp_fwd",
    )(where, in_hbm(mid), norms, *group)


def mlp_bwd(place, where, dz, mid, gp, norms, group):
    rows = D // place.shards
    n = mid.shape[0]
    sources = len(group)
    per = W // rows

    def kernel(where_ref, dz_ref, mid_ref, gp_ref, norm_ref, *refs):
        pieces, refs = refs[:sources], refs[sources:]
        dmid_ref, dh_ref, du_ref, c_ref, dm_ref, dn_ref, up_ref, down_ref, sem = refs
        i = pl.program_id(0)
        fill_weights(i, where_ref, pieces, mlp_targets(up_ref, down_ref, rows), sem)
        dm = dz_ref[...].astype(BF16)
        dm_ref[...] = dm

        def upper(b):
            return dense_nt(dm, down_ref[per * b : per * b + per].reshape(W, D))

        dc = jnp.zeros((LEN, D), F32)
        ahead = upper(0)
        for b in range(FF // W):
            cols = slice(W * b, W * b + W)
            da = ahead
            if b + 1 < FF // W:
                ahead = upper(b + 1)
            if b > 0:
                dc = dc + dense_nt(last, up_ref[b - 1])
            last = (gp_ref[:, cols].astype(F32) * da).astype(BF16)
            du_ref[:, cols] = last
        dc = dc + dense_nt(last, up_ref[FF // W - 1])
        xhat, rstd = norm_parts(mid_ref[...])
        gain = norm_ref[2:3, :]
        c_ref[...] = (xhat * gain + norm_ref[3:4, :]).astype(BF16)
        dmid = dz_ref[...] + norm_back(xhat, rstd, dc, gain)
        dmid_ref[...] = dmid
        dh_ref[...] = dmid.astype(BF16)

        @pl.when(i == 0)
        def _():
            dn_ref[...] = jnp.zeros_like(dn_ref)

        dn_ref[0:1, :] += jnp.sum(dc * xhat, 0, keepdims=True)
        dn_ref[1:2, :] += jnp.sum(dc, 0, keepdims=True)

    def row(width):
        return pl.BlockSpec((LEN, width), lambda i: (i, 0))

    return pl.pallas_call(
        kernel,
        grid=(n // LEN,),
        in_specs=[SMEM, row(D), row(D), row(FF), whole((4, D))] + [ANY] * sources,
        out_specs=[row(D), row(D), row(FF), row(D), row(D), whole((8, D))],
        out_shape=[
            jax.ShapeDtypeStruct((n, D), F32),
            jax.ShapeDtypeStruct((n, D), BF16),
            pltpu.HBM((n, FF), BF16),
            jax.ShapeDtypeStruct((n, D), BF16),
            jax.ShapeDtypeStruct((n, D), BF16),
            jax.ShapeDtypeStruct((8, D), F32),
        ],
        scratch_shapes=[
            pltpu.VMEM((4, D, W), BF16),
            pltpu.VMEM((FF // rows, rows, D), BF16),
            pltpu.SemaphoreType.DMA((copies_of(group),)),
        ],
        compiler_params=params(),
        cost_estimate=cost(4 * n * D * FF, n * D * 32),
        name="mlp_bwd",
    )(where, dz, in_hbm(mid), in_hbm(gp), norms, *group)


def attn_bwd(place, where, dmid, dh, x, qkv, pt, ot, norms, group):
    rows = D // place.shards
    n = x.shape[0]
    seqs = n // LEN
    sources = len(group)

    def kernel(where_ref, dmid_ref, dh_ref, x_ref, qkv_ref, pt_ref, ot_ref, norm_ref, *refs):
        pieces, refs = refs[:sources], refs[sources:]
        dx_ref, dqkv_ref, a_ref, dn_ref, w_ref, dqt_ref, sem = refs
        i = pl.program_id(0)
        fill_weights(i, where_ref, pieces, attn_targets(w_ref, rows), sem)
        spans = [slice(None)]
        do, delta, kt = [], [], []
        for s, span in enumerate(spans):
            do.append(dense_nt(dh_ref[span], w_ref[3]).astype(BF16))
            along = do[s].T.astype(F32) * ot_ref[s].astype(F32)
            delta.append([jnp.sum(along[head_of(h), :], axis=0, keepdims=True) for h in range(H)])
            kt.append(qkv_ref[span, D : 2 * D].T)

        def first(s, h):
            doh = head_lanes(do[s], h)
            v = qkv_ref[spans[s], 2 * D + 128 * (h // 2) : 2 * D + 128 * (h // 2) + 128]
            return dense_nt(v, doh), dense(pt_ref[s, h], doh)

        halves = {}

        def second(s, h, dst, dv):
            q = qkv_ref[spans[s], pair_of(h)]
            lane = lax.broadcasted_iota(jnp.int32, (LEN, 128), 1)
            own = (lane < DH) if h % 2 == 0 else (lane >= DH)
            dk = dense(dst, jnp.where(own, q, 0))
            dqt_ref[s, head_of(h), :] = (dense(kt[s][head_of(h), :], dst) * DH**-0.5).astype(BF16)
            if h % 2 == 0:
                halves[s] = (dk, dv)
                return
            at = 128 * (h // 2)
            dk, dv = dk + halves[s][0], dv + halves[s][1]
            dqkv_ref[spans[s], D + at : D + at + 128] = dk.astype(BF16)
            dqkv_ref[spans[s], 2 * D + at : 2 * D + at + 128] = dv.astype(BF16)

        items = [(s, h) for h in range(H) for s in range(1)]
        ahead = first(*items[0])
        last = None
        for at, (s, h) in enumerate(items):
            dpt, dv = ahead
            if at + 1 < len(items):
                ahead = first(*items[at + 1])
            if last is not None:
                second(*last)
            dst = (pt_ref[s, h].astype(F32) * (dpt - delta[s][h])).astype(BF16)
            last = (s, h, dst, dv)
        second(*last)

        @pl.when(i == 0)
        def _():
            dn_ref[...] = jnp.zeros_like(dn_ref)

        gain = norm_ref[0:1, :]
        for s, span in enumerate(spans):
            da = dense_nt(dqkv_ref[span, D : 2 * D], w_ref[1])
            da = da + dense_nt(dqkv_ref[span, 2 * D :], w_ref[2])
            dq = dqt_ref[s].T
            dqkv_ref[span, :D] = dq
            da = da + dense_nt(dq, w_ref[0])
            xhat, rstd = norm_parts(x_ref[span])
            a_ref[span] = (xhat * gain + norm_ref[1:2, :]).astype(BF16)
            dx_ref[span] = dmid_ref[span] + norm_back(xhat, rstd, da, gain)
            dn_ref[0:1, :] += jnp.sum(da * xhat, 0, keepdims=True)
            dn_ref[1:2, :] += jnp.sum(da, 0, keepdims=True)

    def row(width):
        return pl.BlockSpec((LEN, width), lambda i: (i, 0))

    return pl.pallas_call(
        kernel,
        grid=(seqs,),
        in_specs=[
            SMEM,
            row(D),
            row(D),
            row(D),
            row(3 * D),
            pl.BlockSpec((1, H, LEN, LEN), lambda i: (i, 0, 0, 0)),
            pl.BlockSpec((1, D, LEN), lambda i: (i, 0, 0)),
            whole((4, D)),
        ]
        + [ANY] * sources,
        out_specs=[row(D), row(3 * D), row(D), whole((8, D))],
        out_shape=[
            jax.ShapeDtypeStruct((n, D), F32),
            jax.ShapeDtypeStruct((n, 3 * D), BF16),
            jax.ShapeDtypeStruct((n, D), BF16),
            jax.ShapeDtypeStruct((8, D), F32),
        ],
        scratch_shapes=[
            pltpu.VMEM((4, D, W), BF16),
            pltpu.VMEM((1, D, LEN), BF16),
            pltpu.SemaphoreType.DMA((copies_of(group),)),
        ],
        compiler_params=params(),
        cost_estimate=cost(2 * n * D * (4 * D + 5 * LEN), n * D * 32),
        name="attn_bwd",
    )(where, dmid, dh, x, in_hbm(qkv), in_hbm(pt), in_hbm(ot), norms, *group)


def head_step(place, x, target, maskf, head, norms, count):
    n = x.shape[0]

    def kernel(x_ref, target_ref, mask_ref, head_ref, norm_ref, dx_ref, loss_ref, gh_ref, dn_ref):
        i = pl.program_id(0)
        xhat, rstd = norm_parts(x_ref[...])
        gain = norm_ref[0:1, :]
        y = (xhat * gain + norm_ref[1:2, :]).astype(BF16)
        masked = mask_ref[...]
        err = (dense_nt(y, head_ref[...]) - target_ref[...].astype(F32)) * masked
        dpred = (err * (2.0 / (P_SIZE * count))).astype(BF16)
        dy = dense(dpred, head_ref[...])
        dx_ref[...] = norm_back(xhat, rstd, dy, gain)

        @pl.when(i == 0)
        def _():
            loss_ref[...] = jnp.zeros_like(loss_ref)
            gh_ref[...] = jnp.zeros_like(gh_ref)
            dn_ref[...] = jnp.zeros_like(dn_ref)

        loss_ref[...] += jnp.sum(err * err, 0, keepdims=True)
        gh_ref[...] += dense_tn(dpred, y)
        dn_ref[0:1, :] += jnp.sum(dy * xhat, 0, keepdims=True)
        dn_ref[1:2, :] += jnp.sum(dy, 0, keepdims=True)

    def row(width):
        return pl.BlockSpec((LEN, width), lambda i: (i, 0))

    return pl.pallas_call(
        kernel,
        grid=(n // LEN,),
        in_specs=[row(D), row(P_SIZE), row(1), whole((P_SIZE, D)), whole((2, D))],
        out_specs=[row(D), whole((1, P_SIZE)), whole((P_SIZE, D)), whole((8, D))],
        out_shape=[
            jax.ShapeDtypeStruct((n, D), F32),
            jax.ShapeDtypeStruct((1, P_SIZE), F32),
            jax.ShapeDtypeStruct((P_SIZE, D), F32),
            jax.ShapeDtypeStruct((8, D), F32),
        ],
        compiler_params=params(),
        cost_estimate=cost(6 * n * D * P_SIZE, n * D * 8),
        name="head_step",
    )(x, target, maskf, head, norms)


def put_block(core, block, lead, send_ref, keep_ref, at):
    rows = block.shape[0]
    halves = block.reshape(lead + (2, rows // (2 * lead_size(lead)), W))
    first, second = halves[..., 0, :, :], halves[..., 1, :, :]
    keep_ref[at] = jnp.where(core == 0, first, second)
    send_ref[at] = jnp.where(core == 0, second, first)


def lead_size(lead):
    size = 1
    for n in lead:
        size *= n
    return size


def grad_mlp(place, where, c, du, act, dm, ot, dh):
    shards = place.shards
    rows = D // shards
    n = c.shape[0]
    seqs = n // LEN
    wide = 2 * W
    steps = FF // wide
    per = shards // steps
    blocks = 9

    def kernel(where_ref, c_ref, du_ref, act_ref, dm_ref, ot_ref, dh_ref, send_ref, keep_ref, ct_ref):
        i = pl.program_id(0)
        core = where_ref[1]

        @pl.when(i == 0)
        def _():
            ct_ref[...] = c_ref[...].T

        @pl.when(i < steps)
        def _():
            block = dense(ct_ref[...], du_ref[...]).astype(BF16)
            for b in range(wide // W):
                at = (slice(None), i * (wide // W) + b)
                put_block(core, block[:, W * b : W * b + W], (shards,), send_ref, keep_ref, at)

        @pl.when((i >= steps) & (i < 2 * steps))
        def _():
            block = dense_tn(act_ref[...], dm_ref[...]).astype(BF16)
            at = (pl.ds((i - steps) * per, per), slice(4, 8))
            put_block(core, block, (per, 4), send_ref, keep_ref, at)

        @pl.when(i == 2 * steps)
        def _():
            total = dense(ot_ref[0], dh_ref[:LEN, :])
            for s in range(1, seqs):
                total = total + dense(ot_ref[s], dh_ref[LEN * s : LEN * s + LEN, :])
            put_block(core, total.astype(BF16), (shards,), send_ref, keep_ref, (slice(None), 8))

    shape = (shards, blocks, rows // 2, W)
    return pl.pallas_call(
        kernel,
        grid=(2 * steps + 1,),
        in_specs=[
            SMEM,
            whole((n, D)),
            pl.BlockSpec((n, wide), lambda i: (0, jnp.minimum(i, steps - 1))),
            pl.BlockSpec((n, wide), lambda i: (0, jnp.clip(i - steps, 0, steps - 1))),
            whole((n, D)),
            whole((seqs, D, LEN)),
            whole((n, D)),
        ],
        out_specs=[whole(shape), whole(shape)],
        scratch_shapes=[pltpu.VMEM((D, n), BF16)],
        out_shape=[jax.ShapeDtypeStruct(shape, BF16)] * 2,
        compiler_params=params(),
        cost_estimate=cost(4 * n * D * FF, n * (4 * D + 4 * FF) + 4 * D * FF),
        name="grad_mlp",
    )(where, c, in_hbm(du), in_hbm(act), dm, in_hbm(ot), dh)


def grad_qkv(place, where, a, dqkv, small=()):
    shards = place.shards
    rows = D // shards
    half = rows // 2
    n = a.shape[0]
    blocks = 3 + bool(small)
    extra = len(small)

    def kernel(where_ref, a_ref, dqkv_ref, *refs):
        small_refs, refs = refs[:extra], refs[extra:]
        send_ref, keep_ref, at_ref = refs[:3]
        i = pl.program_id(0)

        @pl.when(i == 0)
        def _():
            at_ref[...] = a_ref[...].T

        @pl.when(i < 3)
        def _():
            block = dense(at_ref[...], dqkv_ref[...]).astype(BF16)
            put_block(where_ref[1], block, (shards,), send_ref, keep_ref, (slice(None), i))

        if extra:
            table_ref = refs[3]
            inputs_ref, dx_ref, head_ref = small_refs[:3]

            @pl.when(i == 3)
            def _():
                dx = dx_ref[...]
                table_ref[:P_SIZE] = dense_tn(inputs_ref[...], dx.astype(BF16)).astype(BF16)
                table_ref[P_SIZE : 2 * P_SIZE] = head_ref[...].astype(BF16)
                total = dx[:LEN]
                for s in range(1, n // LEN):
                    total = total + dx[s * LEN : s * LEN + LEN]
                table_ref[2 * P_SIZE : 2 * P_SIZE + LEN] = total.astype(BF16)
                norms = jnp.concatenate(
                    [ref[0:2, :] for ref in small_refs[3:]]
                    + [jnp.zeros((16 - 2 * (extra - 3), D), F32)],
                    0,
                )
                start = 2 * P_SIZE + LEN
                table_ref[start : start + 16] = norms.astype(BF16)
                table_ref[start + 16 :] = jnp.zeros((SMALL - start - 16, D), BF16)
                for core in range(2):

                    @pl.when(where_ref[1] == core)
                    def _(core=core):
                        for h in range(2):
                            out_ref = keep_ref if h == core else send_ref
                            for j in range(shards):
                                for q in range(W // rows):
                                    first = h * (SMALL // 2) + q * half
                                    value = table_ref[first : first + half, j * rows : j * rows + rows]
                                    out_ref[j, 3, :, q * rows : q * rows + rows] = value

    shape = (shards, blocks, half, W)
    return pl.pallas_call(
        kernel,
        grid=(blocks,),
        in_specs=[SMEM, whole((n, D)), pl.BlockSpec((n, W), lambda i: (0, jnp.minimum(i, 2)))]
        + [whole(x.shape) for x in small],
        out_specs=[whole(shape), whole(shape)],
        scratch_shapes=[pltpu.VMEM((D, n), BF16)] + [pltpu.VMEM((SMALL, D), BF16)] * bool(small),
        out_shape=[jax.ShapeDtypeStruct(shape, BF16)] * 2,
        compiler_params=params(),
        cost_estimate=cost(6 * n * D * D, n * 8 * D + 6 * D * D),
        name="grad_qkv",
    )(where, a, dqkv, *small)


def adam(weight, first, second, tenth, rate):
    scale = (1 - BETA_ONE**STEP_COUNT) / rate
    first = BETA_ONE * first + tenth
    second = BETA_TWO * second + tenth * ((1 - BETA_TWO) / (1 - BETA_ONE) ** 2) * tenth
    spread = second * (scale * scale / (1 - BETA_TWO**STEP_COUNT))
    step = first * (1.0 / (spread * lax.rsqrt(spread) + ADAM_EPS * scale))
    return (weight * (1 - rate * DECAY) - step, first, second)


def fetch(arrays, where):
    def kernel(where_ref, *refs):
        sem = refs[-1]
        count = len(arrays)
        copies = [
            pltpu.make_async_copy(refs[n], refs[count + n], sem.at[n]) for n in range(count)
        ]
        for copy in copies:
            copy.start()
        for copy in copies:
            copy.wait()

    return pl.pallas_call(
        kernel,
        in_specs=[SMEM] + [pl.BlockSpec(memory_space=pltpu.HBM)] * len(arrays),
        out_specs=[pl.BlockSpec(memory_space=pltpu.VMEM)] * len(arrays),
        out_shape=[pltpu.VMEM(x.shape, x.dtype) for x in arrays],
        scratch_shapes=[pltpu.SemaphoreType.DMA((len(arrays),))],
        compiler_params=params(4),
        name="fetch",
    )(where, *map(in_hbm, arrays))


def adam_step(place, where, both, count, state, small, grads):
    rows = D // place.shards
    half = rows // 2
    few = half // 2
    flat = [x for group in state for x in group]
    tiny = [x for group in small for x in group]

    def spec(x):
        if x.ndim == 4:
            return pl.BlockSpec((None, 4, few, W), lambda i, h, q: (i, 0, 2 * h + q, 0))
        return pl.BlockSpec((None, few, x.shape[2]), lambda i, h, q: (i, 2 * h + q, 0))

    gflat, spots = [], []
    for layer in grads:
        spots.append([])
        for pieces, first, bit in layer:
            known = [n for n, x in enumerate(gflat) if x is pieces[0]]
            spots[-1].append((known[0] if known else len(gflat), len(pieces), first, bit))
            gflat += [] if known else list(pieces)
    total = len(flat) + len(tiny)

    def kernel(where_ref, *refs):
        both_refs, refs = refs[: len(both)], refs[len(both) :]
        grad_refs, refs = refs[: len(gflat)], refs[len(gflat) :]
        ins, outs, table_ref = refs[:total], refs[total : 2 * total], refs[-1]
        loss_ref, norm_ref = refs[2 * total : 2 * total + 2]
        layer, h, q = pl.program_id(0), pl.program_id(1), pl.program_id(2)
        values = [ref[...] for ref in both_refs]
        sums = jnp.zeros((1, 2), F32)
        for j in range(len(values)):
            sums = sums + select_of(values, where_ref[0] ^ j)
        norm = jnp.sqrt(sums[:, 1:2])
        loss_ref[...] = sums[:, 0:1] / count
        norm_ref[...] = norm
        scale = (1 - BETA_ONE) * CLIP / jnp.maximum(norm, CLIP)
        own = where_ref[1] == h

        def update(n, at, grad, rate):
            got = adam(ins[3 * n][at], ins[3 * n + 1][at], ins[3 * n + 2][at], grad, rate)
            for k in range(3):
                outs[3 * n + k][at] = got[k]

        part = pl.ds(pl.multiple_of(q * few, few), few)

        def run(layer):
            def grad(group, b):
                base, count, first, bit = spots[layer][group]
                refs = grad_refs[base : base + count]
                if count == 2:
                    got = jnp.where(own, refs[0][first + b, part], refs[1][first + b, part])
                else:
                    close = jnp.where(own, refs[0][first + b], refs[1][first + b])
                    away = jnp.where(own, refs[2][first + b], refs[3][first + b])
                    got = jnp.where(where_ref[bit] == q, close, away)
                return got.astype(F32) * scale

            for b in range(3):
                update(0, (slice(None), slice(W * b, W * b + W)), grad(0, b), RATE)
            update(1, (slice(None), slice(None)), grad(1, 8), RATE)
            for b in range(4):
                update(2, (slice(None), slice(W * b, W * b + W)), grad(1, b), RATE)
                update(3, (b,), grad(1, 4 + b), RATE)

        for i in range(L):

            @pl.when(layer == i)
            def _(i=i):
                run(i)

        @pl.when((layer == 0) & (h == 0) & (q == 0))
        def _():
            base, _, at, _ = spots[0][0]
            mine, other = grad_refs[base][at + 3], grad_refs[base + 1][at + 3]
            first = where_ref[1] == 0
            for n, block in enumerate((jnp.where(first, mine, other), jnp.where(first, other, mine))):
                for k in range(W // rows):
                    start = n * (SMALL // 2) + k * half
                    table_ref[start : start + half] = (
                        block[:, k * rows : k * rows + rows].astype(F32) * scale
                    )
            count = 2 * P_SIZE + LEN
            update(4, (slice(None), slice(None)), table_ref[:count], TABLE_RATE)
            norms = small[1][0].shape[0]
            update(5, (slice(None), slice(None)), table_ref[count : count + norms], TABLE_RATE)

    out = pl.pallas_call(
        kernel,
        grid=(L, 2, 2),
        in_specs=[SMEM]
        + [whole((1, 2)) for _ in both]
        + [whole(g.shape) for g in gflat]
        + [spec(x) for x in flat]
        + [whole(x.shape) for x in tiny],
        out_specs=[spec(x) for x in flat] + [whole(x.shape) for x in tiny] + [whole((1, 1))] * 2,
        out_shape=[pltpu.HBM(x.shape, F32) for x in flat + tiny]
        + [jax.ShapeDtypeStruct((1, 1), F32)] * 2,
        scratch_shapes=[pltpu.VMEM((SMALL, rows), F32)],
        compiler_params=params(20),
        cost_estimate=cost(20 * L * 12 * rows * W, 24 * L * 12 * rows * W),
        name="adam_step",
    )(where, *both, *gflat, *flat, *map(in_hbm, tiny))
    news = [tuple(out[3 * n : 3 * n + 3]) for n in range(len(state) + len(small))]
    return out[-2].reshape(()), out[-1].reshape(()), news


def on_device(
    series,
    mask,
    qkv_w,
    out_w,
    up_w,
    down_w,
    patch_maps,
    norm_params,
    qkv_m,
    out_m,
    up_m,
    down_m,
    patch_m,
    norm_m,
    qkv_v,
    out_v,
    up_v,
    down_v,
    patch_v,
    norm_v,
):
    place = Place()
    shards = place.shards
    rows = D // shards
    half = rows // 2
    seqs = series.shape[0]
    count = MASKED * seqs * shards * place.replicas
    shard_bits = [(place.shard >> bit) & 1 for bit in bits_of(shards)]
    chip_bits = [(place.chip >> bit) & 1 for bit in bits_of(place.chips)]
    where = jnp.stack([place.shard, place.core] + shard_bits + chip_bits).astype(jnp.int32)
    chip = 2 + len(shard_bits)

    small_now = [patch_maps, norm_params]
    packs = [
        (
            pack(place, where, i, [qkv_w, out_w], [], small_now if i == 0 else []),
            pack(place, where, i, [up_w], [down_w], []),
        )
        for i in range(L)
    ]

    def group_of(packed, ours, theirs):
        return [packed[0]] + ours + [theirs]

    attn_groups = [None] * L
    mlp_groups = [None] * L
    target = series.reshape(seqs * LEN, P_SIZE)
    maskf = mask.reshape(seqs * LEN, 1).astype(F32)
    ours = gather_shards(place, packs[0][0][1])
    theirs = gather_cores(place, ours, *[p[1] for pair in packs for p in pair], target, maskf)
    attn_groups[0] = group_of(packs[0][0], ours, theirs)
    mine = gate(packs[0][1][1], *ours)
    ours_mlp = gather_shards(place, mine)

    x, inputs, head, norms_all = embed_step(place, where, target, gate(maskf, mine), attn_groups[0])
    saved = []
    for index in range(L):
        norms = norms_all[4 * index : 4 * index + 4]
        held = in_hbm(x) if index == 0 else x
        mid, qkv, pt, ot = attn_fwd(place, where, held, norms, attn_groups[index])
        held = mid
        if index + 1 < L:
            got = gates(ours_mlp, mid)
            mine = gate(packs[index + 1][0][1], *got)
            ours_attn = gather_shards(place, mine)
            held = gate(mid, mine)
        theirs = gather_cores(place, ours_mlp, mid)
        mlp_groups[index] = group_of(packs[index][1], ours_mlp, theirs)
        pieces = mlp_groups[index] if index == 0 else [in_hbm(x) for x in mlp_groups[index]]
        y, act, gp = mlp_fwd(place, where, held, norms, pieces)
        if index + 1 < L:
            got = gates(ours_attn, y)
            theirs = gather_cores(place, got)
            attn_groups[index + 1] = group_of(packs[index + 1][0], ours_attn, theirs)
            mine = gate(packs[index + 1][1][1], *got)
            ours_mlp = gather_shards(place, mine)
            y = gate(y, mine)
        saved.append((x, mid, qkv, pt, ot, act, gp, norms))
        x = y

    grad, loss, g_head, dn_final = head_step(
        place, x, target, maskf, head, norms_all[4 * L : 4 * L + 2], count
    )
    loss = (jnp.sum(loss) / P_SIZE).reshape(1, 1)

    norm_grads = {}

    def backward_mlp(index, grad):
        x, mid, qkv, pt, ot, act, gp, norms = saved[index]
        dmid, dh, du, c, dm, dn = mlp_bwd(
            place, where, grad, mid, gp, norms, mlp_groups[index]
        )
        norm_grads[index, 1] = dn
        return dmid, dh, du, c, dm

    def backward_attn(index, dmid, dh):
        x, mid, qkv, pt, ot, act, gp, norms = saved[index]
        grad, dqkv, a, dn = attn_bwd(
            place, where, dmid, dh, x, qkv, pt, ot, norms, attn_groups[index]
        )
        norm_grads[index, 0] = dn
        return grad, dqkv, a

    def grads_mlp(index, du, c, dm, dh):
        return grad_mlp(place, where, c, du, saved[index][5], dm, saved[index][4], dh)

    one, two = Flow(place, True, True), Flow(place, True)
    ahead, end = Flow(place, False), Flow(place, False)

    def advance(flows, *after):
        token = sum_round(where, flows, *after)
        for flow in flows:
            flow.launch()
        return token

    loss = loss + place.to_core(loss)
    dmid, dh, du, c, dm = backward_mlp(1, grad)
    token = one.begin(*grads_mlp(1, du, c, dm, dh), (0, 5, 0), (5, 4, 1))
    grad, dqkv_one, a_one = backward_attn(1, gate(dmid, token), dh)
    token = advance([one], grad)
    dmid, dh, du, c, dm = backward_mlp(0, gate(grad, token))
    token = advance([one], dmid)
    token = two.begin(*grads_mlp(0, du, gate(c, token), dm, dh), (0, 5, 0), (5, 4, 1))
    token = advance([one], token)
    token = ahead.begin(*grad_qkv(place, where, gate(a_one, token), dqkv_one), (0, 3, 1))
    token = advance([two], token)
    grad, dqkv, a = backward_attn(0, gate(dmid, token), dh)
    token = sum_round(where, [one, two, ahead], grad)
    small = [inputs, grad, g_head]
    small += [norm_grads[i, k] for i in range(L) for k in range(2)] + [dn_final]
    token = end.begin(*grad_qkv(place, where, gate(a, token), dqkv, small), (0, 4, 0))
    one.launch()
    two.launch()
    ahead.launch()
    while not one.last():
        token = advance([one], token)
    token = sum_round(where, [one, two, end], token)
    end.launch()
    end.join(ahead)
    two.launch()
    one.to_neighbours()
    hops = bits_of(place.chips)

    def pass_loss(loss, token):
        if not hops:
            return loss
        return loss + place.to_chip(gate(loss, token), 1 << hops.pop(0))

    while end.step < end.steps - 2:
        loss = pass_loss(loss, token)
        token = sum_round(where, [end] + ([two] if not two.last() else []), token, loss)
        end.launch()
        if two.step == two.steps - 1:
            break
        if not two.last():
            two.launch()
    behind = not two.last()
    while end.step < end.steps - 1:
        loss = pass_loss(loss, token)
        token = advance([end], token, *one.pieces, loss)
    one.to_last()
    if behind:
        two.launch()
    while hops:
        loss = pass_loss(loss, token)
    state = [(qkv_w, qkv_m, qkv_v), (out_w, out_m, out_v), (up_w, up_m, up_v)]
    state.append(tuple(x.reshape(L, 4, rows, W) for x in (down_w, down_m, down_v)))
    token = sum_round(where, [end, two], token, loss)
    end.launch()
    two.to_neighbours()
    near = fetch([x for group in state for x in group], gate(where, token))
    state = [tuple(near[3 * n : 3 * n + 3]) for n in range(len(state))]
    token = sum_round(where, [end], token, *two.pieces, near[0])
    end.to_neighbours()
    two.to_last()
    grads = [
        [(end.pieces, 3, 0), (two.pieces, 0, chip + two.chip_bits[0])],
        [(end.pieces, 0, 0), (one.pieces, 0, chip + one.chip_bits[0])],
    ]
    done_one, done_two, done_last = one.pieces, two.pieces, end.pieces

    both = square_sum(done_one + done_two + done_last, loss)
    both = [both] + [place.to_shard(both, k) for k in range(1, shards)]

    small = [(patch_maps, patch_m, patch_v), (norm_params, norm_m, norm_v)]
    loss, grad_norm, results = adam_step(place, where, both, count, state, small, grads)
    results[3] = tuple(x.reshape(down_w.shape) for x in results[3])
    news = tuple(r[0] for r in results)
    new_m = tuple(r[1] for r in results)
    new_v = tuple(r[2] for r in results)
    return (loss, grad_norm) + news + new_m + new_v


def solution(mesh):
    batch = P(("shard", "replica"), None)
    stack = P(None, "shard", None)
    flat = P(None, "shard")
    state = (stack, stack, stack, stack, flat, flat)
    return jax.shard_map(
        on_device,
        mesh=mesh,
        in_specs=(batch, batch) + state * 3,
        out_specs=(P(), P()) + state * 3,
        check_vma=False,
    )
```

```python
import jax
import jax.numpy as jnp
from jax import lax
from jax.experimental import pallas as pl
from jax.experimental.pallas import tpu as pltpu
from jax.sharding import PartitionSpec as P

D = 512
H = 8
DH = 64
FF = 2048
P_SIZE = 64
LEN = 256
L = 2
MASKED = 102

EPS = 1e-05
CLIP = 0.001
RATE = 0.05
TABLE_RATE = 0.3
BETA_ONE = 0.9
BETA_TWO = 0.999
ADAM_EPS = 1e-08
DECAY = 0.1
STEP_COUNT = 10

W = 512
SMALL = 512
NORMS_LOW = 2 * P_SIZE + LEN + 16
F32 = jnp.float32
BF16 = jnp.bfloat16


def dense(left, right):
    return jnp.dot(left, right, preferred_element_type=F32)


def dense_tn(left, right):
    return lax.dot_general(left, right, (((0,), (0,)), ((), ())), preferred_element_type=F32)


def dense_nt(left, right):
    return lax.dot_general(left, right, (((1,), (1,)), ((), ())), preferred_element_type=F32)


def layer_norm(x, gain, bias):
    center = x - jnp.mean(x, -1, keepdims=True)
    spread = jnp.mean(center * center, -1, keepdims=True)
    return center * lax.rsqrt(spread + EPS) * gain + bias


def params(mib=30):
    return pltpu.CompilerParams(vmem_limit_bytes=mib * 2**20)


def cost(flops, data, trans=0):
    return pl.CostEstimate(
        flops=int(30 * flops), bytes_accessed=int(30 * data), transcendentals=int(30 * trans)
    )


def whole(shape):
    return pl.BlockSpec(shape, lambda *_: (0,) * len(shape))


def in_hbm(x):
    return pltpu.with_memory_space_constraint(x, pltpu.HBM)


ANY = pl.BlockSpec(memory_space=pl.ANY)
SMEM = pl.BlockSpec(memory_space=pltpu.SMEM)


def permute(x, axis, mask, size):
    return lax.ppermute(x, axis, [(i, i ^ mask) for i in range(size)])


def pick(x, index):
    return lax.dynamic_index_in_dim(x, index, 0, keepdims=False)


class Place:
    def __init__(self):
        self.shards = lax.axis_size("shard")
        self.replicas = lax.axis_size("replica")
        self.chips = self.replicas // 2
        self.shard = lax.axis_index("shard")
        replica = lax.axis_index("replica")
        self.core = replica % 2
        self.chip = replica // 2

    def to_core(self, x):
        return permute(x, "replica", 1, self.replicas)

    def to_shard(self, x, mask):
        return permute(x, "shard", mask, self.shards)

    def to_chip(self, x, mask):
        return permute(x, "replica", 2 * mask, self.replicas)


def gate(x, *after):
    return lax.optimization_barrier((x,) + after)[0]


def gather_shards(place, mine):
    return [place.to_shard(mine, mask) for mask in range(1, place.shards)]


def gather_cores(place, ours, *after):
    items = gates(ours, *after)
    return place.to_core(stack(items) if items[0].shape[0] % 4 == 0 else jnp.stack(items))


def stack(items):
    def kernel(*refs):
        for n, ref in enumerate(refs[:-1]):
            refs[-1][n] = ref[...]

    few, rows, width = items[0].shape
    part = pl.BlockSpec((few // 2, rows, width), lambda i: (i, 0, 0))
    return pl.pallas_call(
        kernel,
        grid=(2,),
        in_specs=[part] * len(items),
        out_specs=pl.BlockSpec((len(items), few // 2, rows, width), lambda i: (0, i, 0, 0)),
        out_shape=jax.ShapeDtypeStruct((len(items), few, rows, width), items[0].dtype),
        compiler_params=params(12),
        cost_estimate=cost(10**5, 10**5),
        name="stack",
    )(*items)


def gates(items, *after):
    return list(lax.optimization_barrier(tuple(items) + after)[: len(items)])


def select_of(items, index):
    out = items[0]
    for k in range(1, len(items)):
        out = jnp.where(index == k, items[k], out)
    return out


def bits_of(size):
    return list(range(size.bit_length() - 1))


def total_of(values):
    total = values[0].astype(F32)
    for value in values[1:]:
        total = total + value.astype(F32)
    return total


def combine(where, jobs, name):
    lanes = W // 2
    arrays, leads, plans, shapes = [], [], [], []

    def number(array, lead):
        for n, known in enumerate(arrays):
            if known is array:
                return n
        arrays.append(array)
        leads.append(lead)
        return len(arrays) - 1

    for segments, lead, cut, bit in jobs:
        plans.append([[(number(a, lead), f, b) for a, f, b in parts] for parts in segments])
        blocks = sum(parts[0][2] for parts in segments)
        rows = segments[0][0][0].shape[-2]
        if cut is None:
            shapes.append(lead + (blocks, rows, W))
        elif cut == "rows":
            shapes += [lead + (blocks, rows // 2, W)] * 2
        else:
            shapes += [lead[:cut] + lead[cut + 1 :] + (blocks, rows, W)] * 2
    arrays = [a.reshape(lead + a.shape[-3:]) for a, lead in zip(arrays, leads)]

    def block(shape):
        zeros = (0,) * (len(shape) - 1)
        return pl.BlockSpec(shape[:-1] + (lanes,), lambda i: zeros + (i,))

    def kernel(where_ref, *refs):
        ins, outs = refs[: len(arrays)], list(refs[len(arrays) :])
        for (segments, lead, cut, bit), plan in zip(jobs, plans):
            some = (slice(None),) * len(lead)
            fewer = (slice(None),) * (len(lead) - (cut is not None and cut != "rows"))
            if cut is None:
                targets = [(outs.pop(0), None)]
            else:
                value = where_ref[bit]
                targets = [(outs.pop(0), 1 - value), (outs.pop(0), value)]
            for out_ref, at in targets:
                start = 0
                for parts in plan:
                    got = []
                    for n, f, b in parts:
                        index = some
                        if cut is not None and cut != "rows":
                            index = some[:cut] + (at,) + some[cut + 1 :]
                        index += (slice(f, f + b),)
                        if cut == "rows":
                            few = ins[n].shape[-2] // 2
                            index += (pl.ds(pl.multiple_of(at * few, few), few),)
                        got.append(ins[n][index])
                    out_ref[fewer + (slice(start, start + parts[0][2]),)] = total_of(got).astype(BF16)
                    start += parts[0][2]

    size = sum(a.size for a in arrays) * 4
    return pl.pallas_call(
        kernel,
        grid=(2,),
        in_specs=[SMEM] + [block(a.shape) for a in arrays],
        out_specs=[block(s) for s in shapes],
        out_shape=[jax.ShapeDtypeStruct(s, BF16) for s in shapes],
        compiler_params=params(12),
        cost_estimate=cost(size, size),
        name=name,
    )(where, *arrays)


class Flow:
    def __init__(self, place, spread, far_first=False):
        self.place, self.spread = place, spread
        self.chip_bits = bits_of(place.chips)[:: -1 if far_first else 1]
        self.bits = bits_of(place.shards)
        self.steps = len(self.bits) + len(bits_of(place.chips))
        self.step = 0
        self.inputs = []
        self.ranges = []

    def begin(self, send, keep, *ranges):
        other = self.place.to_core(send)
        for first, blocks, order in ranges:
            self.ranges.append((len(self.inputs), first, blocks, order))
        self.inputs += [keep, other]
        self.left = [list(reversed(self.bits)) for _ in self.ranges]
        return send

    def join(self, other):
        self.inputs = other.inputs + self.inputs
        self.ranges = other.ranges + self.ranges
        self.left = other.left + self.left

    def last(self):
        return self.step == self.steps

    def plan(self, flat):
        if self.step == 0:
            parts = [[(flat[n], f, b), (flat[n + 1], f, b)] for n, f, b, _ in self.ranges]
        else:
            parts = [
                [(x, 0, x.shape[-3]) for x in flat[2 * n : 2 * n + 2]]
                for n in range(len(flat) // 2)
            ]
        if self.step >= len(self.bits):
            cut = self.spread and self.step == len(self.bits)
            bit = 2 + len(self.bits) + self.chip_bits[0]
            return [(parts, (), "rows", bit) if cut else (parts, (), None, 0)]
        jobs, self.chosen = [], []
        for n, (_, _, _, order) in enumerate(self.ranges):
            bit = (self.bits if order == 0 else self.bits[::-1])[self.step]
            jobs.append(([parts[n]], (2,) * len(self.left[n]), self.left[n].index(bit), 2 + bit))
            self.left[n].remove(bit)
            self.chosen.append(bit)
        return jobs

    def take(self, out):
        if self.step < len(self.bits):
            self.sends, self.stays = out[0::2], out[1::2]
        else:
            self.sends, self.stays = out[:1], out[-1:]
        return self.sends[0]

    def launch(self):
        place = self.place
        if self.step < len(self.bits):
            got = [place.to_shard(x, 1 << bit) for x, bit in zip(self.sends, self.chosen)]
        else:
            bit = self.chip_bits[self.step - len(self.bits)]
            got = [place.to_chip(x, 1 << bit) for x in self.sends]
        self.inputs = [x for pair in zip(self.stays, got) for x in pair]
        self.step += 1

    def to_neighbours(self):
        self.pieces = [self.sends[0], self.place.to_core(self.sends[0])]
        if self.spread:
            self.pieces.append(self.place.to_chip(self.sends[0], 1 << self.chip_bits[0]))

    def to_last(self):
        if self.spread:
            self.pieces.append(self.place.to_core(self.pieces[2]))


def sum_round(where, flows, *after):
    flat = gates([x for flow in flows for x in flow.inputs], *after)
    jobs, counts = [], []
    for flow in flows:
        few = len(flow.inputs)
        some = flow.plan(flat[:few])
        flat = flat[few:]
        jobs += some
        counts.append(sum(1 if cut is None else 2 for _, _, cut, _ in some))
    out = combine(where, jobs, "sum_round")
    for flow, count in zip(flows, counts):
        token = flow.take(out[:count])
        out = out[count:]
    return token


def square_sum(pieces, loss):
    def kernel(loss_ref, *refs):
        total = jnp.zeros((1, W), F32)
        for ref in refs[:-1]:
            for b in range(ref.shape[0]):
                x = ref[b].astype(F32)
                total = total + jnp.sum(x * x, 0, keepdims=True)
        refs[-1][:, 0:1] = loss_ref[...]
        refs[-1][:, 1:2] = jnp.sum(total, 1, keepdims=True)

    return pl.pallas_call(
        kernel,
        grid=(1,),
        in_specs=[whole((1, 1))] + [whole(p.shape) for p in pieces],
        out_specs=whole((1, 2)),
        out_shape=jax.ShapeDtypeStruct((1, 2), F32),
        compiler_params=params(8),
        cost_estimate=cost(10**6, 10**6),
        name="square_sum",
    )(loss, *pieces)


def fill_weights(step, where_ref, sources, targets, sem):
    shard, core = where_ref[0], where_ref[1]
    count = len(sources) - 2

    @pl.when(step == 0)
    def _():
        made = targets(sources[0], shard, None)
        for k in range(count):
            made += targets(sources[1 + k], shard ^ (k + 1), core)
            made += targets(sources[-1].at[k], shard ^ (k + 1), 1 - core)
        todo = [pltpu.make_async_copy(s, t, sem.at[n]) for n, (s, t) in enumerate(made)]
        for copy in todo:
            copy.start()
        for copy in todo:
            copy.wait()


def attn_targets(w_ref, rows):
    def targets(piece, at, half):
        if half is None:
            return [(piece.at[pl.ds(0, 4)], w_ref.at[:, pl.ds(pl.multiple_of(at * rows, rows), rows)])]
        start = pl.multiple_of(at * rows + half * (rows // 2), rows // 2)
        return [(piece.at[pl.ds(0, 4)], w_ref.at[:, pl.ds(start, rows // 2)])]

    return targets


def mlp_targets(up_ref, down_ref, rows):
    def targets(piece, at, half):
        few = rows if half is None else rows // 2
        skip = 0 if half is None else half * few
        start = pl.multiple_of(at * rows + skip, few)
        skip = pl.multiple_of(skip, few) if half is not None else 0
        return [
            (piece.at[pl.ds(0, 4)], up_ref.at[:, pl.ds(start, few)]),
            (piece.at[pl.ds(4, 4)], down_ref.at[pl.ds(at * 4, 4), pl.ds(skip, few)]),
        ]

    return targets


def pack(place, where, index, tall, wide, small):
    rows = D // place.shards
    half = rows // 2
    wide = [x.reshape(L, 4, rows, W) for x in wide]
    total = sum(x.shape[2] // W for x in tall) + 4 * len(wide) + bool(small)
    count = len(tall) + len(wide)

    def kernel(where_ref, *refs):
        full_ref, mine_ref = refs[count + len(small) : count + len(small) + 2]

        def run(core):
            own = slice(core * half, core * half + half)
            at = 0
            for ref in refs[: len(tall)]:
                for b in range(ref.shape[1] // W):
                    block = ref[:, W * b : W * b + W].astype(BF16)
                    full_ref[at] = block
                    mine_ref[at] = block[own]
                    at += 1
            for ref in refs[len(tall) : count]:
                for b in range(4):
                    block = ref[b].astype(BF16)
                    full_ref[at] = block
                    mine_ref[at] = block[own]
                    at += 1
            if small:
                table_ref = refs[-1]
                start = 0
                for ref in refs[count : count + len(small)]:
                    table_ref[start : start + ref.shape[0]] = ref[...]
                    start += ref.shape[0]
                table_ref[start:] = jnp.zeros((SMALL - start, rows), F32)
                norms = refs[count + 1][...]
                left = norms - norms.astype(BF16).astype(F32)
                table_ref[NORMS_LOW : NORMS_LOW + norms.shape[0]] = left
                for h in range(2):
                    for q in range(W // rows):
                        first = h * (SMALL // 2) + q * half
                        value = table_ref[first : first + half, :].astype(BF16)
                        spot = slice(q * rows, q * rows + rows)
                        full_ref[at, h * half : h * half + half, spot] = value
                        if h == core:
                            mine_ref[at, :, spot] = value

        for core in range(2):

            @pl.when(where_ref[1] == core)
            def _(core=core):
                run(core)

    return pl.pallas_call(
        kernel,
        grid=(1,),
        in_specs=[SMEM]
        + [pl.BlockSpec((None, rows, x.shape[2]), lambda i: (index, 0, 0)) for x in tall]
        + [pl.BlockSpec((None, 4, rows, W), lambda i: (index, 0, 0, 0)) for x in wide]
        + [whole(x.shape) for x in small],
        out_specs=[whole((total, rows, W)), whole((total, half, W))],
        out_shape=[
            pltpu.HBM((total, rows, W), BF16),
            pltpu.HBM((total, half, W), BF16),
        ],
        scratch_shapes=[pltpu.VMEM((SMALL, rows), F32)] * bool(small),
        compiler_params=params(),
        cost_estimate=cost(total * rows * W, total * rows * W * 7),
        name="pack",
    )(where, *map(in_hbm, tall), *map(in_hbm, wide), *map(in_hbm, small))


def embed_step(place, where, target, maskf, group):
    shards = place.shards
    rows = D // shards
    half = rows // 2
    n = target.shape[0]
    sources = len(group)

    def kernel(where_ref, target_ref, mask_ref, *refs):
        pieces, refs = refs[:sources], refs[sources:]
        x_ref, inputs_ref, head_ref, norm_ref, got_ref, table_ref, sem = refs

        def targets(piece, at, part):
            start = 0 if part is None else pl.multiple_of(part * half, half)
            few = rows if part is None else half
            return [(piece.at[4], got_ref.at[at, pl.ds(start, few)])]

        fill_weights(0, where_ref, pieces, targets, sem)
        for j in range(shards):
            for h in range(2):
                for q in range(W // rows):
                    spot = slice(q * rows, q * rows + rows)
                    part = slice(h * half, h * half + half)
                    value = got_ref[j, part, spot].astype(F32)
                    first = h * (SMALL // 2) + q * half
                    table_ref[first : first + half, j * rows : j * rows + rows] = value
        inputs = jnp.where(mask_ref[...] > 0, 0.0, target_ref[...].astype(F32)).astype(BF16)
        inputs_ref[...] = inputs
        embed = table_ref[:P_SIZE].astype(BF16)
        for s in range(n // LEN):
            part = slice(s * LEN, s * LEN + LEN)
            x_ref[part] = dense(inputs[part], embed) + table_ref[2 * P_SIZE : 2 * P_SIZE + LEN]
        head_ref[...] = table_ref[P_SIZE : 2 * P_SIZE].astype(BF16)
        low = table_ref[NORMS_LOW : NORMS_LOW + 16]
        norm_ref[...] = table_ref[NORMS_LOW - 16 : NORMS_LOW] + low

    return pl.pallas_call(
        kernel,
        grid=(1,),
        in_specs=[SMEM, whole((n, P_SIZE)), whole((n, 1))] + [ANY] * sources,
        out_specs=[whole((n, D)), whole((n, P_SIZE)), whole((P_SIZE, D)), whole((16, D))],
        out_shape=[
            pltpu.HBM((n, D), F32),
            jax.ShapeDtypeStruct((n, P_SIZE), BF16),
            jax.ShapeDtypeStruct((P_SIZE, D), BF16),
            jax.ShapeDtypeStruct((16, D), F32),
        ],
        scratch_shapes=[
            pltpu.VMEM((shards, rows, W), BF16),
            pltpu.VMEM((SMALL, D), F32),
            pltpu.SemaphoreType.DMA((copies_of(group),)),
        ],
        compiler_params=params(),
        cost_estimate=cost(2 * n * D * P_SIZE, n * D * 5),
        name="embed_step",
    )(where, target, maskf, in_hbm(group[0]), *group[1:])


def copies_of(group):
    return 2 * (2 * (len(group) - 2) + 1)


def norm_parts(x):
    center = x - jnp.mean(x, -1, keepdims=True)
    rstd = lax.rsqrt(jnp.mean(center * center, -1, keepdims=True) + EPS)
    return center * rstd, rstd


def norm_back(xhat, rstd, dy, gain):
    dxh = dy * gain
    return rstd * (
        dxh - jnp.mean(dxh, -1, keepdims=True) - xhat * jnp.mean(dxh * xhat, -1, keepdims=True)
    )


def head_lanes(x, h):
    lane = lax.broadcasted_iota(jnp.int32, (x.shape[0], 128), 1)
    own = (lane < DH) if h % 2 == 0 else (lane >= DH)
    return jnp.where(own, x[:, pair_of(h)], 0)


def pair_of(h):
    return slice(128 * (h // 2), 128 * (h // 2) + 128)


def head_of(h):
    return slice(DH * h, DH * h + DH)


SP = 1


def attn_fwd(place, where, x, norms, group):
    rows = D // place.shards
    n = x.shape[0]
    seqs = n // LEN
    sources = len(group)

    def kernel(where_ref, x_ref, norm_ref, *refs):
        pieces, refs = refs[:sources], refs[sources:]
        mid_ref, qkv_ref, pt_ref, ot_ref, w_ref, sem = refs
        fill_weights(pl.program_id(0), where_ref, pieces, attn_targets(w_ref, rows), sem)
        spans = [slice(LEN * s, LEN * s + LEN) for s in range(SP)]
        a, q, k, vt = [], [], [], []
        for s, span in enumerate(spans):
            xhat, _ = norm_parts(x_ref[span])
            a.append((xhat * norm_ref[0:1, :] + norm_ref[1:2, :]).astype(BF16))
            q.append((dense(a[s], w_ref[0]) * DH**-0.5).astype(BF16))
            k.append(dense(a[s], w_ref[1]).astype(BF16))
            qkv_ref[span, :D] = q[s]
            qkv_ref[span, D : 2 * D] = k[s]

        def scores(s, h):
            return dense_nt(k[s][:, pair_of(h)], head_lanes(q[s], h))

        def gather_values(s, h, p):
            ot_ref[s, head_of(h), :] = dense(vt[s][head_of(h), :], p).astype(BF16)

        items = [(s, h) for h in range(H) for s in range(SP)]
        ahead = scores(*items[0])
        for s, span in enumerate(spans):
            v = dense(a[s], w_ref[2]).astype(BF16)
            qkv_ref[span, 2 * D :] = v
            vt.append(v.T)
        last = None
        for at, (s, h) in enumerate(items):
            st = ahead
            if at + 1 < len(items):
                ahead = scores(*items[at + 1])
            if last is not None:
                gather_values(*last)
            e = jnp.exp(st - jnp.max(st, axis=0, keepdims=True))
            p = (e * (1.0 / jnp.sum(e, axis=0, keepdims=True))).astype(BF16)
            pt_ref[s, h] = p
            last = (s, h, p)
        gather_values(*last)
        for s, span in enumerate(spans):
            mid_ref[span] = x_ref[span] + dense_tn(ot_ref[s], w_ref[3])

    return pl.pallas_call(
        kernel,
        grid=(seqs // SP,),
        in_specs=[SMEM, pl.BlockSpec((SP * LEN, D), lambda i: (i, 0)), whole((4, D))]
        + [ANY] * sources,
        out_specs=[
            pl.BlockSpec((SP * LEN, D), lambda i: (i, 0)),
            pl.BlockSpec((SP * LEN, 3 * D), lambda i: (i, 0)),
            pl.BlockSpec((SP, H, LEN, LEN), lambda i: (i, 0, 0, 0)),
            pl.BlockSpec((SP, D, LEN), lambda i: (i, 0, 0)),
        ],
        out_shape=[
            pltpu.HBM((n, D), F32),
            pltpu.HBM((n, 3 * D), BF16),
            pltpu.HBM((seqs, H, LEN, LEN), BF16),
            pltpu.HBM((seqs, D, LEN), BF16),
        ],
        scratch_shapes=[
            pltpu.VMEM((4, D, W), BF16),
            pltpu.SemaphoreType.DMA((copies_of(group),)),
        ],
        compiler_params=params(),
        cost_estimate=cost(2 * n * D * (4 * D + 2 * LEN), n * D * 20, n * H * LEN),
        name="attn_fwd",
    )(where, x, norms, in_hbm(group[0]), *group[1:])


def gelu_pair(u):
    cdf = 0.5 * lax.erf(u * 0.7071067811865476) + 0.5
    density = jnp.exp(u * u * -0.5) * 0.3989422804014327
    return u * cdf, cdf + u * density


def mlp_fwd(place, where, mid, norms, group):
    rows = D // place.shards
    n = mid.shape[0]
    tall = LEN
    step = W // 2
    sources = len(group)
    per = W // rows

    def kernel(where_ref, mid_ref, norm_ref, *refs):
        pieces, refs = refs[:sources], refs[sources:]
        out_ref, act_ref, gp_ref, up_ref, down_ref, sem = refs
        fill_weights(pl.program_id(0), where_ref, pieces, mlp_targets(up_ref, down_ref, rows), sem)
        mid = mid_ref[...]
        xhat, _ = norm_parts(mid)
        c = (xhat * norm_ref[2:3, :] + norm_ref[3:4, :]).astype(BF16)
        total = mid

        def upper(b):
            cols = slice(step * (b % 2), step * (b % 2) + step)
            return dense(c, up_ref[b // 2, :, cols])

        def lower(act, b):
            few = per // 2
            return dense(act, down_ref[few * b : few * b + few].reshape(step, D))

        ahead = upper(0)
        for b in range(FF // step):
            cols = slice(step * b, step * b + step)
            u = ahead
            if b + 1 < FF // step:
                ahead = upper(b + 1)
            if b > 0:
                total = total + lower(last, b - 1)
            act, slope = gelu_pair(u)
            last = act.astype(BF16)
            act_ref[:, cols] = last
            gp_ref[:, cols] = slope.astype(BF16)
        out_ref[...] = total + lower(last, FF // step - 1)

    def row(width):
        return pl.BlockSpec((tall, width), lambda i: (i, 0))

    return pl.pallas_call(
        kernel,
        grid=(n // tall,),
        in_specs=[SMEM, row(D), whole((4, D))] + [ANY] * sources,
        out_specs=[row(D), row(FF), row(FF)],
        out_shape=[
            jax.ShapeDtypeStruct((n, D), F32),
            pltpu.HBM((n, FF), BF16),
            pltpu.HBM((n, FF), BF16),
        ],
        scratch_shapes=[
            pltpu.VMEM((4, D, W), BF16),
            pltpu.VMEM((FF // rows, rows, D), BF16),
            pltpu.SemaphoreType.DMA((copies_of(group),)),
        ],
        compiler_params=params(),
        cost_estimate=cost(4 * n * D * FF, n * D * 24, n * FF * 2),
        name="mlp_fwd",
    )(where, in_hbm(mid), norms, *group)


def mlp_bwd(place, where, dz, mid, gp, norms, group):
    rows = D // place.shards
    n = mid.shape[0]
    sources = len(group)
    per = W // rows

    def kernel(where_ref, dz_ref, mid_ref, gp_ref, norm_ref, *refs):
        pieces, refs = refs[:sources], refs[sources:]
        dmid_ref, dh_ref, du_ref, c_ref, dm_ref, dn_ref, up_ref, down_ref, sem = refs
        i = pl.program_id(0)
        fill_weights(i, where_ref, pieces, mlp_targets(up_ref, down_ref, rows), sem)
        dm = dz_ref[...].astype(BF16)
        dm_ref[...] = dm

        def upper(b):
            return dense_nt(dm, down_ref[per * b : per * b + per].reshape(W, D))

        dc = jnp.zeros((LEN, D), F32)
        ahead = upper(0)
        for b in range(FF // W):
            cols = slice(W * b, W * b + W)
            da = ahead
            if b + 1 < FF // W:
                ahead = upper(b + 1)
            if b > 0:
                dc = dc + dense_nt(last, up_ref[b - 1])
            last = (gp_ref[:, cols].astype(F32) * da).astype(BF16)
            du_ref[:, cols] = last
        dc = dc + dense_nt(last, up_ref[FF // W - 1])
        xhat, rstd = norm_parts(mid_ref[...])
        gain = norm_ref[2:3, :]
        c_ref[...] = (xhat * gain + norm_ref[3:4, :]).astype(BF16)
        dmid = dz_ref[...] + norm_back(xhat, rstd, dc, gain)
        dmid_ref[...] = dmid
        dh_ref[...] = dmid.astype(BF16)

        @pl.when(i == 0)
        def _():
            dn_ref[...] = jnp.zeros_like(dn_ref)

        dn_ref[0:1, :] += jnp.sum(dc * xhat, 0, keepdims=True)
        dn_ref[1:2, :] += jnp.sum(dc, 0, keepdims=True)

    def row(width):
        return pl.BlockSpec((LEN, width), lambda i: (i, 0))

    return pl.pallas_call(
        kernel,
        grid=(n // LEN,),
        in_specs=[SMEM, row(D), row(D), row(FF), whole((4, D))] + [ANY] * sources,
        out_specs=[row(D), row(D), row(FF), row(D), row(D), whole((8, D))],
        out_shape=[
            jax.ShapeDtypeStruct((n, D), F32),
            jax.ShapeDtypeStruct((n, D), BF16),
            pltpu.HBM((n, FF), BF16),
            jax.ShapeDtypeStruct((n, D), BF16),
            jax.ShapeDtypeStruct((n, D), BF16),
            jax.ShapeDtypeStruct((8, D), F32),
        ],
        scratch_shapes=[
            pltpu.VMEM((4, D, W), BF16),
            pltpu.VMEM((FF // rows, rows, D), BF16),
            pltpu.SemaphoreType.DMA((copies_of(group),)),
        ],
        compiler_params=params(),
        cost_estimate=cost(4 * n * D * FF, n * D * 32),
        name="mlp_bwd",
    )(where, dz, in_hbm(mid), in_hbm(gp), norms, *group)


def attn_bwd(place, where, dmid, dh, x, qkv, pt, ot, norms, group):
    rows = D // place.shards
    n = x.shape[0]
    seqs = n // LEN
    sources = len(group)

    def kernel(where_ref, dmid_ref, dh_ref, x_ref, qkv_ref, pt_ref, ot_ref, norm_ref, *refs):
        pieces, refs = refs[:sources], refs[sources:]
        dx_ref, dqkv_ref, a_ref, dn_ref, w_ref, dqt_ref, sem = refs
        i = pl.program_id(0)
        fill_weights(i, where_ref, pieces, attn_targets(w_ref, rows), sem)
        spans = [slice(None)]
        do, delta, kt = [], [], []
        for s, span in enumerate(spans):
            do.append(dense_nt(dh_ref[span], w_ref[3]).astype(BF16))
            along = do[s].T.astype(F32) * ot_ref[s].astype(F32)
            delta.append([jnp.sum(along[head_of(h), :], axis=0, keepdims=True) for h in range(H)])
            kt.append(qkv_ref[span, D : 2 * D].T)

        def first(s, h):
            doh = head_lanes(do[s], h)
            v = qkv_ref[spans[s], 2 * D + 128 * (h // 2) : 2 * D + 128 * (h // 2) + 128]
            return dense_nt(v, doh), dense(pt_ref[s, h], doh)

        halves = {}

        def second(s, h, dst, dv):
            q = qkv_ref[spans[s], pair_of(h)]
            lane = lax.broadcasted_iota(jnp.int32, (LEN, 128), 1)
            own = (lane < DH) if h % 2 == 0 else (lane >= DH)
            dk = dense(dst, jnp.where(own, q, 0))
            dqt_ref[s, head_of(h), :] = (dense(kt[s][head_of(h), :], dst) * DH**-0.5).astype(BF16)
            if h % 2 == 0:
                halves[s] = (dk, dv)
                return
            at = 128 * (h // 2)
            dk, dv = dk + halves[s][0], dv + halves[s][1]
            dqkv_ref[spans[s], D + at : D + at + 128] = dk.astype(BF16)
            dqkv_ref[spans[s], 2 * D + at : 2 * D + at + 128] = dv.astype(BF16)

        items = [(s, h) for h in range(H) for s in range(1)]
        ahead = first(*items[0])
        last = None
        for at, (s, h) in enumerate(items):
            dpt, dv = ahead
            if at + 1 < len(items):
                ahead = first(*items[at + 1])
            if last is not None:
                second(*last)
            dst = (pt_ref[s, h].astype(F32) * (dpt - delta[s][h])).astype(BF16)
            last = (s, h, dst, dv)
        second(*last)

        @pl.when(i == 0)
        def _():
            dn_ref[...] = jnp.zeros_like(dn_ref)

        gain = norm_ref[0:1, :]
        for s, span in enumerate(spans):
            da = dense_nt(dqkv_ref[span, D : 2 * D], w_ref[1])
            da = da + dense_nt(dqkv_ref[span, 2 * D :], w_ref[2])
            dq = dqt_ref[s].T
            dqkv_ref[span, :D] = dq
            da = da + dense_nt(dq, w_ref[0])
            xhat, rstd = norm_parts(x_ref[span])
            a_ref[span] = (xhat * gain + norm_ref[1:2, :]).astype(BF16)
            dx_ref[span] = dmid_ref[span] + norm_back(xhat, rstd, da, gain)
            dn_ref[0:1, :] += jnp.sum(da * xhat, 0, keepdims=True)
            dn_ref[1:2, :] += jnp.sum(da, 0, keepdims=True)

    def row(width):
        return pl.BlockSpec((LEN, width), lambda i: (i, 0))

    return pl.pallas_call(
        kernel,
        grid=(seqs,),
        in_specs=[
            SMEM,
            row(D),
            row(D),
            row(D),
            row(3 * D),
            pl.BlockSpec((1, H, LEN, LEN), lambda i: (i, 0, 0, 0)),
            pl.BlockSpec((1, D, LEN), lambda i: (i, 0, 0)),
            whole((4, D)),
        ]
        + [ANY] * sources,
        out_specs=[row(D), row(3 * D), row(D), whole((8, D))],
        out_shape=[
            jax.ShapeDtypeStruct((n, D), F32),
            jax.ShapeDtypeStruct((n, 3 * D), BF16),
            jax.ShapeDtypeStruct((n, D), BF16),
            jax.ShapeDtypeStruct((8, D), F32),
        ],
        scratch_shapes=[
            pltpu.VMEM((4, D, W), BF16),
            pltpu.VMEM((1, D, LEN), BF16),
            pltpu.SemaphoreType.DMA((copies_of(group),)),
        ],
        compiler_params=params(),
        cost_estimate=cost(2 * n * D * (4 * D + 5 * LEN), n * D * 32),
        name="attn_bwd",
    )(where, dmid, dh, x, in_hbm(qkv), in_hbm(pt), in_hbm(ot), norms, *group)


def head_step(place, x, target, maskf, head, norms, count):
    n = x.shape[0]

    def kernel(x_ref, target_ref, mask_ref, head_ref, norm_ref, dx_ref, loss_ref, gh_ref, dn_ref):
        i = pl.program_id(0)
        xhat, rstd = norm_parts(x_ref[...])
        gain = norm_ref[0:1, :]
        y = (xhat * gain + norm_ref[1:2, :]).astype(BF16)
        masked = mask_ref[...]
        err = (dense_nt(y, head_ref[...]) - target_ref[...].astype(F32)) * masked
        dpred = (err * (2.0 / (P_SIZE * count))).astype(BF16)
        dy = dense(dpred, head_ref[...])
        dx_ref[...] = norm_back(xhat, rstd, dy, gain)

        @pl.when(i == 0)
        def _():
            loss_ref[...] = jnp.zeros_like(loss_ref)
            gh_ref[...] = jnp.zeros_like(gh_ref)
            dn_ref[...] = jnp.zeros_like(dn_ref)

        loss_ref[...] += jnp.sum(err * err, 0, keepdims=True)
        gh_ref[...] += dense_tn(dpred, y)
        dn_ref[0:1, :] += jnp.sum(dy * xhat, 0, keepdims=True)
        dn_ref[1:2, :] += jnp.sum(dy, 0, keepdims=True)

    def row(width):
        return pl.BlockSpec((LEN, width), lambda i: (i, 0))

    return pl.pallas_call(
        kernel,
        grid=(n // LEN,),
        in_specs=[row(D), row(P_SIZE), row(1), whole((P_SIZE, D)), whole((2, D))],
        out_specs=[row(D), whole((1, P_SIZE)), whole((P_SIZE, D)), whole((8, D))],
        out_shape=[
            jax.ShapeDtypeStruct((n, D), F32),
            jax.ShapeDtypeStruct((1, P_SIZE), F32),
            jax.ShapeDtypeStruct((P_SIZE, D), F32),
            jax.ShapeDtypeStruct((8, D), F32),
        ],
        compiler_params=params(),
        cost_estimate=cost(6 * n * D * P_SIZE, n * D * 8),
        name="head_step",
    )(x, target, maskf, head, norms)


def put_block(core, block, lead, send_ref, keep_ref, at):
    rows = block.shape[0]
    halves = block.reshape(lead + (2, rows // (2 * lead_size(lead)), W))
    first, second = halves[..., 0, :, :], halves[..., 1, :, :]
    keep_ref[at] = jnp.where(core == 0, first, second)
    send_ref[at] = jnp.where(core == 0, second, first)


def lead_size(lead):
    size = 1
    for n in lead:
        size *= n
    return size


def grad_mlp(place, where, c, du, act, dm, ot, dh):
    shards = place.shards
    rows = D // shards
    n = c.shape[0]
    seqs = n // LEN
    wide = 2 * W
    steps = FF // wide
    per = shards // steps
    blocks = 9

    def kernel(where_ref, c_ref, du_ref, act_ref, dm_ref, ot_ref, dh_ref, send_ref, keep_ref, ct_ref):
        i = pl.program_id(0)
        core = where_ref[1]

        @pl.when(i == 0)
        def _():
            ct_ref[...] = c_ref[...].T

        @pl.when(i < steps)
        def _():
            block = dense(ct_ref[...], du_ref[...]).astype(BF16)
            for b in range(wide // W):
                at = (slice(None), i * (wide // W) + b)
                put_block(core, block[:, W * b : W * b + W], (shards,), send_ref, keep_ref, at)

        @pl.when((i >= steps) & (i < 2 * steps))
        def _():
            block = dense_tn(act_ref[...], dm_ref[...]).astype(BF16)
            at = (pl.ds((i - steps) * per, per), slice(4, 8))
            put_block(core, block, (per, 4), send_ref, keep_ref, at)

        @pl.when(i == 2 * steps)
        def _():
            total = dense(ot_ref[0], dh_ref[:LEN, :])
            for s in range(1, seqs):
                total = total + dense(ot_ref[s], dh_ref[LEN * s : LEN * s + LEN, :])
            put_block(core, total.astype(BF16), (shards,), send_ref, keep_ref, (slice(None), 8))

    shape = (shards, blocks, rows // 2, W)
    return pl.pallas_call(
        kernel,
        grid=(2 * steps + 1,),
        in_specs=[
            SMEM,
            whole((n, D)),
            pl.BlockSpec((n, wide), lambda i: (0, jnp.minimum(i, steps - 1))),
            pl.BlockSpec((n, wide), lambda i: (0, jnp.clip(i - steps, 0, steps - 1))),
            whole((n, D)),
            whole((seqs, D, LEN)),
            whole((n, D)),
        ],
        out_specs=[whole(shape), whole(shape)],
        scratch_shapes=[pltpu.VMEM((D, n), BF16)],
        out_shape=[jax.ShapeDtypeStruct(shape, BF16)] * 2,
        compiler_params=params(),
        cost_estimate=cost(4 * n * D * FF, n * (4 * D + 4 * FF) + 4 * D * FF),
        name="grad_mlp",
    )(where, c, in_hbm(du), in_hbm(act), dm, in_hbm(ot), dh)


def grad_qkv(place, where, a, dqkv, small=()):
    shards = place.shards
    rows = D // shards
    half = rows // 2
    n = a.shape[0]
    blocks = 3 + bool(small)
    extra = len(small)

    def kernel(where_ref, a_ref, dqkv_ref, *refs):
        small_refs, refs = refs[:extra], refs[extra:]
        send_ref, keep_ref, at_ref = refs[:3]
        i = pl.program_id(0)

        @pl.when(i == 0)
        def _():
            at_ref[...] = a_ref[...].T

        @pl.when(i < 3)
        def _():
            block = dense(at_ref[...], dqkv_ref[...]).astype(BF16)
            put_block(where_ref[1], block, (shards,), send_ref, keep_ref, (slice(None), i))

        if extra:
            table_ref = refs[3]
            inputs_ref, dx_ref, head_ref = small_refs[:3]

            @pl.when(i == 3)
            def _():
                dx = dx_ref[...]
                table_ref[:P_SIZE] = dense_tn(inputs_ref[...], dx.astype(BF16)).astype(BF16)
                table_ref[P_SIZE : 2 * P_SIZE] = head_ref[...].astype(BF16)
                total = dx[:LEN]
                for s in range(1, n // LEN):
                    total = total + dx[s * LEN : s * LEN + LEN]
                table_ref[2 * P_SIZE : 2 * P_SIZE + LEN] = total.astype(BF16)
                norms = jnp.concatenate(
                    [ref[0:2, :] for ref in small_refs[3:]]
                    + [jnp.zeros((16 - 2 * (extra - 3), D), F32)],
                    0,
                )
                start = 2 * P_SIZE + LEN
                table_ref[start : start + 16] = norms.astype(BF16)
                table_ref[start + 16 :] = jnp.zeros((SMALL - start - 16, D), BF16)
                for core in range(2):

                    @pl.when(where_ref[1] == core)
                    def _(core=core):
                        for h in range(2):
                            out_ref = keep_ref if h == core else send_ref
                            for j in range(shards):
                                for q in range(W // rows):
                                    first = h * (SMALL // 2) + q * half
                                    value = table_ref[first : first + half, j * rows : j * rows + rows]
                                    out_ref[j, 3, :, q * rows : q * rows + rows] = value

    shape = (shards, blocks, half, W)
    return pl.pallas_call(
        kernel,
        grid=(blocks,),
        in_specs=[SMEM, whole((n, D)), pl.BlockSpec((n, W), lambda i: (0, jnp.minimum(i, 2)))]
        + [whole(x.shape) for x in small],
        out_specs=[whole(shape), whole(shape)],
        scratch_shapes=[pltpu.VMEM((D, n), BF16)] + [pltpu.VMEM((SMALL, D), BF16)] * bool(small),
        out_shape=[jax.ShapeDtypeStruct(shape, BF16)] * 2,
        compiler_params=params(),
        cost_estimate=cost(6 * n * D * D, n * 8 * D + 6 * D * D),
        name="grad_qkv",
    )(where, a, dqkv, *small)


def adam(weight, first, second, tenth, rate):
    scale = (1 - BETA_ONE**STEP_COUNT) / rate
    first = BETA_ONE * first + tenth
    second = BETA_TWO * second + tenth * ((1 - BETA_TWO) / (1 - BETA_ONE) ** 2) * tenth
    spread = second * (scale * scale / (1 - BETA_TWO**STEP_COUNT))
    step = first * (1.0 / (spread * lax.rsqrt(spread) + ADAM_EPS * scale))
    return (weight * (1 - rate * DECAY) - step, first, second)


def fetch(arrays, where):
    def kernel(where_ref, *refs):
        sem = refs[-1]
        count = len(arrays)
        copies = [
            pltpu.make_async_copy(refs[n], refs[count + n], sem.at[n]) for n in range(count)
        ]
        for copy in copies:
            copy.start()
        for copy in copies:
            copy.wait()

    return pl.pallas_call(
        kernel,
        in_specs=[SMEM] + [pl.BlockSpec(memory_space=pltpu.HBM)] * len(arrays),
        out_specs=[pl.BlockSpec(memory_space=pltpu.VMEM)] * len(arrays),
        out_shape=[pltpu.VMEM(x.shape, x.dtype) for x in arrays],
        scratch_shapes=[pltpu.SemaphoreType.DMA((len(arrays),))],
        compiler_params=params(4),
        name="fetch",
    )(where, *map(in_hbm, arrays))


def adam_step(place, where, both, count, state, small, grads):
    rows = D // place.shards
    half = rows // 2
    few = half // 2
    flat = [x for group in state for x in group]
    tiny = [x for group in small for x in group]

    def spec(x):
        if x.ndim == 4:
            return pl.BlockSpec((None, 4, few, W), lambda i, h, q: (i, 0, 2 * h + q, 0))
        return pl.BlockSpec((None, few, x.shape[2]), lambda i, h, q: (i, 2 * h + q, 0))

    gflat, spots = [], []
    for layer in grads:
        spots.append([])
        for pieces, first, bit in layer:
            known = [n for n, x in enumerate(gflat) if x is pieces[0]]
            spots[-1].append((known[0] if known else len(gflat), len(pieces), first, bit))
            gflat += [] if known else list(pieces)
    total = len(flat) + len(tiny)

    def kernel(where_ref, *refs):
        both_refs, refs = refs[: len(both)], refs[len(both) :]
        grad_refs, refs = refs[: len(gflat)], refs[len(gflat) :]
        ins, outs, table_ref = refs[:total], refs[total : 2 * total], refs[-1]
        loss_ref, norm_ref = refs[2 * total : 2 * total + 2]
        layer, h, q = pl.program_id(0), pl.program_id(1), pl.program_id(2)
        values = [ref[...] for ref in both_refs]
        sums = jnp.zeros((1, 2), F32)
        for j in range(len(values)):
            sums = sums + select_of(values, where_ref[0] ^ j)
        norm = jnp.sqrt(sums[:, 1:2])
        loss_ref[...] = sums[:, 0:1] / count
        norm_ref[...] = norm
        scale = (1 - BETA_ONE) * CLIP / jnp.maximum(norm, CLIP)
        own = where_ref[1] == h

        def update(n, at, grad, rate):
            got = adam(ins[3 * n][at], ins[3 * n + 1][at], ins[3 * n + 2][at], grad, rate)
            for k in range(3):
                outs[3 * n + k][at] = got[k]

        part = pl.ds(pl.multiple_of(q * few, few), few)

        def run(layer):
            def grad(group, b):
                base, count, first, bit = spots[layer][group]
                refs = grad_refs[base : base + count]
                if count == 2:
                    got = jnp.where(own, refs[0][first + b, part], refs[1][first + b, part])
                else:
                    close = jnp.where(own, refs[0][first + b], refs[1][first + b])
                    away = jnp.where(own, refs[2][first + b], refs[3][first + b])
                    got = jnp.where(where_ref[bit] == q, close, away)
                return got.astype(F32) * scale

            for b in range(3):
                update(0, (slice(None), slice(W * b, W * b + W)), grad(0, b), RATE)
            update(1, (slice(None), slice(None)), grad(1, 8), RATE)
            for b in range(4):
                update(2, (slice(None), slice(W * b, W * b + W)), grad(1, b), RATE)
                update(3, (b,), grad(1, 4 + b), RATE)

        for i in range(L):

            @pl.when(layer == i)
            def _(i=i):
                run(i)

        @pl.when((layer == 0) & (h == 0) & (q == 0))
        def _():
            base, _, at, _ = spots[0][0]
            mine, other = grad_refs[base][at + 3], grad_refs[base + 1][at + 3]
            first = where_ref[1] == 0
            for n, block in enumerate((jnp.where(first, mine, other), jnp.where(first, other, mine))):
                for k in range(W // rows):
                    start = n * (SMALL // 2) + k * half
                    table_ref[start : start + half] = (
                        block[:, k * rows : k * rows + rows].astype(F32) * scale
                    )
            count = 2 * P_SIZE + LEN
            update(4, (slice(None), slice(None)), table_ref[:count], TABLE_RATE)
            norms = small[1][0].shape[0]
            update(5, (slice(None), slice(None)), table_ref[count : count + norms], TABLE_RATE)

    out = pl.pallas_call(
        kernel,
        grid=(L, 2, 2),
        in_specs=[SMEM]
        + [whole((1, 2)) for _ in both]
        + [whole(g.shape) for g in gflat]
        + [spec(x) for x in flat]
        + [whole(x.shape) for x in tiny],
        out_specs=[spec(x) for x in flat] + [whole(x.shape) for x in tiny] + [whole((1, 1))] * 2,
        out_shape=[pltpu.HBM(x.shape, F32) for x in flat + tiny]
        + [jax.ShapeDtypeStruct((1, 1), F32)] * 2,
        scratch_shapes=[pltpu.VMEM((SMALL, rows), F32)],
        compiler_params=params(20),
        cost_estimate=cost(20 * L * 12 * rows * W, 24 * L * 12 * rows * W),
        name="adam_step",
    )(where, *both, *gflat, *flat, *map(in_hbm, tiny))
    news = [tuple(out[3 * n : 3 * n + 3]) for n in range(len(state) + len(small))]
    return out[-2].reshape(()), out[-1].reshape(()), news


def on_device(
    series,
    mask,
    qkv_w,
    out_w,
    up_w,
    down_w,
    patch_maps,
    norm_params,
    qkv_m,
    out_m,
    up_m,
    down_m,
    patch_m,
    norm_m,
    qkv_v,
    out_v,
    up_v,
    down_v,
    patch_v,
    norm_v,
):
    place = Place()
    shards = place.shards
    rows = D // shards
    half = rows // 2
    seqs = series.shape[0]
    count = MASKED * seqs * shards * place.replicas
    shard_bits = [(place.shard >> bit) & 1 for bit in bits_of(shards)]
    chip_bits = [(place.chip >> bit) & 1 for bit in bits_of(place.chips)]
    where = jnp.stack([place.shard, place.core] + shard_bits + chip_bits).astype(jnp.int32)
    chip = 2 + len(shard_bits)

    small_now = [patch_maps, norm_params]
    packs = [
        (
            pack(place, where, i, [qkv_w, out_w], [], small_now if i == 0 else []),
            pack(place, where, i, [up_w], [down_w], []),
        )
        for i in range(L)
    ]

    def group_of(packed, ours, theirs):
        return [packed[0]] + ours + [theirs]

    attn_groups = [None] * L
    mlp_groups = [None] * L
    target = series.reshape(seqs * LEN, P_SIZE)
    maskf = mask.reshape(seqs * LEN, 1).astype(F32)
    ours = gather_shards(place, packs[0][0][1])
    theirs = gather_cores(place, ours, *[p[1] for pair in packs for p in pair], target, maskf)
    attn_groups[0] = group_of(packs[0][0], ours, theirs)
    mine = gate(packs[0][1][1], *ours)
    ours_mlp = gather_shards(place, mine)

    x, inputs, head, norms_all = embed_step(place, where, target, gate(maskf, mine), attn_groups[0])
    saved = []
    for index in range(L):
        norms = norms_all[4 * index : 4 * index + 4]
        held = in_hbm(x) if index == 0 else x
        mid, qkv, pt, ot = attn_fwd(place, where, held, norms, attn_groups[index])
        held = mid
        if index + 1 < L:
            got = gates(ours_mlp, mid)
            mine = gate(packs[index + 1][0][1], *got)
            ours_attn = gather_shards(place, mine)
            held = gate(mid, mine)
        theirs = gather_cores(place, ours_mlp, mid)
        mlp_groups[index] = group_of(packs[index][1], ours_mlp, theirs)
        pieces = [in_hbm(x) if n < 2 * index else x for n, x in enumerate(mlp_groups[index])]
        y, act, gp = mlp_fwd(place, where, held, norms, pieces)
        if index + 1 < L:
            got = gates(ours_attn, y)
            theirs = gather_cores(place, got)
            attn_groups[index + 1] = group_of(packs[index + 1][0], ours_attn, theirs)
            mine = gate(packs[index + 1][1][1], *got)
            ours_mlp = gather_shards(place, mine)
            y = gate(y, mine)
        saved.append((x, mid, qkv, pt, ot, act, gp, norms))
        x = y

    grad, loss, g_head, dn_final = head_step(
        place, x, target, maskf, head, norms_all[4 * L : 4 * L + 2], count
    )
    loss = (jnp.sum(loss) / P_SIZE).reshape(1, 1)

    norm_grads = {}

    def backward_mlp(index, grad):
        x, mid, qkv, pt, ot, act, gp, norms = saved[index]
        dmid, dh, du, c, dm, dn = mlp_bwd(
            place, where, grad, mid, gp, norms, mlp_groups[index]
        )
        norm_grads[index, 1] = dn
        return dmid, dh, du, c, dm

    def backward_attn(index, dmid, dh):
        x, mid, qkv, pt, ot, act, gp, norms = saved[index]
        grad, dqkv, a, dn = attn_bwd(
            place, where, dmid, dh, x, qkv, pt, ot, norms, attn_groups[index]
        )
        norm_grads[index, 0] = dn
        return grad, dqkv, a

    def grads_mlp(index, du, c, dm, dh):
        return grad_mlp(place, where, c, du, saved[index][5], dm, saved[index][4], dh)

    one, two = Flow(place, True, True), Flow(place, True)
    ahead, end = Flow(place, False), Flow(place, False)

    def advance(flows, *after):
        token = sum_round(where, flows, *after)
        for flow in flows:
            flow.launch()
        return token

    loss = loss + place.to_core(loss)
    dmid, dh, du, c, dm = backward_mlp(1, grad)
    token = one.begin(*grads_mlp(1, du, c, dm, dh), (0, 5, 0), (5, 4, 1))
    grad, dqkv_one, a_one = backward_attn(1, gate(dmid, token), dh)
    token = advance([one], grad)
    dmid, dh, du, c, dm = backward_mlp(0, gate(grad, token))
    token = advance([one], dmid)
    token = two.begin(*grads_mlp(0, du, gate(c, token), dm, dh), (0, 5, 0), (5, 4, 1))
    token = advance([one], token)
    token = ahead.begin(*grad_qkv(place, where, gate(a_one, token), dqkv_one), (0, 3, 1))
    token = advance([two], token)
    grad, dqkv, a = backward_attn(0, gate(dmid, token), dh)
    token = sum_round(where, [one, two, ahead], grad)
    small = [inputs, grad, g_head]
    small += [norm_grads[i, k] for i in range(L) for k in range(2)] + [dn_final]
    token = end.begin(*grad_qkv(place, where, gate(a, token), dqkv, small), (0, 4, 0))
    one.launch()
    two.launch()
    ahead.launch()
    while not one.last():
        token = advance([one], token)
    token = sum_round(where, [one, two, end], token)
    end.launch()
    end.join(ahead)
    two.launch()
    one.to_neighbours()
    hops = bits_of(place.chips)

    def pass_loss(loss, token):
        if not hops:
            return loss
        return loss + place.to_chip(gate(loss, token), 1 << hops.pop(0))

    while end.step < end.steps - 2:
        loss = pass_loss(loss, token)
        token = sum_round(where, [end] + ([two] if not two.last() else []), token, loss)
        end.launch()
        if two.step == two.steps - 1:
            break
        if not two.last():
            two.launch()
    behind = not two.last()
    while end.step < end.steps - 1:
        loss = pass_loss(loss, token)
        token = advance([end], token, *one.pieces, loss)
    one.to_last()
    if behind:
        two.launch()
    while hops:
        loss = pass_loss(loss, token)
    state = [(qkv_w, qkv_m, qkv_v), (out_w, out_m, out_v), (up_w, up_m, up_v)]
    state.append(tuple(x.reshape(L, 4, rows, W) for x in (down_w, down_m, down_v)))
    token = sum_round(where, [end, two], token, loss)
    end.launch()
    two.to_neighbours()
    near = fetch([x for group in state for x in group], gate(where, token))
    state = [tuple(near[3 * n : 3 * n + 3]) for n in range(len(state))]
    token = sum_round(where, [end], token, *two.pieces, near[0])
    end.to_neighbours()
    two.to_last()
    grads = [
        [(end.pieces, 3, 0), (two.pieces, 0, chip + two.chip_bits[0])],
        [(end.pieces, 0, 0), (one.pieces, 0, chip + one.chip_bits[0])],
    ]
    done_one, done_two, done_last = one.pieces, two.pieces, end.pieces

    both = square_sum(done_one + done_two + done_last, loss)
    both = [both] + [place.to_shard(both, k) for k in range(1, shards)]

    small = [(patch_maps, patch_m, patch_v), (norm_params, norm_m, norm_v)]
    loss, grad_norm, results = adam_step(place, where, both, count, state, small, grads)
    results[3] = tuple(x.reshape(down_w.shape) for x in results[3])
    news = tuple(r[0] for r in results)
    new_m = tuple(r[1] for r in results)
    new_v = tuple(r[2] for r in results)
    return (loss, grad_norm) + news + new_m + new_v


def solution(mesh):
    batch = P(("shard", "replica"), None)
    stack = P(None, "shard", None)
    flat = P(None, "shard")
    state = (stack, stack, stack, stack, flat, flat)
    return jax.shard_map(
        on_device,
        mesh=mesh,
        in_specs=(batch, batch) + state * 3,
        out_specs=(P(), P()) + state * 3,
        check_vma=False,
    )
```
